256 devices in a mesh: row: 8 (over y, x_lo), col: 32 (over z, x_hi, core).
Axes of the slice: x: 4 (x_hi: 2, x_lo: 2; x = x_hi * 2 + x_lo), y: 4, z: 8, core: 2. Of those that a mesh axis runs over, the one named last changes fastest.
Arguments:
- blocks: bfloat16 [32, 4096, 8192], P('row', 'col'), may hold values from -1800 to 1800, as said below
- factor_b: float32 [8192, 256], P('col'), may hold values from -6 to 6
- factor_c: float32 [64, 256], replicated, may hold values from -0.75 to 0.75
- block_pos: int32 [32, 32], P('row', 'col'), may hold values from 0 to 7, as said below
- block_count: int32 [8, 32], P('row', 'col'), may hold values from 1 to 4, as said below
Outputs:
- factor_a_new: float32 [4096, 256], P(('row', 'col'))
- factor_b_new: float32 [8192, 256], P(('col', 'row'))
The draws below stay inside these ranges and needn't reach their ends.
Inputs may be any that keep to these rules, and one draw needn't show every extreme that they name: `blocks`: every entry is finite. `block_pos`: the 4 positions of one device are distinct. `block_count`: some device has all 4 slots live.
All inputs are finite; a program needn't handle non-finite values.
Results may differ from the reference program's by a relative error of at most 0.007.
Values may be sent and summed in bfloat16 or wider, within the bound.
A program may use at most 64 MiB of HBM per device.

```python
import jax
import jax.numpy as jnp
from jax import lax

R = 256
K = 64
BLK = 128
SLOTS = 4
IB_DEV = 4
JB_DEV = 2
ROWS_A = 4096
ROWS_B = 8192
N_ROW = 8
N_COL = 32


def layout_helper(key):
    base = jax.random.fold_in(key, 7)
    count_key, busy_key, pick_key, perm_key = jax.random.split(base, 4)
    counts = jax.random.randint(count_key, (N_ROW, N_COL), 1, 3)
    busy = jax.random.randint(busy_key, (N_ROW, N_COL), 0, 8)
    counts = jnp.where(busy == 0, SLOTS, counts)
    chosen = jax.random.randint(pick_key, (), 0, N_ROW * N_COL)
    flat = jnp.arange(N_ROW * N_COL, dtype=jnp.int32).reshape(N_ROW, N_COL)
    counts = jnp.where(flat == chosen, SLOTS, counts).astype(jnp.int32)
    subkeys = jax.random.split(perm_key, N_ROW * N_COL)

    def pick_order(subkey):
        return jax.random.permutation(subkey, IB_DEV * JB_DEV)[:SLOTS]
    orders = jax.vmap(pick_order)(subkeys).reshape(N_ROW, N_COL, SLOTS)
    orders = orders.transpose(0, 2, 1).reshape(N_ROW * SLOTS, N_COL).astype(jnp.int32)
    return (orders, counts)


def draw_block_pos(key, part):
    return layout_helper(key)[0]


def draw_block_count(key, part):
    return layout_helper(key)[1]


def draw_blocks(key, part):
    noise_key, row_key, col_key = jax.random.split(jax.random.fold_in(key, 3), 3)
    lead = N_ROW * SLOTS
    mid = N_COL * BLK
    row_rise = 3.0 ** ((jnp.arange(lead) // SLOTS).astype(jnp.float32) / max(N_ROW - 1, 1))
    col_rise = 3.0 ** ((jnp.arange(mid) // BLK).astype(jnp.float32) / max(N_COL - 1, 1))
    noise = jnp.clip(jax.random.normal(noise_key, (lead, mid, BLK, K), jnp.float32), -4.0, 4.0)
    row_scale = jnp.exp(jax.random.uniform(row_key, (lead, mid), jnp.float32, 0.0, jnp.log(10.0)))
    col_scale = jnp.exp(jax.random.uniform(col_key, (lead, BLK), jnp.float32, 0.0, jnp.log(3.0)))
    scaled = noise * (row_rise[:, None] * row_scale * col_rise[None, :])[:, :, None, None] * col_scale[:, None, :, None]
    return scaled.reshape(lead, mid, BLK * K).astype(jnp.bfloat16)


def levels(stream_key, dims, cuts, least, high):
    loudness, own = 1.0, jax.random.fold_in(stream_key, 6)
    for axis_at, shards_of in cuts:
        heights = jnp.exp(jax.random.uniform(jax.random.fold_in(own, axis_at), (shards_of,), jnp.float32, least / len(cuts), high / len(cuts)))
        loudness = loudness * jnp.repeat(heights, dims[axis_at] // shards_of).reshape([-1 if axis == axis_at else 1 for axis in range(len(dims))])
    return loudness


def bell_draw(key, dims, width, bound, cuts=(), kind=jnp.bfloat16):
    values = width * jax.random.normal(key, dims, jnp.float32)
    if cuts:
        values = values * levels(key, dims, cuts, -0.22, 0.18)
    return jnp.clip(values, -bound, bound).astype(kind)


def setup_inputs(seed: int = 0) -> dict:
    seeds = jax.random.split(jax.random.key(seed), 6)
    blocks = draw_blocks(jax.random.fold_in(seeds[5], 71), 0)
    factor_b = bell_draw(seeds[1], (ROWS_B, R), 1.0, 6.0, ((0, 32),), jnp.float32)
    factor_c = bell_draw(seeds[2], (K, R), 0.125, 0.75, (), jnp.float32)
    block_pos = draw_block_pos(jax.random.fold_in(seeds[5], 71), 0)
    block_count = draw_block_count(jax.random.fold_in(seeds[5], 71), 0)
    return {"blocks": blocks, "factor_b": factor_b, "factor_c": factor_c, "block_pos": block_pos, "block_count": block_count}


norm_eps = 1e-06

def solve_right(rows_in, matrix):
    lower = jnp.linalg.cholesky(matrix)
    half = lax.linalg.triangular_solve(lower, rows_in, left_side=False, lower=True, transpose_a=True)
    return lax.linalg.triangular_solve(lower, half, left_side=False, lower=True, transpose_a=False)

def reference(blocks, factor_b, factor_c, block_pos, block_count):
    row_slab = IB_DEV * BLK
    col_slab = JB_DEV * BLK
    high = lax.Precision.HIGHEST
    c_low = factor_c.astype(jnp.bfloat16).astype(jnp.float32)
    b_low = factor_b.astype(jnp.bfloat16).astype(jnp.float32)
    gram_c = jnp.dot(factor_c.T, factor_c, precision=high)
    gram_b = jnp.dot(factor_b.T, factor_b, precision=high)
    v_one = gram_b * gram_c
    device_list = jnp.arange(N_ROW * N_COL, dtype=jnp.int32)

    def fetch(rindex, cindex, slot):
        tile = lax.dynamic_slice(blocks, (rindex * SLOTS + slot, cindex * BLK, jnp.int32(0)), (1, BLK, BLK * K))[0]
        return tile.astype(jnp.float32).reshape(BLK, BLK, K)

    def sweep_a(total, device):
        rindex = device // N_COL
        cindex = device % N_COL

        def one_slot(slot, acc):
            place = block_pos[rindex * SLOTS + slot, cindex]
            cube = fetch(rindex, cindex, slot)
            b_tile = lax.dynamic_slice_in_dim(b_low, cindex * col_slab + place % JB_DEV * BLK, BLK, 0)
            inner = jnp.einsum('ijk,jr->ikr', cube, b_tile, precision=high)
            term = lax.optimization_barrier(jnp.sum(inner * c_low[None], axis=1))
            start = rindex * row_slab + place // JB_DEV * BLK
            old = lax.dynamic_slice_in_dim(acc, start, BLK, 0)
            return lax.dynamic_update_slice_in_dim(acc, old + term, start, 0)
        return (lax.fori_loop(0, block_count[rindex, cindex], one_slot, total), None)
    m_one, _ = lax.scan(sweep_a, jnp.zeros((ROWS_A, R), jnp.float32), device_list)
    a_raw = solve_right(m_one, v_one)
    gram_a = jnp.dot(a_raw.T, a_raw, precision=high)
    scale_a = jnp.sqrt(jnp.diagonal(gram_a) / ROWS_A + norm_eps)
    factor_a_new = a_raw / scale_a[None, :]
    a_low = factor_a_new.astype(jnp.bfloat16).astype(jnp.float32)
    v_two = gram_a / (scale_a[:, None] * scale_a[None, :]) * gram_c

    def sweep_b(total, device):
        rindex = device // N_COL
        cindex = device % N_COL

        def one_slot(slot, acc):
            place = block_pos[rindex * SLOTS + slot, cindex]
            cube = fetch(rindex, cindex, slot)
            a_tile = lax.dynamic_slice_in_dim(a_low, rindex * row_slab + place // JB_DEV * BLK, BLK, 0)
            inner = jnp.einsum('ijk,ir->jkr', cube, a_tile, precision=high)
            term = lax.optimization_barrier(jnp.sum(inner * c_low[None], axis=1))
            start = cindex * col_slab + place % JB_DEV * BLK
            old = lax.dynamic_slice_in_dim(acc, start, BLK, 0)
            return lax.dynamic_update_slice_in_dim(acc, old + term, start, 0)
        return (lax.fori_loop(0, block_count[rindex, cindex], one_slot, total), None)
    m_two, _ = lax.scan(sweep_b, jnp.zeros((ROWS_B, R), jnp.float32), device_list)
    b_raw = solve_right(m_two, v_two)
    scale_b = jnp.sqrt(lax.optimization_barrier(jnp.sum(b_raw * b_raw, axis=0)) / ROWS_B + norm_eps)
    factor_b_new = b_raw / scale_b[None, :]
    return (factor_a_new, factor_b_new)
```

```python
import functools

import jax
import jax.numpy as jnp
from jax import lax
from jax.experimental import pallas as pl
from jax.experimental.pallas import tpu as pltpu
from jax.sharding import PartitionSpec as P

MESH = pl.DeviceIdType.MESH
HIGH = lax.Precision.HIGHEST
F32 = jnp.float32
BF16 = jnp.bfloat16
NROW, NCOL = 8, 32
R, K, BLK, SLOTS, IBD, JBD = 256, 64, 128, 4, 4, 2
SLAB_A = IBD * BLK
SLAB_B = JBD * BLK
WIDE = BLK * K
CHUNK = 1024
NCH = WIDE // CHUNK
JPC = CHUNK // K
SHARE_A = SLAB_A // NCOL
SHARE_B = SLAB_B // NROW
ROWS_A = SLAB_A * NROW
ROWS_B = SLAB_B * NCOL
EPS = 1e-06
MAX_IT = 80


def dot_hi(a, b):
    return jnp.dot(a, b, precision=HIGH, preferred_element_type=F32)


def wait_bytes(ref, sem):
    pltpu.make_async_copy(ref, ref, sem).wait()


def greet(axes):
    barrier = pltpu.get_barrier_semaphore()
    total = 0
    for axis, count in axes:
        me = lax.axis_index(axis)

        def one(k, carry, axis=axis, count=count, me=me):
            pl.semaphore_signal(
                barrier, inc=1, device_id={axis: lax.rem(me + k, count)}, device_id_type=MESH
            )
            return carry

        lax.fori_loop(1, count, one, 0)
        total += count - 1
    return barrier, total


def scatter(axis, count, src, dst, send, recv):
    me = lax.axis_index(axis)

    def one(k, carry):
        d = lax.rem(me + k, count)
        pltpu.make_async_remote_copy(
            src_ref=src.at[d], dst_ref=dst.at[k - 1], send_sem=send, recv_sem=recv,
            device_id={axis: d}, device_id_type=MESH,
        ).start()
        return carry

    lax.fori_loop(1, count, one, 0)


def gather(axis, count, piece, send, recv):
    me = lax.axis_index(axis)

    def one(k, carry):
        pltpu.make_async_remote_copy(
            src_ref=piece, dst_ref=piece, send_sem=send, recv_sem=recv,
            device_id={axis: lax.rem(me + k, count)}, device_id_type=MESH,
        ).start()
        return carry

    lax.fori_loop(1, count, one, 0)


def spread(axis, count, src, dst, send, recv):
    me = lax.axis_index(axis)

    def one(k, carry):
        pltpu.make_async_remote_copy(
            src_ref=src, dst_ref=dst.at[k - 1], send_sem=send, recv_sem=recv,
            device_id={axis: lax.rem(me + k, count)}, device_id_type=MESH,
        ).start()
        return carry

    lax.fori_loop(1, count, one, 0)


def kernel_a(
    pos, cnt, x_hbm, b_ref, c_ref,
    gb_out, m16_out, ms_out, g_out,
    x_v, x_sem, br, w_v, acc,
    gram, gb_part, gb_recv, gb_col, gb_full,
    part, m_recv, ms, g_recv, g_piece, g_full,
    send, recv,
):
    me_r, me_c = lax.axis_index("row"), lax.axis_index("col")

    def x_copy(ch):
        cols = pl.ds(pl.multiple_of(ch * CHUNK, CHUNK), CHUNK)
        return pltpu.make_async_copy(x_hbm.at[:, cols], x_v.at[:, cols], x_sem.at[ch])

    for ch in range(NCH):
        x_copy(ch).start()
    barrier, partners = greet((("col", NCOL), ("row", NROW)))

    b = b_ref[...]
    gram[...] = dot_hi(b.T, b)
    rows = gram[pl.ds(pl.multiple_of(me_r * 32, 32), 32), :]
    for i in range(32):
        gb_part[i] = rows[i:i + 1, :]
    br[...] = b.astype(BF16).astype(F32)
    cr = c_ref[...].astype(BF16).astype(F32)
    acc[...] = jnp.zeros_like(acc)

    def mode_one(ch, carry):
        for jb in range(JBD):
            tile = br[pl.ds(pl.multiple_of(jb * BLK + ch * JPC, JPC), JPC), :]
            for j in range(JPC):
                w_v[j * K:(j + 1) * K, jb * R:(jb + 1) * R] = (tile[j:j + 1, :] * cr).astype(BF16)
        x_copy(ch).wait()
        x = x_v[:, pl.ds(pl.multiple_of(ch * CHUNK, CHUNK), CHUNK)]
        acc[...] += jnp.dot(x, w_v[...], preferred_element_type=F32)
        return carry

    lax.fori_loop(0, NCH, mode_one, 0)
    count = cnt[0, 0]
    for ib in range(IBD):
        total = jnp.zeros((BLK, R), F32)
        for s in range(SLOTS):
            p = pos[s, 0]
            live = jnp.where(count > s, 1.0, 0.0).astype(F32)
            for jb in range(JBD):
                keep = jnp.where(p == ib * JBD + jb, live, 0.0)
                total += acc[s * BLK:(s + 1) * BLK, jb * R:(jb + 1) * R] * keep
        low = total.astype(BF16)
        for t in range(BLK // SHARE_A):
            part[ib * (BLK // SHARE_A) + t] = low[t * SHARE_A:(t + 1) * SHARE_A, :]

    pl.semaphore_wait(barrier, partners)
    scatter("col", NCOL, gb_part, gb_recv, send.at[0], recv.at[0])
    scatter("col", NCOL, part, m_recv, send.at[1], recv.at[1])

    wait_bytes(gb_recv, recv.at[0])
    gb_col[me_c] = gb_part[me_c] + jnp.sum(gb_recv[...], axis=0)
    gather("col", NCOL, gb_col.at[me_c], send.at[2], recv.at[2])

    wait_bytes(m_recv, recv.at[1])
    m16 = part[me_c].astype(F32) + jnp.sum(m_recv[...].astype(F32), axis=0)
    m16_out[...] = m16
    ms[me_c] = m16.astype(BF16)
    gather("col", NCOL, ms.at[me_c], send.at[3], recv.at[3])

    wait_bytes(gb_col.at[pl.ds(0, NCOL - 1)], recv.at[2])
    for i in range(32):
        gb_full[me_r, i:i + 1, :] = gb_col[i]
    gather("row", NROW, gb_full.at[me_r], send.at[4], recv.at[4])

    wait_bytes(ms.at[pl.ds(0, NCOL - 1)], recv.at[3])
    slab = ms[...].reshape(SLAB_A, R)
    ms_out[...] = slab
    gram[...] = jnp.dot(slab.T, slab, preferred_element_type=F32)
    g_piece[...] = gram[pl.ds(pl.multiple_of(me_c * 8, 8), 8), :]
    spread("row", NROW, g_piece, g_recv, send.at[5], recv.at[5])

    wait_bytes(gb_full.at[pl.ds(0, NROW - 1)], recv.at[4])
    gb_out[...] = gb_full[...].reshape(R, R)

    wait_bytes(g_recv, recv.at[5])
    g_full[me_c] = g_piece[...] + jnp.sum(g_recv[...], axis=0)
    gather("col", NCOL, g_full.at[me_c], send.at[6], recv.at[6])
    wait_bytes(g_full.at[pl.ds(0, NCOL - 1)], recv.at[6])
    g_out[...] = g_full[...].reshape(R, R)

    wait_bytes(gb_recv, send.at[0])
    wait_bytes(m_recv, send.at[1])
    wait_bytes(gb_col.at[pl.ds(0, NCOL - 1)], send.at[2])
    wait_bytes(ms.at[pl.ds(0, NCOL - 1)], send.at[3])
    wait_bytes(gb_full.at[pl.ds(0, NROW - 1)], send.at[4])
    wait_bytes(g_recv, send.at[5])
    wait_bytes(g_full.at[pl.ds(0, NCOL - 1)], send.at[6])


def eye():
    return lax.broadcasted_iota(jnp.int32, (R, R), 0) == lax.broadcasted_iota(jnp.int32, (R, R), 1)


def diagonals(v):
    only = jnp.where(eye(), v, 0.0)
    return jnp.sum(only, axis=1, keepdims=True), jnp.sum(only, axis=0, keepdims=True)


def inverse(v, x_ref, r_ref, c_ref):
    down, across = diagonals(v)
    down, across = 1.0 / jnp.sqrt(down), 1.0 / jnp.sqrt(across)
    unit = jnp.where(eye(), 1.0, 0.0)
    c = v * down * across
    c_ref[...] = c
    norm = jnp.max(jnp.sum(jnp.abs(c), axis=1, keepdims=True))
    alpha = jnp.where(norm < 1.9, 1.0, 1.0 / norm)
    res = unit - alpha * c
    x_ref[...] = alpha * (unit + res)
    res = unit - dot_hi(c, x_ref[...])
    r_ref[...] = res

    def more(state):
        it, size, before = state
        return (it < MAX_IT) & (size > 1e-5) & ((size > 1e-3) | (size < 0.5 * before))

    def step(state):
        it, size, _ = state
        x = x_ref[...]
        x = x + dot_hi(x, r_ref[...])
        x_ref[...] = x
        res = unit - dot_hi(c_ref[...], x)
        r_ref[...] = res
        return it + 1, jnp.max(jnp.abs(res)), size

    lax.while_loop(more, step, (0, jnp.max(jnp.abs(res)), jnp.float32(1e30)))
    x = x_ref[...]
    x = x + dot_hi(x, r_ref[...])
    return x * down * across


def kernel_b(
    pos, cnt, x_hbm, c_ref, gb_ref, m16_ref, ms_ref, g_ref,
    a_out, pb_out, inv_out,
    x_v, x_sem, x1, r1, c1, slab, lhs, ct, acc,
):
    def x_copy(ch):
        cols = pl.ds(pl.multiple_of(ch * CHUNK, CHUNK), CHUNK)
        return pltpu.make_async_copy(x_hbm.at[:, cols], x_v.at[:, cols], x_sem.at[ch])

    for ch in range(NCH):
        x_copy(ch).start()
    c = c_ref[...]
    gram_c = dot_hi(c.T, c)
    inv1 = inverse(gb_ref[...] * gram_c, x1, r1, c1)
    gram_a = dot_hi(dot_hi(inv1, g_ref[...]), inv1)
    down, across = diagonals(gram_a)
    down = 1.0 / jnp.sqrt(down / ROWS_A + EPS)
    across = 1.0 / jnp.sqrt(across / ROWS_A + EPS)
    a_out[...] = dot_hi(m16_ref[...], inv1) * across
    slab[...] = dot_hi(ms_ref[...].astype(F32), inv1) * across

    inv_out[...] = inverse(gram_a * down * across * gram_c, x1, r1, c1)

    count = cnt[0, 0]
    for s in range(SLOTS):
        p = pos[s, 0]
        tile = slab[pl.ds(pl.multiple_of(lax.shift_right_logical(p, 1) * BLK, BLK), BLK), :].T
        for jb in range(JBD):
            keep = jnp.where((count > s) & ((p & 1) == jb), 1.0, 0.0)
            lhs[jb * R:(jb + 1) * R, s * BLK:(s + 1) * BLK] = (tile * keep).astype(BF16)
    c_low = c.astype(BF16).astype(F32).T
    for jb in range(JBD):
        for t in range(CHUNK // K):
            ct[jb * R:(jb + 1) * R, t * K:(t + 1) * K] = c_low
    acc[...] = jnp.zeros_like(acc)

    def mode_two(ch, carry):
        x_copy(ch).wait()
        x = x_v[:, pl.ds(pl.multiple_of(ch * CHUNK, CHUNK), CHUNK)]
        t = jnp.dot(lhs[...], x, preferred_element_type=F32)
        t = (t * ct[...]).astype(BF16)
        j = lax.shift_right_logical(lax.broadcasted_iota(jnp.int32, (CHUNK, BLK), 0), 6) + ch * JPC
        ones = jnp.where(j == lax.broadcasted_iota(jnp.int32, (CHUNK, BLK), 1), 1.0, 0.0).astype(BF16)
        acc[...] += jnp.dot(t, ones, preferred_element_type=F32)
        return carry

    lax.fori_loop(0, NCH, mode_two, 0)
    for jb in range(JBD):
        pb_out[jb * BLK:(jb + 1) * BLK, :] = acc[jb * R:(jb + 1) * R, :].T.astype(BF16)


def kernel_c(pb_ref, inv_ref, b_out, pb_recv, sq_piece, sq_row, sq_all, sq_col, send, recv):
    me_r = lax.axis_index("row")
    barrier, partners = greet((("row", NROW), ("col", NCOL)))
    pl.semaphore_wait(barrier, partners)
    scatter("row", NROW, pb_ref, pb_recv, send.at[0], recv.at[0])
    wait_bytes(pb_recv, recv.at[0])
    m2 = pb_ref[me_r].astype(F32) + jnp.sum(pb_recv[...].astype(F32), axis=0)
    raw = dot_hi(m2, inv_ref[...])
    sq_piece[...] = jnp.sum(raw * raw, axis=0, keepdims=True)
    spread("row", NROW, sq_piece, sq_row, send.at[1], recv.at[1])
    wait_bytes(sq_row, recv.at[1])
    sq_all[...] = sq_piece[...] + jnp.sum(sq_row[...], axis=0)
    spread("col", NCOL, sq_all, sq_col, send.at[2], recv.at[2])
    wait_bytes(sq_col, recv.at[2])
    squares = sq_all[...] + jnp.sum(sq_col[...], axis=0)
    b_out[...] = raw / jnp.sqrt(squares / ROWS_B + EPS)
    wait_bytes(pb_recv, send.at[0])
    wait_bytes(sq_row, send.at[1])
    wait_bytes(sq_col, send.at[2])


VM = pl.BlockSpec(memory_space=pltpu.VMEM)
SM = pl.BlockSpec(memory_space=pltpu.SMEM)
ANY = pl.BlockSpec(memory_space=pl.ANY)


def shape(dims, kind=F32):
    return jax.ShapeDtypeStruct(dims, kind)


def body(blocks, factor_b, factor_c, block_pos, block_count):
    flat = blocks.reshape(SLOTS * BLK, WIDE)
    vm, dma = pltpu.VMEM, pltpu.SemaphoreType.DMA
    gram_b, m16, ms, g = pl.pallas_call(
        kernel_a,
        name="mode_one",
        out_shape=(shape((R, R)), shape((SHARE_A, R)), shape((SLAB_A, R), BF16), shape((R, R))),
        in_specs=[SM, SM, ANY, VM, VM],
        out_specs=[VM] * 4,
        scratch_shapes=[
            vm((SLAB_A, WIDE), BF16), dma((NCH,)), vm((R, R), F32), vm((CHUNK, JBD * R), BF16), vm((SLAB_A, JBD * R), F32),
            vm((R, R), F32), vm((NCOL, 1, R), F32), vm((NCOL - 1, 1, R), F32), vm((NCOL, 1, R), F32), vm((NROW, 32, R), F32),
            vm((NCOL, SHARE_A, R), BF16), vm((NCOL - 1, SHARE_A, R), BF16), vm((NCOL, SHARE_A, R), BF16),
            vm((NROW - 1, 8, R), F32), vm((8, R), F32), vm((NCOL, 8, R), F32),
            dma((7,)), dma((7,)),
        ],
        compiler_params=pltpu.CompilerParams(collective_id=0, has_side_effects=True),
    )(block_pos, block_count, flat, factor_b, factor_c)
    hat_a, part_b, inv = pl.pallas_call(
        kernel_b,
        name="solve_two",
        out_shape=(shape((SHARE_A, R)), shape((SLAB_B, R), BF16), shape((R, R))),
        in_specs=[SM, SM, ANY, VM, VM, VM, VM, VM],
        out_specs=[VM] * 3,
        scratch_shapes=[
            vm((SLAB_A, WIDE), BF16), dma((NCH,)), vm((R, R), F32), vm((R, R), F32), vm((R, R), F32),
            vm((SLAB_A, R), F32), vm((JBD * R, SLAB_A), BF16), vm((JBD * R, CHUNK), F32), vm((JBD * R, BLK), F32),
        ],
    )(block_pos, block_count, flat, factor_c, gram_b, m16, ms, g)
    hat_b = pl.pallas_call(
        kernel_c,
        name="mode_two",
        out_shape=shape((SHARE_B, R)),
        in_specs=[VM, VM],
        out_specs=VM,
        scratch_shapes=[
            vm((NROW - 1, SHARE_B, R), BF16), vm((1, R), F32), vm((NROW - 1, 1, R), F32), vm((1, R), F32),
            vm((NCOL - 1, 1, R), F32), dma((3,)), dma((3,)),
        ],
        compiler_params=pltpu.CompilerParams(collective_id=1, has_side_effects=True),
    )(part_b.reshape(NROW, SHARE_B, R), inv)
    return hat_a, hat_b


def solution(mesh):
    return jax.shard_map(
        body,
        mesh=mesh,
        in_specs=(P("row", "col", None), P("col", None), P(), P("row", "col"), P("row", "col")),
        out_specs=(P(("row", "col"), None), P(("col", "row"), None)),
        check_vma=False,
    )
```

```python
import functools

import jax
import jax.numpy as jnp
from jax import lax
from jax.experimental import pallas as pl
from jax.experimental.pallas import tpu as pltpu
from jax.sharding import PartitionSpec as P

MESH = pl.DeviceIdType.MESH
HIGH = lax.Precision.HIGHEST
F32 = jnp.float32
BF16 = jnp.bfloat16
NROW, NCOL = 8, 32
R, K, BLK, SLOTS, IBD, JBD = 256, 64, 128, 4, 4, 2
SLAB_A = IBD * BLK
SLAB_B = JBD * BLK
WIDE = BLK * K
CHUNK = 1024
NCH = WIDE // CHUNK
JPC = CHUNK // K
SHARE_A = SLAB_A // NCOL
SHARE_B = SLAB_B // NROW
CHIPS = NCOL // 2
SHARE_G = BLK // NROW
ROWS_A = SLAB_A * NROW
ROWS_B = SLAB_B * NCOL
EPS = 1e-06
MAX_IT = 80


def dot_hi(a, b):
    return jnp.dot(a, b, precision=HIGH, preferred_element_type=F32)


def wait_bytes(ref, sem):
    pltpu.make_async_copy(ref, ref, sem).wait()


def greet(axes):
    barrier = pltpu.get_barrier_semaphore()
    total = 0
    for axis, count in axes:
        me = lax.axis_index(axis)

        def one(k, carry, axis=axis, count=count, me=me):
            pl.semaphore_signal(
                barrier, inc=1, device_id={axis: lax.rem(me + k, count)}, device_id_type=MESH
            )
            return carry

        lax.fori_loop(1, count, one, 0)
        total += count - 1
    return barrier, total


def scatter(axis, count, src, dst, send, recv):
    me = lax.axis_index(axis)

    def one(k, carry):
        d = lax.rem(me + k, count)
        pltpu.make_async_remote_copy(
            src_ref=src.at[d], dst_ref=dst.at[k - 1], send_sem=send, recv_sem=recv,
            device_id={axis: d}, device_id_type=MESH,
        ).start()
        return carry

    lax.fori_loop(1, count, one, 0)


def gather(axis, count, piece, send, recv):
    me = lax.axis_index(axis)

    def one(k, carry):
        pltpu.make_async_remote_copy(
            src_ref=piece, dst_ref=piece, send_sem=send, recv_sem=recv,
            device_id={axis: lax.rem(me + k, count)}, device_id_type=MESH,
        ).start()
        return carry

    lax.fori_loop(1, count, one, 0)


def spread(axis, count, src, dst, send, recv):
    me = lax.axis_index(axis)

    def one(k, carry):
        pltpu.make_async_remote_copy(
            src_ref=src, dst_ref=dst.at[k - 1], send_sem=send, recv_sem=recv,
            device_id={axis: lax.rem(me + k, count)}, device_id_type=MESH,
        ).start()
        return carry

    lax.fori_loop(1, count, one, 0)


def kernel_a(
    pos, cnt, x_hbm, b_ref, c_ref,
    gb_out, m16_out, ms_out, g_out,
    x_v, x_sem, br, w_v, acc,
    gram, gb_part, gb_recv, gb_col, gb_full,
    part, pair_recv, half, m_recv, ms, g_piece, g_recv, g_full,
    send, recv,
):
    me_r, me_c = lax.axis_index("row"), lax.axis_index("col")
    chip, core = me_c // 2, lax.rem(me_c, 2)
    mate = chip * 2 + 1 - core

    def to_mate(src, dst, n):
        pltpu.make_async_remote_copy(
            src_ref=src, dst_ref=dst, send_sem=send.at[n], recv_sem=recv.at[n],
            device_id={"col": mate}, device_id_type=MESH,
        ).start()

    def x_copy(ch):
        cols = pl.ds(pl.multiple_of(ch * CHUNK, CHUNK), CHUNK)
        return pltpu.make_async_copy(x_hbm.at[:, cols], x_v.at[:, cols], x_sem.at[ch])

    for ch in range(NCH):
        x_copy(ch).start()
    barrier, partners = greet((("col", NCOL), ("row", NROW)))

    b = b_ref[...]
    gram[...] = dot_hi(b.T, b)
    rows = gram[pl.ds(pl.multiple_of(me_r * 32, 32), 32), :]
    for i in range(32):
        gb_part[i] = rows[i:i + 1, :]
    br[...] = b.astype(BF16).astype(F32)
    cr = c_ref[...].astype(BF16).astype(F32)
    acc[...] = jnp.zeros_like(acc)

    def mode_one(ch, carry):
        for jb in range(JBD):
            tile = br[pl.ds(pl.multiple_of(jb * BLK + ch * JPC, JPC), JPC), :]
            for j in range(JPC):
                w_v[j * K:(j + 1) * K, jb * R:(jb + 1) * R] = (tile[j:j + 1, :] * cr).astype(BF16)
        x_copy(ch).wait()
        x = x_v[:, pl.ds(pl.multiple_of(ch * CHUNK, CHUNK), CHUNK)]
        acc[...] += jnp.dot(x, w_v[...], preferred_element_type=F32)
        return carry

    lax.fori_loop(0, NCH - 3, mode_one, 0)
    pl.semaphore_wait(barrier, partners)
    scatter("col", NCOL, gb_part, gb_recv, send.at[0], recv.at[0])
    lax.fori_loop(NCH - 3, NCH, mode_one, 0)

    count = cnt[0, 0]
    for ib in range(IBD):
        total = jnp.zeros((BLK, R), F32)
        for s in range(SLOTS):
            p = pos[0, s]
            live = jnp.where(count > s, 1.0, 0.0).astype(F32)
            for jb in range(JBD):
                keep = jnp.where(p == ib * JBD + jb, live, 0.0)
                total += acc[s * BLK:(s + 1) * BLK, jb * R:(jb + 1) * R] * keep
        for t in range(BLK // SHARE_A):
            at = ib * (BLK // SHARE_A) + t
            part[at % 2, at // 2] = total[t * SHARE_A:(t + 1) * SHARE_A, :]

    to_mate(part.at[1 - core], pair_recv, 1)
    wait_bytes(pair_recv, recv.at[1])
    half[...] = (part[core] + pair_recv[...]).astype(BF16)

    def to_chip(k, carry):
        d = lax.rem(chip + k, CHIPS)
        pltpu.make_async_remote_copy(
            src_ref=half.at[d], dst_ref=m_recv.at[k - 1], send_sem=send.at[2], recv_sem=recv.at[2],
            device_id={"col": d * 2 + core}, device_id_type=MESH,
        ).start()
        return carry

    lax.fori_loop(1, CHIPS, to_chip, 0)

    wait_bytes(gb_recv, recv.at[0])
    gb_col[me_c] = gb_part[me_c] + jnp.sum(gb_recv[...], axis=0)
    gather("col", NCOL, gb_col.at[me_c], send.at[3], recv.at[3])

    wait_bytes(m_recv, recv.at[2])
    m16 = part[core, chip] + pair_recv[chip] + jnp.sum(m_recv[...].astype(F32), axis=0)
    ms[core, chip] = m16.astype(BF16)

    def from_chip(k, carry):
        piece = ms.at[core, chip]
        pltpu.make_async_remote_copy(
            src_ref=piece, dst_ref=piece, send_sem=send.at[4], recv_sem=recv.at[4],
            device_id={"col": lax.rem(chip + k, CHIPS) * 2 + core}, device_id_type=MESH,
        ).start()
        return carry

    lax.fori_loop(1, CHIPS, from_chip, 0)
    m16_out[...] = m16

    wait_bytes(gb_col.at[pl.ds(0, NCOL - 1)], recv.at[3])
    for i in range(32):
        gb_full[me_r, i:i + 1, :] = gb_col[i]
    gather("row", NROW, gb_full.at[me_r], send.at[5], recv.at[5])

    wait_bytes(m_recv, recv.at[4])
    to_mate(ms.at[core], ms.at[core], 6)
    wait_bytes(ms.at[0], recv.at[6])

    slab = ms[...].reshape(SLAB_A, R)
    gram[...] = jnp.dot(slab.T, slab, preferred_element_type=F32)
    g_piece[...] = gram[pl.ds(pl.multiple_of(core * BLK, BLK), BLK), :].reshape(NROW, SHARE_G, R)
    scatter("row", NROW, g_piece, g_recv, send.at[7], recv.at[7])
    for at in range(NCOL):
        ms_out[at * SHARE_A:(at + 1) * SHARE_A, :] = ms[at % 2, at // 2]
    wait_bytes(g_recv, recv.at[7])
    g_full[core, me_r] = g_piece[me_r] + jnp.sum(g_recv[...], axis=0)
    gather("row", NROW, g_full.at[core, me_r], send.at[8], recv.at[8])
    wait_bytes(gb_full.at[pl.ds(0, NROW - 1)], recv.at[5])
    gb_out[...] = gb_full[...].reshape(R, R)
    wait_bytes(g_recv, recv.at[8])
    to_mate(g_full.at[core], g_full.at[core], 9)
    wait_bytes(g_full.at[0], recv.at[9])
    g_out[...] = g_full[...].reshape(R, R)

    wait_bytes(gb_recv, send.at[0])
    wait_bytes(pair_recv, send.at[1])
    wait_bytes(m_recv, send.at[2])
    wait_bytes(gb_col.at[pl.ds(0, NCOL - 1)], send.at[3])
    wait_bytes(m_recv, send.at[4])
    wait_bytes(gb_full.at[pl.ds(0, NROW - 1)], send.at[5])
    wait_bytes(ms.at[0], send.at[6])
    wait_bytes(g_recv, send.at[7])
    wait_bytes(g_recv, send.at[8])
    wait_bytes(g_full.at[0], send.at[9])


def eye():
    return lax.broadcasted_iota(jnp.int32, (R, R), 0) == lax.broadcasted_iota(jnp.int32, (R, R), 1)


def diagonals(v):
    only = jnp.where(eye(), v, 0.0)
    return jnp.sum(only, axis=1, keepdims=True), jnp.sum(only, axis=0, keepdims=True)


def inverse(v, x_ref, r_ref, c_ref):
    down, across = diagonals(v)
    down, across = 1.0 / jnp.sqrt(down), 1.0 / jnp.sqrt(across)
    unit = jnp.where(eye(), 1.0, 0.0)
    c = v * down * across
    c_ref[...] = c
    norm = jnp.max(jnp.sum(jnp.abs(c), axis=1, keepdims=True))
    alpha = jnp.where(norm < 1.9, 1.0, 1.0 / norm)
    res = unit - alpha * c
    x_ref[...] = alpha * (unit + res)
    res = unit - dot_hi(c, x_ref[...])
    r_ref[...] = res

    def more(state):
        it, size, before = state
        return (it < MAX_IT) & (size > 1e-5) & ((size > 1e-3) | (size < 0.5 * before))

    def step(state):
        it, size, _ = state
        x = x_ref[...]
        x = x + dot_hi(x, r_ref[...])
        x_ref[...] = x
        res = unit - dot_hi(c_ref[...], x)
        r_ref[...] = res
        return it + 1, jnp.max(jnp.abs(res)), size

    lax.while_loop(more, step, (0, jnp.max(jnp.abs(res)), jnp.float32(1e30)))
    x = x_ref[...]
    x = x + dot_hi(x, r_ref[...])
    return x * down * across


def kernel_b(
    pos, cnt, c_ref, gb_ref, m16_ref, ms_ref, g_ref,
    a_out, lhs_out, inv_out,
    x1, r1, c1, slab,
):
    c = c_ref[...]
    gram_c = dot_hi(c.T, c)
    inv1 = inverse(gb_ref[...] * gram_c, x1, r1, c1)
    gram_a = dot_hi(dot_hi(inv1, g_ref[...]), inv1)
    down, across = diagonals(gram_a)
    down = 1.0 / jnp.sqrt(down / ROWS_A + EPS)
    across = 1.0 / jnp.sqrt(across / ROWS_A + EPS)
    a_out[...] = dot_hi(m16_ref[...], inv1) * across
    slab[...] = dot_hi(ms_ref[...].astype(F32), inv1) * across

    inv_out[...] = inverse(gram_a * down * across * gram_c, x1, r1, c1)

    count = cnt[0, 0]
    for s in range(SLOTS):
        p = pos[0, s]
        tile = slab[pl.ds(pl.multiple_of(lax.shift_right_logical(p, 1) * BLK, BLK), BLK), :].T
        for jb in range(JBD):
            keep = jnp.where((count > s) & ((p & 1) == jb), 1.0, 0.0)
            lhs_out[jb * R:(jb + 1) * R, s * BLK:(s + 1) * BLK] = (tile * keep).astype(BF16)


def kernel_c(
    x_hbm, c_ref, lhs, inv_ref,
    b_out,
    x_v, x_sem, ct, acc, pb, pb_recv, sq_piece, sq_row, sq_all, sq_col, send, recv,
):
    me_r = lax.axis_index("row")

    def x_copy(ch):
        cols = pl.ds(pl.multiple_of(ch * CHUNK, CHUNK), CHUNK)
        return pltpu.make_async_copy(x_hbm.at[:, cols], x_v.at[:, cols], x_sem.at[ch])

    for ch in range(NCH):
        x_copy(ch).start()
    barrier, partners = greet((("row", NROW), ("col", NCOL)))
    c_low = c_ref[...].astype(BF16).astype(F32).T
    for jb in range(JBD):
        for t in range(CHUNK // K):
            ct[jb * R:(jb + 1) * R, t * K:(t + 1) * K] = c_low
    acc[...] = jnp.zeros_like(acc)

    def mode_two(ch, carry):
        x_copy(ch).wait()
        x = x_v[:, pl.ds(pl.multiple_of(ch * CHUNK, CHUNK), CHUNK)]
        t = jnp.dot(lhs[...], x, preferred_element_type=F32)
        t = (t * ct[...]).astype(BF16)
        j = lax.shift_right_logical(lax.broadcasted_iota(jnp.int32, (CHUNK, BLK), 0), 6) + ch * JPC
        ones = jnp.where(j == lax.broadcasted_iota(jnp.int32, (CHUNK, BLK), 1), 1.0, 0.0).astype(BF16)
        acc[...] += jnp.dot(t, ones, preferred_element_type=F32)
        return carry

    lax.fori_loop(0, NCH, mode_two, 0)
    for jb in range(JBD):
        rows = acc[jb * R:(jb + 1) * R, :].T.astype(BF16)
        for t in range(BLK // SHARE_B):
            pb[jb * (BLK // SHARE_B) + t] = rows[t * SHARE_B:(t + 1) * SHARE_B, :]

    pl.semaphore_wait(barrier, partners)
    scatter("row", NROW, pb, pb_recv, send.at[0], recv.at[0])
    wait_bytes(pb_recv, recv.at[0])
    m2 = pb[me_r].astype(F32) + jnp.sum(pb_recv[...].astype(F32), axis=0)
    raw = dot_hi(m2, inv_ref[...])
    sq_piece[...] = jnp.sum(raw * raw, axis=0, keepdims=True)
    spread("row", NROW, sq_piece, sq_row, send.at[1], recv.at[1])
    wait_bytes(sq_row, recv.at[1])
    sq_all[...] = sq_piece[...] + jnp.sum(sq_row[...], axis=0)
    spread("col", NCOL, sq_all, sq_col, send.at[2], recv.at[2])
    wait_bytes(sq_col, recv.at[2])
    squares = sq_all[...] + jnp.sum(sq_col[...], axis=0)
    b_out[...] = raw / jnp.sqrt(squares / ROWS_B + EPS)
    wait_bytes(pb_recv, send.at[0])
    wait_bytes(sq_row, send.at[1])
    wait_bytes(sq_col, send.at[2])


VM = pl.BlockSpec(memory_space=pltpu.VMEM)
SM = pl.BlockSpec(memory_space=pltpu.SMEM)
ANY = pl.BlockSpec(memory_space=pl.ANY)


def shape(dims, kind=F32):
    return jax.ShapeDtypeStruct(dims, kind)


def body(blocks, factor_b, factor_c, block_pos, block_count):
    flat = blocks.reshape(SLOTS * BLK, WIDE)
    place = block_pos.T
    vm, dma = pltpu.VMEM, pltpu.SemaphoreType.DMA
    gram_b, m16, ms, g = pl.pallas_call(
        kernel_a,
        name="mode_one",
        out_shape=(shape((R, R)), shape((SHARE_A, R)), shape((SLAB_A, R), BF16), shape((R, R))),
        in_specs=[SM, SM, ANY, VM, VM],
        out_specs=[VM] * 4,
        scratch_shapes=[
            vm((SLAB_A, WIDE), BF16), dma((NCH,)), vm((R, R), F32), vm((CHUNK, JBD * R), BF16), vm((SLAB_A, JBD * R), F32),
            vm((R, R), F32), vm((NCOL, 1, R), F32), vm((NCOL - 1, 1, R), F32), vm((NCOL, 1, R), F32), vm((NROW, 32, R), F32),
            vm((2, CHIPS, SHARE_A, R), F32), vm((CHIPS, SHARE_A, R), F32), vm((CHIPS, SHARE_A, R), BF16),
            vm((CHIPS - 1, SHARE_A, R), BF16), vm((2, CHIPS, SHARE_A, R), BF16),
            vm((NROW, SHARE_G, R), F32), vm((NROW - 1, SHARE_G, R), F32), vm((2, NROW, SHARE_G, R), F32),
            dma((10,)), dma((10,)),
        ],
        compiler_params=pltpu.CompilerParams(collective_id=0, has_side_effects=True),
    )(place, block_count, flat, factor_b, factor_c)
    hat_a, lhs, inv = pl.pallas_call(
        kernel_b,
        name="solve_two",
        out_shape=(shape((SHARE_A, R)), shape((JBD * R, SLAB_A), BF16), shape((R, R))),
        in_specs=[SM, SM, VM, VM, VM, VM, VM],
        out_specs=[VM] * 3,
        scratch_shapes=[vm((R, R), F32), vm((R, R), F32), vm((R, R), F32), vm((SLAB_A, R), F32)],
    )(place, block_count, factor_c, gram_b, m16, ms, g)
    hat_b = pl.pallas_call(
        kernel_c,
        name="mode_two",
        out_shape=shape((SHARE_B, R)),
        in_specs=[ANY, VM, VM, VM],
        out_specs=VM,
        scratch_shapes=[
            vm((SLAB_A, WIDE), BF16), dma((NCH,)), vm((JBD * R, CHUNK), F32), vm((JBD * R, BLK), F32),
            vm((NROW, SHARE_B, R), BF16), vm((NROW - 1, SHARE_B, R), BF16),
            vm((1, R), F32), vm((NROW - 1, 1, R), F32), vm((1, R), F32), vm((NCOL - 1, 1, R), F32),
            dma((3,)), dma((3,)),
        ],
        compiler_params=pltpu.CompilerParams(collective_id=1, has_side_effects=True),
    )(flat, factor_c, lhs, inv)
    return hat_a, hat_b


def solution(mesh):
    return jax.shard_map(
        body,
        mesh=mesh,
        in_specs=(P("row", "col", None), P("col", None), P(), P("row", "col"), P("row", "col")),
        out_specs=(P(("row", "col"), None), P(("col", "row"), None)),
        check_vma=False,
    )
```

```python
import functools

import jax
import jax.numpy as jnp
from jax import lax
from jax.experimental import pallas as pl
from jax.experimental.pallas import tpu as pltpu
from jax.sharding import PartitionSpec as P

MESH = pl.DeviceIdType.MESH
HIGH = lax.Precision.HIGHEST
F32 = jnp.float32
BF16 = jnp.bfloat16
NROW, NCOL = 8, 32
R, K, BLK, SLOTS, IBD, JBD = 256, 64, 128, 4, 4, 2
SLAB_A = IBD * BLK
SLAB_B = JBD * BLK
WIDE = BLK * K
CHUNK = 1024
NCH = WIDE // CHUNK
JPC = CHUNK // K
SHARE_A = SLAB_A // NCOL
SHARE_B = SLAB_B // NROW
CHIPS = NCOL // 2
SHARE_G = BLK // NROW
ROWS_A = SLAB_A * NROW
ROWS_B = SLAB_B * NCOL
EPS = 1e-06
MAX_IT = 80


def dot_hi(a, b):
    return jnp.dot(a, b, precision=HIGH, preferred_element_type=F32)


def wait_bytes(ref, sem):
    pltpu.make_async_copy(ref, ref, sem).wait()


def greet(axes):
    barrier = pltpu.get_barrier_semaphore()
    total = 0
    for axis, count in axes:
        me = lax.axis_index(axis)

        def one(k, carry, axis=axis, count=count, me=me):
            pl.semaphore_signal(
                barrier, inc=1, device_id={axis: lax.rem(me + k, count)}, device_id_type=MESH
            )
            return carry

        lax.fori_loop(1, count, one, 0)
        total += count - 1
    return barrier, total


def scatter(axis, count, src, dst, send, recv):
    me = lax.axis_index(axis)

    def one(k, carry):
        d = lax.rem(me + k, count)
        pltpu.make_async_remote_copy(
            src_ref=src.at[d], dst_ref=dst.at[k - 1], send_sem=send, recv_sem=recv,
            device_id={axis: d}, device_id_type=MESH,
        ).start()
        return carry

    lax.fori_loop(1, count, one, 0)


def gather(axis, count, piece, send, recv):
    me = lax.axis_index(axis)

    def one(k, carry):
        pltpu.make_async_remote_copy(
            src_ref=piece, dst_ref=piece, send_sem=send, recv_sem=recv,
            device_id={axis: lax.rem(me + k, count)}, device_id_type=MESH,
        ).start()
        return carry

    lax.fori_loop(1, count, one, 0)


def spread(axis, count, src, dst, send, recv):
    me = lax.axis_index(axis)

    def one(k, carry):
        pltpu.make_async_remote_copy(
            src_ref=src, dst_ref=dst.at[k - 1], send_sem=send, recv_sem=recv,
            device_id={axis: lax.rem(me + k, count)}, device_id_type=MESH,
        ).start()
        return carry

    lax.fori_loop(1, count, one, 0)


def kernel_a(
    pos, cnt, x_hbm, b_ref, c_ref,
    gb_out, m16_out, ms_out, g_out,
    x_v, x_sem, br, w_v, acc,
    gram, gb_part, gb_recv, gb_col, gb_full,
    part, pair_recv, half, m_recv, ms, g_piece, g_recv, g_full,
    send, recv,
):
    me_r, me_c = lax.axis_index("row"), lax.axis_index("col")
    chip, core = me_c // 2, lax.rem(me_c, 2)
    mate = chip * 2 + 1 - core

    def to_mate(src, dst, n):
        pltpu.make_async_remote_copy(
            src_ref=src, dst_ref=dst, send_sem=send.at[n], recv_sem=recv.at[n],
            device_id={"col": mate}, device_id_type=MESH,
        ).start()

    def x_copy(ch):
        cols = pl.ds(pl.multiple_of(ch * CHUNK, CHUNK), CHUNK)
        return pltpu.make_async_copy(x_hbm.at[:, cols], x_v.at[:, cols], x_sem.at[ch])

    for ch in range(NCH):
        x_copy(ch).start()
    barrier, partners = greet((("col", NCOL), ("row", NROW)))

    b = b_ref[...]
    gram[...] = dot_hi(b.T, b)
    rows = gram[pl.ds(pl.multiple_of(me_r * 32, 32), 32), :]
    for i in range(32):
        gb_part[i] = rows[i:i + 1, :]
    br[...] = b.astype(BF16).astype(F32)
    cr = c_ref[...].astype(BF16).astype(F32)
    acc[...] = jnp.zeros_like(acc)

    def mode_one(ch, carry):
        for jb in range(JBD):
            tile = br[pl.ds(pl.multiple_of(jb * BLK + ch * JPC, JPC), JPC), :]
            for j in range(JPC):
                w_v[j * K:(j + 1) * K, jb * R:(jb + 1) * R] = (tile[j:j + 1, :] * cr).astype(BF16)
        x_copy(ch).wait()
        x = x_v[:, pl.ds(pl.multiple_of(ch * CHUNK, CHUNK), CHUNK)]
        acc[...] += jnp.dot(x, w_v[...], preferred_element_type=F32)
        return carry

    lax.fori_loop(0, NCH - 3, mode_one, 0)
    pl.semaphore_wait(barrier, partners)
    scatter("col", NCOL, gb_part, gb_recv, send.at[0], recv.at[0])
    lax.fori_loop(NCH - 3, NCH, mode_one, 0)

    count = cnt[0, 0]
    for ib in range(IBD):
        total = jnp.zeros((BLK, R), F32)
        for s in range(SLOTS):
            p = pos[0, s]
            live = jnp.where(count > s, 1.0, 0.0).astype(F32)
            for jb in range(JBD):
                keep = jnp.where(p == ib * JBD + jb, live, 0.0)
                total += acc[s * BLK:(s + 1) * BLK, jb * R:(jb + 1) * R] * keep
        for t in range(BLK // SHARE_A):
            at = ib * (BLK // SHARE_A) + t
            part[at % 2, at // 2] = total[t * SHARE_A:(t + 1) * SHARE_A, :]

    to_mate(part.at[1 - core], pair_recv, 1)
    wait_bytes(pair_recv, recv.at[1])
    half[...] = (part[core] + pair_recv[...]).astype(BF16)

    def to_chip(k, carry):
        d = lax.rem(chip + k, CHIPS)
        pltpu.make_async_remote_copy(
            src_ref=half.at[d], dst_ref=m_recv.at[k - 1], send_sem=send.at[2], recv_sem=recv.at[2],
            device_id={"col": d * 2 + core}, device_id_type=MESH,
        ).start()
        return carry

    lax.fori_loop(1, CHIPS, to_chip, 0)

    wait_bytes(gb_recv, recv.at[0])
    gb_col[me_c] = gb_part[me_c] + jnp.sum(gb_recv[...], axis=0)
    gather("col", NCOL, gb_col.at[me_c], send.at[3], recv.at[3])

    wait_bytes(m_recv, recv.at[2])
    m16 = part[core, chip] + pair_recv[chip] + jnp.sum(m_recv[...].astype(F32), axis=0)
    ms[core, chip] = m16.astype(BF16)

    def from_chip(k, carry):
        piece = ms.at[core, chip]
        pltpu.make_async_remote_copy(
            src_ref=piece, dst_ref=piece, send_sem=send.at[4], recv_sem=recv.at[4],
            device_id={"col": lax.rem(chip + k, CHIPS) * 2 + core}, device_id_type=MESH,
        ).start()
        return carry

    lax.fori_loop(1, CHIPS, from_chip, 0)
    m16_out[...] = m16

    wait_bytes(gb_col.at[pl.ds(0, NCOL - 1)], recv.at[3])
    for i in range(32):
        gb_full[me_r, i:i + 1, :] = gb_col[i]
    gather("row", NROW, gb_full.at[me_r], send.at[5], recv.at[5])

    wait_bytes(m_recv, recv.at[4])
    to_mate(ms.at[core], ms.at[core], 6)
    wait_bytes(ms.at[0], recv.at[6])

    slab = ms[...].reshape(SLAB_A, R)
    gram[...] = jnp.dot(slab.T, slab, preferred_element_type=F32)
    g_piece[...] = gram[pl.ds(pl.multiple_of(core * BLK, BLK), BLK), :].reshape(NROW, SHARE_G, R)
    scatter("row", NROW, g_piece, g_recv, send.at[7], recv.at[7])
    for at in range(NCOL):
        ms_out[at * SHARE_A:(at + 1) * SHARE_A, :] = ms[at % 2, at // 2]
    wait_bytes(g_recv, recv.at[7])
    g_full[core, me_r] = g_piece[me_r] + jnp.sum(g_recv[...], axis=0)
    gather("row", NROW, g_full.at[core, me_r], send.at[8], recv.at[8])
    wait_bytes(gb_full.at[pl.ds(0, NROW - 1)], recv.at[5])
    gb_out[...] = gb_full[...].reshape(R, R)
    wait_bytes(g_recv, recv.at[8])
    to_mate(g_full.at[core], g_full.at[core], 9)
    wait_bytes(g_full.at[0], recv.at[9])
    g_out[...] = g_full[...].reshape(R, R)

    wait_bytes(gb_recv, send.at[0])
    wait_bytes(pair_recv, send.at[1])
    wait_bytes(m_recv, send.at[2])
    wait_bytes(gb_col.at[pl.ds(0, NCOL - 1)], send.at[3])
    wait_bytes(m_recv, send.at[4])
    wait_bytes(gb_full.at[pl.ds(0, NROW - 1)], send.at[5])
    wait_bytes(ms.at[0], send.at[6])
    wait_bytes(g_recv, send.at[7])
    wait_bytes(g_recv, send.at[8])
    wait_bytes(g_full.at[0], send.at[9])


def eye():
    return lax.broadcasted_iota(jnp.int32, (R, R), 0) == lax.broadcasted_iota(jnp.int32, (R, R), 1)


def diagonals(v):
    only = jnp.where(eye(), v, 0.0)
    return jnp.sum(only, axis=1, keepdims=True), jnp.sum(only, axis=0, keepdims=True)


def inverse(v, x_ref, r_ref, c_ref):
    down, across = diagonals(v)
    down, across = 1.0 / jnp.sqrt(down), 1.0 / jnp.sqrt(across)
    unit = jnp.where(eye(), 1.0, 0.0)
    c = v * down * across
    c_ref[...] = c
    norm = jnp.max(jnp.sum(jnp.abs(c), axis=1, keepdims=True))
    alpha = jnp.where(norm < 1.9, 1.0, 1.0 / norm)
    res = unit - alpha * c
    x_ref[...] = alpha * (unit + res)
    res = unit - dot_hi(c, x_ref[...])
    r_ref[...] = res

    def more(state):
        it, size, before = state
        return (it < MAX_IT) & (size > 1e-5) & ((size > 1e-3) | (size < 0.5 * before))

    def step(state):
        it, size, _ = state
        x = x_ref[...]
        x = x + dot_hi(x, r_ref[...])
        x_ref[...] = x
        res = unit - dot_hi(c_ref[...], x)
        r_ref[...] = res
        return it + 1, jnp.max(jnp.abs(res)), size

    lax.while_loop(more, step, (0, jnp.max(jnp.abs(res)), jnp.float32(1e30)))
    x = x_ref[...]
    x = x + dot_hi(x, r_ref[...])
    return x * down * across


def kernel_b(
    pos, cnt, c_ref, gb_ref, m16_ref, ms_ref, g_ref,
    a_out, lhs_out, inv_out,
    x1, r1, c1, slab,
):
    c = c_ref[...]
    gram_c = dot_hi(c.T, c)
    inv1 = inverse(gb_ref[...] * gram_c, x1, r1, c1)
    gram_a = dot_hi(dot_hi(inv1, g_ref[...]), inv1)
    down, across = diagonals(gram_a)
    down = 1.0 / jnp.sqrt(down / ROWS_A + EPS)
    across = 1.0 / jnp.sqrt(across / ROWS_A + EPS)
    a_out[...] = dot_hi(m16_ref[...], inv1) * across
    slab[...] = dot_hi(ms_ref[...].astype(F32), inv1) * across

    inv_out[...] = inverse(gram_a * down * across * gram_c, x1, r1, c1)

    count = cnt[0, 0]
    for s in range(SLOTS):
        p = pos[0, s]
        tile = slab[pl.ds(pl.multiple_of(lax.shift_right_logical(p, 1) * BLK, BLK), BLK), :].T
        for jb in range(JBD):
            keep = jnp.where((count > s) & ((p & 1) == jb), 1.0, 0.0)
            lhs_out[jb * R:(jb + 1) * R, s * BLK:(s + 1) * BLK] = (tile * keep).astype(BF16)


def kernel_c(
    x_hbm, c_ref, lhs, inv_ref,
    b_out,
    x_v, x_sem, ct, acc, pb, pb_recv, sq_piece, sq_row, sq_all, sq_col, send, recv,
):
    me_r = lax.axis_index("row")

    def x_copy(ch):
        cols = pl.ds(pl.multiple_of(ch * CHUNK, CHUNK), CHUNK)
        return pltpu.make_async_copy(x_hbm.at[:, cols], x_v.at[:, cols], x_sem.at[ch])

    for ch in range(NCH):
        x_copy(ch).start()
    barrier, partners = greet((("row", NROW), ("col", NCOL)))
    c_low = c_ref[...].astype(BF16).astype(F32).T
    for jb in range(JBD):
        for t in range(CHUNK // K):
            ct[jb * R:(jb + 1) * R, t * K:(t + 1) * K] = c_low
    acc[...] = jnp.zeros_like(acc)

    def mode_two(ch, carry):
        x_copy(ch).wait()
        x = x_v[:, pl.ds(pl.multiple_of(ch * CHUNK, CHUNK), CHUNK)]
        t = jnp.dot(lhs[...], x, preferred_element_type=F32)
        t = (t * ct[...]).astype(BF16)
        j = lax.shift_right_logical(lax.broadcasted_iota(jnp.int32, (CHUNK, BLK), 0), 6) + ch * JPC
        ones = jnp.where(j == lax.broadcasted_iota(jnp.int32, (CHUNK, BLK), 1), 1.0, 0.0).astype(BF16)
        acc[...] += jnp.dot(t, ones, preferred_element_type=F32)
        return carry

    lax.fori_loop(0, NCH, mode_two, 0)
    for jb in range(JBD):
        rows = acc[jb * R:(jb + 1) * R, :].T.astype(BF16)
        for t in range(BLK // SHARE_B):
            pb[jb * (BLK // SHARE_B) + t] = rows[t * SHARE_B:(t + 1) * SHARE_B, :]

    pl.semaphore_wait(barrier, partners)
    scatter("row", NROW, pb, pb_recv, send.at[0], recv.at[0])
    wait_bytes(pb_recv, recv.at[0])
    m2 = pb[me_r].astype(F32) + jnp.sum(pb_recv[...].astype(F32), axis=0)
    raw = dot_hi(m2, inv_ref[...])
    sq_piece[...] = jnp.sum(raw * raw, axis=0, keepdims=True)
    spread("row", NROW, sq_piece, sq_row, send.at[1], recv.at[1])
    wait_bytes(sq_row, recv.at[1])
    sq_all[...] = sq_piece[...] + jnp.sum(sq_row[...], axis=0)
    spread("col", NCOL, sq_all, sq_col, send.at[2], recv.at[2])
    wait_bytes(sq_col, recv.at[2])
    squares = sq_all[...] + jnp.sum(sq_col[...], axis=0)
    b_out[...] = raw / jnp.sqrt(squares / ROWS_B + EPS)
    wait_bytes(pb_recv, send.at[0])
    wait_bytes(sq_row, send.at[1])
    wait_bytes(sq_col, send.at[2])


def low_dot(a, b):
    return jnp.dot(a.astype(BF16), b.astype(BF16), preferred_element_type=F32)


def short_inverse(v):
    down, across = diagonals(v)
    down, across = 1.0 / jnp.sqrt(down), 1.0 / jnp.sqrt(across)
    unit = jnp.where(eye(), 1.0, 0.0)
    c = v * down * across
    norm = jnp.max(jnp.sum(jnp.abs(c), axis=0, keepdims=True), axis=1, keepdims=True)
    alpha = jnp.where(norm < 1.9, 1.0, 1.0 / norm)
    res = unit - alpha * c
    x = alpha * (unit + res)
    x = x + low_dot(x, low_dot(res, res))
    x = x + low_dot(x, unit - dot_hi(c, x))
    res = unit - dot_hi(c, x)
    worst = jnp.max(jnp.sum(jnp.abs(res), axis=0, keepdims=True), axis=1, keepdims=True)
    x = x + low_dot(x, res)
    return x * down * across, worst


def kernel_m(
    pos, cnt, x_hbm, b_ref, c_ref,
    a_out, b_out, worst_out,
    x_v, x_sem, br, w_v, acc,
    gram, gb_part, gb_recv, gb_col, gb_full,
    part, pair_recv, half, m_recv, ms, m16, g_piece, g_recv, g_full,
    gram_c, inv1, slab, turned, lhs, ct, acc2,
    pb, pb_recv, sq_piece, sq_row, sq_all, sq_col,
    send, recv,
):
    me_r, me_c = lax.axis_index("row"), lax.axis_index("col")
    chip, core = me_c // 2, lax.rem(me_c, 2)
    mate = chip * 2 + 1 - core

    def to_mate(src, dst, n):
        pltpu.make_async_remote_copy(
            src_ref=src, dst_ref=dst, send_sem=send.at[n], recv_sem=recv.at[n],
            device_id={"col": mate}, device_id_type=MESH,
        ).start()

    def chunk(ch):
        return pl.ds(pl.multiple_of(ch * CHUNK, CHUNK), CHUNK)

    def x_copy(ch):
        return pltpu.make_async_copy(x_hbm.at[:, chunk(ch)], x_v.at[:, chunk(ch)], x_sem.at[ch])

    for ch in range(NCH):
        x_copy(ch).start()
    barrier, partners = greet((("col", NCOL), ("row", NROW)))

    b = b_ref[...]
    gram[...] = dot_hi(b.T, b)
    rows = gram[pl.ds(pl.multiple_of(me_r * 32, 32), 32), :]
    for i in range(32):
        gb_part[i] = rows[i:i + 1, :]
    br[...] = b.astype(BF16).astype(F32)
    cr = c_ref[...].astype(BF16).astype(F32)
    acc[...] = jnp.zeros_like(acc)

    def mode_one(ch, carry):
        for jb in range(JBD):
            tile = br[pl.ds(pl.multiple_of(jb * BLK + ch * JPC, JPC), JPC), :]
            for j in range(JPC):
                w_v[j * K:(j + 1) * K, jb * R:(jb + 1) * R] = (tile[j:j + 1, :] * cr).astype(BF16)
        x_copy(ch).wait()
        acc[...] += jnp.dot(x_v[:, chunk(ch)], w_v[...], preferred_element_type=F32)
        return carry

    lax.fori_loop(0, NCH - 3, mode_one, 0)
    pl.semaphore_wait(barrier, partners)
    scatter("col", NCOL, gb_part, gb_recv, send.at[0], recv.at[0])
    lax.fori_loop(NCH - 3, NCH, mode_one, 0)

    count = cnt[0, 0]
    for ib in range(IBD):
        total = jnp.zeros((BLK, R), F32)
        for s in range(SLOTS):
            p = pos[0, s]
            live = jnp.where(count > s, 1.0, 0.0).astype(F32)
            for jb in range(JBD):
                keep = jnp.where(p == ib * JBD + jb, live, 0.0)
                total += acc[s * BLK:(s + 1) * BLK, jb * R:(jb + 1) * R] * keep
        for t in range(BLK // SHARE_A):
            at = ib * (BLK // SHARE_A) + t
            part[at % 2, at // 2] = total[t * SHARE_A:(t + 1) * SHARE_A, :]

    to_mate(part.at[1 - core], pair_recv, 1)
    c = c_ref[...]
    gram_c[...] = dot_hi(c.T, c)
    wait_bytes(pair_recv, recv.at[1])
    half[...] = (part[core] + pair_recv[...]).astype(BF16)

    def to_chip(k, carry):
        d = lax.rem(chip + k, CHIPS)
        pltpu.make_async_remote_copy(
            src_ref=half.at[d], dst_ref=m_recv.at[k - 1], send_sem=send.at[2], recv_sem=recv.at[2],
            device_id={"col": d * 2 + core}, device_id_type=MESH,
        ).start()
        return carry

    lax.fori_loop(1, CHIPS, to_chip, 0)

    wait_bytes(gb_recv, recv.at[0])
    gb_col[me_c] = gb_part[me_c] + jnp.sum(gb_recv[...], axis=0)
    gather("col", NCOL, gb_col.at[me_c], send.at[3], recv.at[3])
    c_low = cr.T
    for jb in range(JBD):
        for t in range(CHUNK // K):
            ct[jb * R:(jb + 1) * R, t * K:(t + 1) * K] = c_low
    acc2[...] = jnp.zeros_like(acc2)
    wait_bytes(gb_col.at[pl.ds(0, NCOL - 1)], recv.at[3])
    for i in range(32):
        gb_full[me_r, i:i + 1, :] = gb_col[i]
    gather("row", NROW, gb_full.at[me_r], send.at[5], recv.at[5])

    wait_bytes(m_recv, recv.at[2])
    mine = part[core, chip] + pair_recv[chip] + jnp.sum(m_recv[...].astype(F32), axis=0)
    ms[core, chip] = mine.astype(BF16)

    def from_chip(k, carry):
        piece = ms.at[core, chip]
        pltpu.make_async_remote_copy(
            src_ref=piece, dst_ref=piece, send_sem=send.at[4], recv_sem=recv.at[4],
            device_id={"col": lax.rem(chip + k, CHIPS) * 2 + core}, device_id_type=MESH,
        ).start()
        return carry

    lax.fori_loop(1, CHIPS, from_chip, 0)

    wait_bytes(gb_full.at[pl.ds(0, NROW - 1)], recv.at[5])
    solved, worst_one = short_inverse(gb_full[...].reshape(R, R) * gram_c[...])
    inv1[...] = solved
    m16[...] = dot_hi(mine, solved)

    wait_bytes(m_recv, recv.at[4])
    to_mate(ms.at[core], ms.at[core], 6)
    wait_bytes(ms.at[0], recv.at[6])
    for at in range(NCOL):
        slab[at * SHARE_A:(at + 1) * SHARE_A, :] = ms[at % 2, at // 2]

    gram[...] = jnp.dot(slab[...].T, slab[...], preferred_element_type=F32)
    g_piece[...] = gram[pl.ds(pl.multiple_of(core * BLK, BLK), BLK), :].reshape(NROW, SHARE_G, R)
    scatter("row", NROW, g_piece, g_recv, send.at[7], recv.at[7])

    top = inv1[...].astype(BF16)
    rest = (inv1[...] - top.astype(F32)).astype(BF16)
    last = (((1,), (1,)), ((), ()))
    turned[...] = lax.dot_general(top, slab[...], last, preferred_element_type=F32) + lax.dot_general(
        rest, slab[...], last, preferred_element_type=F32
    )
    for s in range(SLOTS):
        p = pos[0, s]
        live = jnp.where(count > s, 1.0, 0.0).astype(F32)
        for jb in range(JBD):
            tile = jnp.zeros((R, BLK), F32)
            for ib in range(IBD):
                tile += turned[:, ib * BLK:(ib + 1) * BLK] * jnp.where(p == ib * JBD + jb, live, 0.0)
            lhs[jb * R:(jb + 1) * R, s * BLK:(s + 1) * BLK] = tile.astype(BF16)

    def mode_two(ch, carry):
        t = jnp.dot(lhs[...], x_v[:, chunk(ch)], preferred_element_type=F32)
        t = (t * ct[...]).astype(BF16)
        j = lax.shift_right_logical(lax.broadcasted_iota(jnp.int32, (CHUNK, BLK), 0), 6) + ch * JPC
        ones = jnp.where(j == lax.broadcasted_iota(jnp.int32, (CHUNK, BLK), 1), 1.0, 0.0).astype(BF16)
        acc2[...] += jnp.dot(t, ones, preferred_element_type=F32)
        return carry

    lax.fori_loop(0, NCH - 4, mode_two, 0)
    wait_bytes(g_recv, recv.at[7])
    g_full[core, me_r] = g_piece[me_r] + jnp.sum(g_recv[...], axis=0)
    gather("row", NROW, g_full.at[core, me_r], send.at[8], recv.at[8])
    lax.fori_loop(NCH - 4, NCH, mode_two, 0)
    for jb in range(JBD):
        rows = acc2[jb * R:(jb + 1) * R, :].T.astype(BF16)
        for t in range(BLK // SHARE_B):
            pb[jb * (BLK // SHARE_B) + t] = rows[t * SHARE_B:(t + 1) * SHARE_B, :]
    wait_bytes(g_recv, recv.at[8])
    to_mate(g_full.at[core], g_full.at[core], 9)
    scatter("row", NROW, pb, pb_recv, send.at[10], recv.at[10])

    wait_bytes(g_full.at[0], recv.at[9])
    solved = inv1[...]
    gram_a = dot_hi(dot_hi(solved, g_full[...].reshape(R, R)), solved)
    down, across = diagonals(gram_a)
    down = 1.0 / jnp.sqrt(down / ROWS_A + EPS)
    across = 1.0 / jnp.sqrt(across / ROWS_A + EPS)
    a_out[...] = m16[...] * across
    inv2, worst_two = short_inverse(gram_a * down * across * gram_c[...])
    worst_out[...] = jnp.full((8, 128), 1.0, F32) * jnp.maximum(worst_one, worst_two)

    wait_bytes(pb_recv, recv.at[10])
    m2 = (pb[me_r].astype(F32) + jnp.sum(pb_recv[...].astype(F32), axis=0)) * across
    raw = dot_hi(m2, inv2)
    sq_piece[...] = jnp.sum(raw * raw, axis=0, keepdims=True)
    spread("row", NROW, sq_piece, sq_row, send.at[11], recv.at[11])
    wait_bytes(sq_row, recv.at[11])
    sq_all[...] = sq_piece[...] + jnp.sum(sq_row[...], axis=0)
    spread("col", NCOL, sq_all, sq_col, send.at[12], recv.at[12])
    wait_bytes(gb_recv, send.at[0])
    wait_bytes(pair_recv, send.at[1])
    wait_bytes(m_recv, send.at[2])
    wait_bytes(gb_col.at[pl.ds(0, NCOL - 1)], send.at[3])
    wait_bytes(m_recv, send.at[4])
    wait_bytes(gb_full.at[pl.ds(0, NROW - 1)], send.at[5])
    wait_bytes(ms.at[0], send.at[6])
    wait_bytes(g_recv, send.at[7])
    wait_bytes(g_recv, send.at[8])
    wait_bytes(g_full.at[0], send.at[9])
    wait_bytes(pb_recv, send.at[10])
    wait_bytes(sq_row, send.at[11])
    wait_bytes(sq_col, recv.at[12])
    squares = sq_all[...] + jnp.sum(sq_col[...], axis=0)
    b_out[...] = raw / jnp.sqrt(squares / ROWS_B + EPS)
    wait_bytes(sq_col, send.at[12])


VM = pl.BlockSpec(memory_space=pltpu.VMEM)
SM = pl.BlockSpec(memory_space=pltpu.SMEM)
ANY = pl.BlockSpec(memory_space=pl.ANY)


def shape(dims, kind=F32):
    return jax.ShapeDtypeStruct(dims, kind)


def three_kernels(place, block_count, flat, factor_b, factor_c):
    vm, dma = pltpu.VMEM, pltpu.SemaphoreType.DMA
    gram_b, m16, ms, g = pl.pallas_call(
        kernel_a,
        name="mode_one",
        out_shape=(shape((R, R)), shape((SHARE_A, R)), shape((SLAB_A, R), BF16), shape((R, R))),
        in_specs=[SM, SM, ANY, VM, VM],
        out_specs=[VM] * 4,
        scratch_shapes=[
            vm((SLAB_A, WIDE), BF16), dma((NCH,)), vm((R, R), F32), vm((CHUNK, JBD * R), BF16), vm((SLAB_A, JBD * R), F32),
            vm((R, R), F32), vm((NCOL, 1, R), F32), vm((NCOL - 1, 1, R), F32), vm((NCOL, 1, R), F32), vm((NROW, 32, R), F32),
            vm((2, CHIPS, SHARE_A, R), F32), vm((CHIPS, SHARE_A, R), F32), vm((CHIPS, SHARE_A, R), BF16),
            vm((CHIPS - 1, SHARE_A, R), BF16), vm((2, CHIPS, SHARE_A, R), BF16),
            vm((NROW, SHARE_G, R), F32), vm((NROW - 1, SHARE_G, R), F32), vm((2, NROW, SHARE_G, R), F32),
            dma((10,)), dma((10,)),
        ],
        compiler_params=pltpu.CompilerParams(collective_id=1, has_side_effects=True),
    )(place, block_count, flat, factor_b, factor_c)
    hat_a, lhs, inv = pl.pallas_call(
        kernel_b,
        name="solve_two",
        out_shape=(shape((SHARE_A, R)), shape((JBD * R, SLAB_A), BF16), shape((R, R))),
        in_specs=[SM, SM, VM, VM, VM, VM, VM],
        out_specs=[VM] * 3,
        scratch_shapes=[vm((R, R), F32), vm((R, R), F32), vm((R, R), F32), vm((SLAB_A, R), F32)],
    )(place, block_count, factor_c, gram_b, m16, ms, g)
    hat_b = pl.pallas_call(
        kernel_c,
        name="mode_two",
        out_shape=shape((SHARE_B, R)),
        in_specs=[ANY, VM, VM, VM],
        out_specs=VM,
        scratch_shapes=[
            vm((SLAB_A, WIDE), BF16), dma((NCH,)), vm((JBD * R, CHUNK), F32), vm((JBD * R, BLK), F32),
            vm((NROW, SHARE_B, R), BF16), vm((NROW - 1, SHARE_B, R), BF16),
            vm((1, R), F32), vm((NROW - 1, 1, R), F32), vm((1, R), F32), vm((NCOL - 1, 1, R), F32),
            dma((3,)), dma((3,)),
        ],
        compiler_params=pltpu.CompilerParams(collective_id=2, has_side_effects=True),
    )(flat, factor_c, lhs, inv)
    return hat_a, hat_b


def body(blocks, factor_b, factor_c, block_pos, block_count):
    args = (block_pos.T, block_count, blocks.reshape(SLOTS * BLK, WIDE), factor_b, factor_c)
    vm, dma = pltpu.VMEM, pltpu.SemaphoreType.DMA
    hat_a, hat_b, worst = pl.pallas_call(
        kernel_m,
        name="sweep",
        out_shape=(shape((SHARE_A, R)), shape((SHARE_B, R)), shape((8, 128))),
        in_specs=[SM, SM, ANY, VM, VM],
        out_specs=[VM] * 3,
        scratch_shapes=[
            vm((SLAB_A, WIDE), BF16), dma((NCH,)), vm((R, R), F32), vm((CHUNK, JBD * R), BF16), vm((SLAB_A, JBD * R), F32),
            vm((R, R), F32), vm((NCOL, 1, R), F32), vm((NCOL - 1, 1, R), F32), vm((NCOL, 1, R), F32), vm((NROW, 32, R), F32),
            vm((2, CHIPS, SHARE_A, R), F32), vm((CHIPS, SHARE_A, R), F32), vm((CHIPS, SHARE_A, R), BF16),
            vm((CHIPS - 1, SHARE_A, R), BF16), vm((2, CHIPS, SHARE_A, R), BF16), vm((SHARE_A, R), F32),
            vm((NROW, SHARE_G, R), F32), vm((NROW - 1, SHARE_G, R), F32), vm((2, NROW, SHARE_G, R), F32),
            vm((R, R), F32), vm((R, R), F32), vm((SLAB_A, R), BF16), vm((R, SLAB_A), F32), vm((JBD * R, SLAB_A), BF16),
            vm((JBD * R, CHUNK), F32), vm((JBD * R, BLK), F32),
            vm((NROW, SHARE_B, R), BF16), vm((NROW - 1, SHARE_B, R), BF16),
            vm((1, R), F32), vm((NROW - 1, 1, R), F32), vm((1, R), F32), vm((NCOL - 1, 1, R), F32),
            dma((13,)), dma((13,)),
        ],
        compiler_params=pltpu.CompilerParams(collective_id=0, has_side_effects=True),
    )(*args)
    return lax.cond(worst[0, 0] <= 1e-3, lambda: (hat_a, hat_b), lambda: three_kernels(*args))


def solution(mesh):
    return jax.shard_map(
        body,
        mesh=mesh,
        in_specs=(P("row", "col", None), P("col", None), P(), P("row", "col"), P("row", "col")),
        out_specs=(P(("row", "col"), None), P(("col", "row"), None)),
        check_vma=False,
    )
```

```python
import functools

import jax
import jax.numpy as jnp
from jax import lax
from jax.experimental import pallas as pl
from jax.experimental.pallas import tpu as pltpu
from jax.sharding import PartitionSpec as P

MESH = pl.DeviceIdType.MESH
HIGH = lax.Precision.HIGHEST
F32 = jnp.float32
BF16 = jnp.bfloat16
NROW, NCOL = 8, 32
R, K, BLK, SLOTS, IBD, JBD = 256, 64, 128, 4, 4, 2
SLAB_A = IBD * BLK
SLAB_B = JBD * BLK
WIDE = BLK * K
CHUNK = 1024
NCH = WIDE // CHUNK
JPC = CHUNK // K
SHARE_A = SLAB_A // NCOL
SHARE_B = SLAB_B // NROW
CHIPS = NCOL // 2
SHARE_G = BLK // NROW
ROWS_A = SLAB_A * NROW
ROWS_B = SLAB_B * NCOL
EPS = 1e-06
MAX_IT = 80


def dot_hi(a, b):
    return jnp.dot(a, b, precision=HIGH, preferred_element_type=F32)


def wait_bytes(ref, sem):
    pltpu.make_async_copy(ref, ref, sem).wait()


def greet(axes):
    barrier = pltpu.get_barrier_semaphore()
    total = 0
    for axis, count in axes:
        me = lax.axis_index(axis)

        def one(k, carry, axis=axis, count=count, me=me):
            pl.semaphore_signal(
                barrier, inc=1, device_id={axis: lax.rem(me + k, count)}, device_id_type=MESH
            )
            return carry

        lax.fori_loop(1, count, one, 0)
        total += count - 1
    return barrier, total


def scatter(axis, count, src, dst, send, recv):
    me = lax.axis_index(axis)

    def one(k, carry):
        d = lax.rem(me + k, count)
        pltpu.make_async_remote_copy(
            src_ref=src.at[d], dst_ref=dst.at[k - 1], send_sem=send, recv_sem=recv,
            device_id={axis: d}, device_id_type=MESH,
        ).start()
        return carry

    lax.fori_loop(1, count, one, 0)


def gather(axis, count, piece, send, recv):
    me = lax.axis_index(axis)

    def one(k, carry):
        pltpu.make_async_remote_copy(
            src_ref=piece, dst_ref=piece, send_sem=send, recv_sem=recv,
            device_id={axis: lax.rem(me + k, count)}, device_id_type=MESH,
        ).start()
        return carry

    lax.fori_loop(1, count, one, 0)


def spread(axis, count, src, dst, send, recv):
    me = lax.axis_index(axis)

    def one(k, carry):
        pltpu.make_async_remote_copy(
            src_ref=src, dst_ref=dst.at[k - 1], send_sem=send, recv_sem=recv,
            device_id={axis: lax.rem(me + k, count)}, device_id_type=MESH,
        ).start()
        return carry

    lax.fori_loop(1, count, one, 0)


def kernel_a(
    pos, cnt, x_hbm, b_ref, c_ref,
    gb_out, m16_out, ms_out, g_out,
    x_v, x_sem, br, w_v, acc,
    gram, gb_part, gb_recv, gb_col, gb_full,
    part, pair_recv, half, m_recv, ms, g_piece, g_recv, g_full,
    send, recv,
):
    me_r, me_c = lax.axis_index("row"), lax.axis_index("col")
    chip, core = me_c // 2, lax.rem(me_c, 2)
    mate = chip * 2 + 1 - core

    def to_mate(src, dst, n):
        pltpu.make_async_remote_copy(
            src_ref=src, dst_ref=dst, send_sem=send.at[n], recv_sem=recv.at[n],
            device_id={"col": mate}, device_id_type=MESH,
        ).start()

    def x_copy(ch):
        cols = pl.ds(pl.multiple_of(ch * CHUNK, CHUNK), CHUNK)
        return pltpu.make_async_copy(x_hbm.at[:, cols], x_v.at[:, cols], x_sem.at[ch])

    for ch in range(NCH):
        x_copy(ch).start()
    barrier, partners = greet((("col", NCOL), ("row", NROW)))

    b = b_ref[...]
    gram[...] = dot_hi(b.T, b)
    rows = gram[pl.ds(pl.multiple_of(me_r * 32, 32), 32), :]
    for i in range(32):
        gb_part[i] = rows[i:i + 1, :]
    br[...] = b.astype(BF16).astype(F32)
    cr = c_ref[...].astype(BF16).astype(F32)
    acc[...] = jnp.zeros_like(acc)

    def mode_one(ch, carry):
        for jb in range(JBD):
            tile = br[pl.ds(pl.multiple_of(jb * BLK + ch * JPC, JPC), JPC), :]
            for j in range(JPC):
                w_v[j * K:(j + 1) * K, jb * R:(jb + 1) * R] = (tile[j:j + 1, :] * cr).astype(BF16)
        x_copy(ch).wait()
        x = x_v[:, pl.ds(pl.multiple_of(ch * CHUNK, CHUNK), CHUNK)]
        acc[...] += jnp.dot(x, w_v[...], preferred_element_type=F32)
        return carry

    lax.fori_loop(0, NCH - 3, mode_one, 0)
    pl.semaphore_wait(barrier, partners)
    scatter("col", NCOL, gb_part, gb_recv, send.at[0], recv.at[0])
    lax.fori_loop(NCH - 3, NCH, mode_one, 0)

    count = cnt[0, 0]
    for ib in range(IBD):
        total = jnp.zeros((BLK, R), F32)
        for s in range(SLOTS):
            p = pos[0, s]
            live = jnp.where(count > s, 1.0, 0.0).astype(F32)
            for jb in range(JBD):
                keep = jnp.where(p == ib * JBD + jb, live, 0.0)
                total += acc[s * BLK:(s + 1) * BLK, jb * R:(jb + 1) * R] * keep
        for t in range(BLK // SHARE_A):
            at = ib * (BLK // SHARE_A) + t
            part[at % 2, at // 2] = total[t * SHARE_A:(t + 1) * SHARE_A, :]

    to_mate(part.at[1 - core], pair_recv, 1)
    wait_bytes(pair_recv, recv.at[1])
    half[...] = (part[core] + pair_recv[...]).astype(BF16)

    def to_chip(k, carry):
        d = lax.rem(chip + k, CHIPS)
        pltpu.make_async_remote_copy(
            src_ref=half.at[d], dst_ref=m_recv.at[k - 1], send_sem=send.at[2], recv_sem=recv.at[2],
            device_id={"col": d * 2 + core}, device_id_type=MESH,
        ).start()
        return carry

    lax.fori_loop(1, CHIPS, to_chip, 0)

    wait_bytes(gb_recv, recv.at[0])
    gb_col[me_c] = gb_part[me_c] + jnp.sum(gb_recv[...], axis=0)
    gather("col", NCOL, gb_col.at[me_c], send.at[3], recv.at[3])

    wait_bytes(m_recv, recv.at[2])
    m16 = part[core, chip] + pair_recv[chip] + jnp.sum(m_recv[...].astype(F32), axis=0)
    ms[core, chip] = m16.astype(BF16)

    def from_chip(k, carry):
        piece = ms.at[core, chip]
        pltpu.make_async_remote_copy(
            src_ref=piece, dst_ref=piece, send_sem=send.at[4], recv_sem=recv.at[4],
            device_id={"col": lax.rem(chip + k, CHIPS) * 2 + core}, device_id_type=MESH,
        ).start()
        return carry

    lax.fori_loop(1, CHIPS, from_chip, 0)
    m16_out[...] = m16

    wait_bytes(gb_col.at[pl.ds(0, NCOL - 1)], recv.at[3])
    for i in range(32):
        gb_full[me_r, i:i + 1, :] = gb_col[i]
    gather("row", NROW, gb_full.at[me_r], send.at[5], recv.at[5])

    wait_bytes(m_recv, recv.at[4])
    to_mate(ms.at[core], ms.at[core], 6)
    wait_bytes(ms.at[0], recv.at[6])

    slab = ms[...].reshape(SLAB_A, R)
    gram[...] = jnp.dot(slab.T, slab, preferred_element_type=F32)
    g_piece[...] = gram[pl.ds(pl.multiple_of(core * BLK, BLK), BLK), :].reshape(NROW, SHARE_G, R)
    scatter("row", NROW, g_piece, g_recv, send.at[7], recv.at[7])
    for at in range(NCOL):
        ms_out[at * SHARE_A:(at + 1) * SHARE_A, :] = ms[at % 2, at // 2]
    wait_bytes(g_recv, recv.at[7])
    g_full[core, me_r] = g_piece[me_r] + jnp.sum(g_recv[...], axis=0)
    gather("row", NROW, g_full.at[core, me_r], send.at[8], recv.at[8])
    wait_bytes(gb_full.at[pl.ds(0, NROW - 1)], recv.at[5])
    gb_out[...] = gb_full[...].reshape(R, R)
    wait_bytes(g_recv, recv.at[8])
    to_mate(g_full.at[core], g_full.at[core], 9)
    wait_bytes(g_full.at[0], recv.at[9])
    g_out[...] = g_full[...].reshape(R, R)

    wait_bytes(gb_recv, send.at[0])
    wait_bytes(pair_recv, send.at[1])
    wait_bytes(m_recv, send.at[2])
    wait_bytes(gb_col.at[pl.ds(0, NCOL - 1)], send.at[3])
    wait_bytes(m_recv, send.at[4])
    wait_bytes(gb_full.at[pl.ds(0, NROW - 1)], send.at[5])
    wait_bytes(ms.at[0], send.at[6])
    wait_bytes(g_recv, send.at[7])
    wait_bytes(g_recv, send.at[8])
    wait_bytes(g_full.at[0], send.at[9])


def eye():
    return lax.broadcasted_iota(jnp.int32, (R, R), 0) == lax.broadcasted_iota(jnp.int32, (R, R), 1)


def diagonals(v):
    only = jnp.where(eye(), v, 0.0)
    return jnp.sum(only, axis=1, keepdims=True), jnp.sum(only, axis=0, keepdims=True)


def inverse(v, x_ref, r_ref, c_ref):
    down, across = diagonals(v)
    down, across = 1.0 / jnp.sqrt(down), 1.0 / jnp.sqrt(across)
    unit = jnp.where(eye(), 1.0, 0.0)
    c = v * down * across
    c_ref[...] = c
    norm = jnp.max(jnp.sum(jnp.abs(c), axis=1, keepdims=True))
    alpha = jnp.where(norm < 1.9, 1.0, 1.0 / norm)
    res = unit - alpha * c
    x_ref[...] = alpha * (unit + res)
    res = unit - dot_hi(c, x_ref[...])
    r_ref[...] = res

    def more(state):
        it, size, before = state
        return (it < MAX_IT) & (size > 1e-5) & ((size > 1e-3) | (size < 0.5 * before))

    def step(state):
        it, size, _ = state
        x = x_ref[...]
        x = x + dot_hi(x, r_ref[...])
        x_ref[...] = x
        res = unit - dot_hi(c_ref[...], x)
        r_ref[...] = res
        return it + 1, jnp.max(jnp.abs(res)), size

    lax.while_loop(more, step, (0, jnp.max(jnp.abs(res)), jnp.float32(1e30)))
    x = x_ref[...]
    x = x + dot_hi(x, r_ref[...])
    return x * down * across


def kernel_b(
    pos, cnt, c_ref, gb_ref, m16_ref, ms_ref, g_ref,
    a_out, lhs_out, inv_out,
    x1, r1, c1, slab,
):
    c = c_ref[...]
    gram_c = dot_hi(c.T, c)
    inv1 = inverse(gb_ref[...] * gram_c, x1, r1, c1)
    gram_a = dot_hi(dot_hi(inv1, g_ref[...]), inv1)
    down, across = diagonals(gram_a)
    down = 1.0 / jnp.sqrt(down / ROWS_A + EPS)
    across = 1.0 / jnp.sqrt(across / ROWS_A + EPS)
    a_out[...] = dot_hi(m16_ref[...], inv1) * across
    slab[...] = dot_hi(ms_ref[...].astype(F32), inv1) * across

    inv_out[...] = inverse(gram_a * down * across * gram_c, x1, r1, c1)

    count = cnt[0, 0]
    for s in range(SLOTS):
        p = pos[0, s]
        tile = slab[pl.ds(pl.multiple_of(lax.shift_right_logical(p, 1) * BLK, BLK), BLK), :].T
        for jb in range(JBD):
            keep = jnp.where((count > s) & ((p & 1) == jb), 1.0, 0.0)
            lhs_out[jb * R:(jb + 1) * R, s * BLK:(s + 1) * BLK] = (tile * keep).astype(BF16)


def kernel_c(
    x_hbm, c_ref, lhs, inv_ref,
    b_out,
    x_v, x_sem, ct, acc, pb, pb_recv, sq_piece, sq_row, sq_all, sq_col, send, recv,
):
    me_r = lax.axis_index("row")

    def x_copy(ch):
        cols = pl.ds(pl.multiple_of(ch * CHUNK, CHUNK), CHUNK)
        return pltpu.make_async_copy(x_hbm.at[:, cols], x_v.at[:, cols], x_sem.at[ch])

    for ch in range(NCH):
        x_copy(ch).start()
    barrier, partners = greet((("row", NROW), ("col", NCOL)))
    c_low = c_ref[...].astype(BF16).astype(F32).T
    for jb in range(JBD):
        for t in range(CHUNK // K):
            ct[jb * R:(jb + 1) * R, t * K:(t + 1) * K] = c_low
    acc[...] = jnp.zeros_like(acc)

    def mode_two(ch, carry):
        x_copy(ch).wait()
        x = x_v[:, pl.ds(pl.multiple_of(ch * CHUNK, CHUNK), CHUNK)]
        t = jnp.dot(lhs[...], x, preferred_element_type=F32)
        t = (t * ct[...]).astype(BF16)
        j = lax.shift_right_logical(lax.broadcasted_iota(jnp.int32, (CHUNK, BLK), 0), 6) + ch * JPC
        ones = jnp.where(j == lax.broadcasted_iota(jnp.int32, (CHUNK, BLK), 1), 1.0, 0.0).astype(BF16)
        acc[...] += jnp.dot(t, ones, preferred_element_type=F32)
        return carry

    lax.fori_loop(0, NCH, mode_two, 0)
    for jb in range(JBD):
        rows = acc[jb * R:(jb + 1) * R, :].T.astype(BF16)
        for t in range(BLK // SHARE_B):
            pb[jb * (BLK // SHARE_B) + t] = rows[t * SHARE_B:(t + 1) * SHARE_B, :]

    pl.semaphore_wait(barrier, partners)
    scatter("row", NROW, pb, pb_recv, send.at[0], recv.at[0])
    wait_bytes(pb_recv, recv.at[0])
    m2 = pb[me_r].astype(F32) + jnp.sum(pb_recv[...].astype(F32), axis=0)
    raw = dot_hi(m2, inv_ref[...])
    sq_piece[...] = jnp.sum(raw * raw, axis=0, keepdims=True)
    spread("row", NROW, sq_piece, sq_row, send.at[1], recv.at[1])
    wait_bytes(sq_row, recv.at[1])
    sq_all[...] = sq_piece[...] + jnp.sum(sq_row[...], axis=0)
    spread("col", NCOL, sq_all, sq_col, send.at[2], recv.at[2])
    wait_bytes(sq_col, recv.at[2])
    squares = sq_all[...] + jnp.sum(sq_col[...], axis=0)
    b_out[...] = raw / jnp.sqrt(squares / ROWS_B + EPS)
    wait_bytes(pb_recv, send.at[0])
    wait_bytes(sq_row, send.at[1])
    wait_bytes(sq_col, send.at[2])


def low_dot(a, b):
    return jnp.dot(a.astype(BF16), b.astype(BF16), preferred_element_type=F32)


def dot_three(a, b):
    a_top, b_top = a.astype(BF16), b.astype(BF16)
    a_rest, b_rest = (a - a_top.astype(F32)).astype(BF16), (b - b_top.astype(F32)).astype(BF16)
    cross = jnp.dot(a_top, b_rest, preferred_element_type=F32) + jnp.dot(a_rest, b_top, preferred_element_type=F32)
    return jnp.dot(a_top, b_top, preferred_element_type=F32) + cross


def short_inverse(v):
    down, across = diagonals(v)
    down, across = 1.0 / jnp.sqrt(down), 1.0 / jnp.sqrt(across)
    unit = jnp.where(eye(), 1.0, 0.0)
    c = v * down * across
    norm = jnp.max(jnp.sum(jnp.abs(c), axis=0, keepdims=True), axis=1, keepdims=True)
    alpha = jnp.where(norm < 1.9, 1.0, 1.0 / norm)
    res = unit - alpha * c
    x = alpha * (unit + res)
    x = x + low_dot(x, low_dot(res, res))
    x = x + low_dot(x, unit - dot_three(c, x))
    res = unit - dot_hi(c, x)
    worst = jnp.max(jnp.sum(jnp.abs(res), axis=0, keepdims=True), axis=1, keepdims=True)
    x = x + low_dot(x, res)
    return x * down * across, worst


def kernel_m(
    pos, cnt, x_hbm, b_ref, c_ref,
    a_out, b_out, worst_out,
    x_v, x_sem, br, w_even, w_odd, acc,
    gram, gb_part, gb_recv, gb_col, gb_full,
    part, pair_recv, half, m_recv, ms, m16, g_piece, g_recv, g_full,
    gram_c, inv1, slab, turned, lhs, ct, ones,
    pb, pb_recv, sq_piece, sq_row, sq_all, sq_col,
    send, recv,
):
    me_r, me_c = lax.axis_index("row"), lax.axis_index("col")
    chip, core = me_c // 2, lax.rem(me_c, 2)
    mate = chip * 2 + 1 - core

    def to_mate(src, dst, n):
        pltpu.make_async_remote_copy(
            src_ref=src, dst_ref=dst, send_sem=send.at[n], recv_sem=recv.at[n],
            device_id={"col": mate}, device_id_type=MESH,
        ).start()

    def chunk(ch):
        return pl.ds(pl.multiple_of(ch * CHUNK, CHUNK), CHUNK)

    def x_copy(ch):
        return pltpu.make_async_copy(x_hbm.at[:, chunk(ch)], x_v.at[:, chunk(ch)], x_sem.at[ch])

    for ch in range(NCH):
        x_copy(ch).start()
    barrier, partners = greet((("col", NCOL), ("row", NROW)))

    b = b_ref[...]
    gram[...] = dot_hi(b.T, b)
    rows = gram[pl.ds(pl.multiple_of(me_r * 32, 32), 32), :]
    for i in range(32):
        gb_part[i] = rows[i:i + 1, :]
    br[...] = b.astype(BF16).astype(F32)
    cr = c_ref[...].astype(BF16).astype(F32)
    acc[...] = jnp.zeros_like(acc)

    cb = cr.astype(BF16)

    def build(ch, w):
        for jb in range(JBD):
            tile = br[pl.ds(pl.multiple_of(jb * BLK + ch * JPC, JPC), JPC), :]
            for j in range(JPC):
                w[jb, j * K:(j + 1) * K, :] = jnp.broadcast_to(tile[j:j + 1, :].astype(BF16), (K, R)) * cb

    def add(ch, w):
        x_copy(ch).wait()
        for s in range(SLOTS):
            rows = slice(s * BLK, (s + 1) * BLK)
            acc[rows, :] += jnp.dot(x_v[rows, chunk(ch)], w[pos[0, s] & 1], preferred_element_type=F32)

    def mode_one(pair, carry):
        add(2 * pair, w_even)
        build(2 * pair + 1, w_odd)
        add(2 * pair + 1, w_odd)
        build(lax.rem(2 * pair + 2, NCH), w_even)
        return carry

    build(0, w_even)
    lax.fori_loop(0, NCH // 2 - 1, mode_one, 0)
    pl.semaphore_wait(barrier, partners)
    scatter("col", NCOL, gb_part, gb_recv, send.at[0], recv.at[0])
    lax.fori_loop(NCH // 2 - 1, NCH // 2, mode_one, 0)

    count = cnt[0, 0]
    for ib in range(IBD):
        total = jnp.zeros((BLK, R), F32)
        for s in range(SLOTS):
            live = jnp.where(count > s, 1.0, 0.0).astype(F32)
            keep = jnp.where(lax.shift_right_logical(pos[0, s], 1) == ib, live, 0.0)
            total += acc[s * BLK:(s + 1) * BLK, :] * keep
        for t in range(BLK // SHARE_A):
            at = ib * (BLK // SHARE_A) + t
            part[at % 2, at // 2] = total[t * SHARE_A:(t + 1) * SHARE_A, :]

    to_mate(part.at[1 - core], pair_recv, 1)
    c = c_ref[...]
    gram_c[...] = dot_hi(c.T, c)
    wait_bytes(pair_recv, recv.at[1])
    half[...] = (part[core] + pair_recv[...]).astype(BF16)

    def to_chip(k, carry):
        d = lax.rem(chip + k, CHIPS)
        pltpu.make_async_remote_copy(
            src_ref=half.at[d], dst_ref=m_recv.at[k - 1], send_sem=send.at[2], recv_sem=recv.at[2],
            device_id={"col": d * 2 + core}, device_id_type=MESH,
        ).start()
        return carry

    lax.fori_loop(1, CHIPS, to_chip, 0)

    wait_bytes(gb_recv, recv.at[0])
    gb_col[me_c] = gb_part[me_c] + jnp.sum(gb_recv[...], axis=0)
    gather("col", NCOL, gb_col.at[me_c], send.at[3], recv.at[3])
    c_low = cr.T
    for jb in range(JBD):
        for t in range(CHUNK // K):
            ct[jb * R:(jb + 1) * R, t * K:(t + 1) * K] = c_low
    whose = lax.shift_right_logical(lax.broadcasted_iota(jnp.int32, (JPC, CHUNK), 1), 6)
    ones[...] = jnp.where(whose == lax.broadcasted_iota(jnp.int32, (JPC, CHUNK), 0), 1.0, 0.0).astype(BF16)
    wait_bytes(gb_col.at[pl.ds(0, NCOL - 1)], recv.at[3])
    for i in range(32):
        gb_full[me_r, i:i + 1, :] = gb_col[i]
    gather("row", NROW, gb_full.at[me_r], send.at[5], recv.at[5])

    wait_bytes(m_recv, recv.at[2])
    mine = part[core, chip] + pair_recv[chip] + jnp.sum(m_recv[...].astype(F32), axis=0)
    ms[core, chip] = mine.astype(BF16)

    def from_chip(k, carry):
        piece = ms.at[core, chip]
        pltpu.make_async_remote_copy(
            src_ref=piece, dst_ref=piece, send_sem=send.at[4], recv_sem=recv.at[4],
            device_id={"col": lax.rem(chip + k, CHIPS) * 2 + core}, device_id_type=MESH,
        ).start()
        return carry

    lax.fori_loop(1, CHIPS, from_chip, 0)

    wait_bytes(gb_full.at[pl.ds(0, NROW - 1)], recv.at[5])
    solved, worst_one = short_inverse(gb_full[...].reshape(R, R) * gram_c[...])
    inv1[...] = solved
    m16[...] = dot_hi(mine, solved)

    wait_bytes(m_recv, recv.at[4])
    to_mate(ms.at[core], ms.at[core], 6)
    wait_bytes(ms.at[0], recv.at[6])
    for at in range(NCOL):
        slab[at * SHARE_A:(at + 1) * SHARE_A, :] = ms[at % 2, at // 2]

    gram[...] = jnp.dot(slab[...].T, slab[...], preferred_element_type=F32)
    g_piece[...] = gram[pl.ds(pl.multiple_of(core * BLK, BLK), BLK), :].reshape(NROW, SHARE_G, R)
    scatter("row", NROW, g_piece, g_recv, send.at[7], recv.at[7])

    top = inv1[...].astype(BF16)
    rest = (inv1[...] - top.astype(F32)).astype(BF16)
    last = (((1,), (1,)), ((), ()))
    turned[...] = lax.dot_general(top, slab[...], last, preferred_element_type=F32) + lax.dot_general(
        rest, slab[...], last, preferred_element_type=F32
    )
    for s in range(SLOTS):
        p = pos[0, s]
        live = jnp.where(count > s, 1.0, 0.0).astype(F32)
        for jb in range(JBD):
            tile = jnp.zeros((R, BLK), F32)
            for ib in range(IBD):
                tile += turned[:, ib * BLK:(ib + 1) * BLK] * jnp.where(p == ib * JBD + jb, live, 0.0)
            lhs[jb * R:(jb + 1) * R, s * BLK:(s + 1) * BLK] = tile.astype(BF16)

    def mode_two(group, carry):
        for side in range(2):
            ch = 2 * group + side
            t = jnp.dot(lhs[...], x_v[:, chunk(ch)], preferred_element_type=F32)
            t = (t * ct[...]).astype(BF16)
            rows = lax.dot_general(ones[...], t, last, preferred_element_type=F32).astype(BF16)
            for jb in range(JBD):
                pb[jb * (NROW // 2) + group, side * JPC:(side + 1) * JPC, :] = rows[:, jb * R:(jb + 1) * R]
        for jb in range(JBD):
            to = jb * (NROW // 2) + group

            @pl.when(to != me_r)
            def _():
                pltpu.make_async_remote_copy(
                    src_ref=pb.at[to], dst_ref=pb_recv.at[lax.rem(to - me_r + NROW, NROW) - 1],
                    send_sem=send.at[10], recv_sem=recv.at[10],
                    device_id={"row": to}, device_id_type=MESH,
                ).start()

        return carry

    lax.fori_loop(0, 2, mode_two, 0)
    wait_bytes(g_recv, recv.at[7])
    g_full[core, me_r] = g_piece[me_r] + jnp.sum(g_recv[...], axis=0)
    gather("row", NROW, g_full.at[core, me_r], send.at[8], recv.at[8])
    lax.fori_loop(2, 4, mode_two, 0)
    wait_bytes(g_recv, recv.at[8])
    to_mate(g_full.at[core], g_full.at[core], 9)

    wait_bytes(g_full.at[0], recv.at[9])
    solved = inv1[...]
    gram_a = dot_three(dot_three(solved, g_full[...].reshape(R, R)), solved)
    down, across = diagonals(gram_a)
    down = 1.0 / jnp.sqrt(down / ROWS_A + EPS)
    across = 1.0 / jnp.sqrt(across / ROWS_A + EPS)
    a_out[...] = m16[...] * across
    inv2, worst_two = short_inverse(gram_a * down * across * gram_c[...])
    worst_out[...] = jnp.maximum(worst_one, worst_two)

    wait_bytes(pb_recv, recv.at[10])
    m2 = (pb[me_r].astype(F32) + jnp.sum(pb_recv[...].astype(F32), axis=0)) * across
    raw = dot_hi(m2, inv2)
    sq_piece[...] = jnp.sum(raw * raw, axis=0, keepdims=True)
    spread("row", NROW, sq_piece, sq_row, send.at[11], recv.at[11])
    wait_bytes(sq_row, recv.at[11])
    sq_all[...] = sq_piece[...] + jnp.sum(sq_row[...], axis=0)
    spread("col", NCOL, sq_all, sq_col, send.at[12], recv.at[12])
    wait_bytes(gb_recv, send.at[0])
    wait_bytes(pair_recv, send.at[1])
    wait_bytes(m_recv, send.at[2])
    wait_bytes(gb_col.at[pl.ds(0, NCOL - 1)], send.at[3])
    wait_bytes(m_recv, send.at[4])
    wait_bytes(gb_full.at[pl.ds(0, NROW - 1)], send.at[5])
    wait_bytes(ms.at[0], send.at[6])
    wait_bytes(g_recv, send.at[7])
    wait_bytes(g_recv, send.at[8])
    wait_bytes(g_full.at[0], send.at[9])
    wait_bytes(pb_recv, send.at[10])
    wait_bytes(sq_row, send.at[11])
    wait_bytes(sq_col, recv.at[12])
    squares = sq_all[...] + jnp.sum(sq_col[...], axis=0)
    b_out[...] = raw / jnp.sqrt(squares / ROWS_B + EPS)
    wait_bytes(sq_col, send.at[12])


VM = pl.BlockSpec(memory_space=pltpu.VMEM)
SM = pl.BlockSpec(memory_space=pltpu.SMEM)
ANY = pl.BlockSpec(memory_space=pl.ANY)


def shape(dims, kind=F32):
    return jax.ShapeDtypeStruct(dims, kind)


def three_kernels(place, block_count, flat, factor_b, factor_c):
    vm, dma = pltpu.VMEM, pltpu.SemaphoreType.DMA
    gram_b, m16, ms, g = pl.pallas_call(
        kernel_a,
        name="mode_one",
        out_shape=(shape((R, R)), shape((SHARE_A, R)), shape((SLAB_A, R), BF16), shape((R, R))),
        in_specs=[SM, SM, ANY, VM, VM],
        out_specs=[VM] * 4,
        scratch_shapes=[
            vm((SLAB_A, WIDE), BF16), dma((NCH,)), vm((R, R), F32), vm((CHUNK, JBD * R), BF16), vm((SLAB_A, JBD * R), F32),
            vm((R, R), F32), vm((NCOL, 1, R), F32), vm((NCOL - 1, 1, R), F32), vm((NCOL, 1, R), F32), vm((NROW, 32, R), F32),
            vm((2, CHIPS, SHARE_A, R), F32), vm((CHIPS, SHARE_A, R), F32), vm((CHIPS, SHARE_A, R), BF16),
            vm((CHIPS - 1, SHARE_A, R), BF16), vm((2, CHIPS, SHARE_A, R), BF16),
            vm((NROW, SHARE_G, R), F32), vm((NROW - 1, SHARE_G, R), F32), vm((2, NROW, SHARE_G, R), F32),
            dma((10,)), dma((10,)),
        ],
        compiler_params=pltpu.CompilerParams(collective_id=1, has_side_effects=True),
    )(place, block_count, flat, factor_b, factor_c)
    hat_a, lhs, inv = pl.pallas_call(
        kernel_b,
        name="solve_two",
        out_shape=(shape((SHARE_A, R)), shape((JBD * R, SLAB_A), BF16), shape((R, R))),
        in_specs=[SM, SM, VM, VM, VM, VM, VM],
        out_specs=[VM] * 3,
        scratch_shapes=[vm((R, R), F32), vm((R, R), F32), vm((R, R), F32), vm((SLAB_A, R), F32)],
    )(place, block_count, factor_c, gram_b, m16, ms, g)
    hat_b = pl.pallas_call(
        kernel_c,
        name="mode_two",
        out_shape=shape((SHARE_B, R)),
        in_specs=[ANY, VM, VM, VM],
        out_specs=VM,
        scratch_shapes=[
            vm((SLAB_A, WIDE), BF16), dma((NCH,)), vm((JBD * R, CHUNK), F32), vm((JBD * R, BLK), F32),
            vm((NROW, SHARE_B, R), BF16), vm((NROW - 1, SHARE_B, R), BF16),
            vm((1, R), F32), vm((NROW - 1, 1, R), F32), vm((1, R), F32), vm((NCOL - 1, 1, R), F32),
            dma((3,)), dma((3,)),
        ],
        compiler_params=pltpu.CompilerParams(collective_id=2, has_side_effects=True),
    )(flat, factor_c, lhs, inv)
    return hat_a, hat_b


def body(blocks, factor_b, factor_c, block_pos, block_count):
    args = (block_pos.T, block_count, blocks.reshape(SLOTS * BLK, WIDE), factor_b, factor_c)
    vm, dma = pltpu.VMEM, pltpu.SemaphoreType.DMA
    hat_a, hat_b, worst = pl.pallas_call(
        kernel_m,
        name="sweep",
        out_shape=(shape((SHARE_A, R)), shape((SHARE_B, R)), shape((1, 1))),
        in_specs=[SM, SM, ANY, VM, VM],
        out_specs=[VM] * 3,
        scratch_shapes=[
            vm((SLAB_A, WIDE), BF16), dma((NCH,)), vm((R, R), F32), vm((JBD, CHUNK, R), BF16),
            vm((JBD, CHUNK, R), BF16), vm((SLAB_A, R), F32),
            vm((R, R), F32), vm((NCOL, 1, R), F32), vm((NCOL - 1, 1, R), F32), vm((NCOL, 1, R), F32), vm((NROW, 32, R), F32),
            vm((2, CHIPS, SHARE_A, R), F32), vm((CHIPS, SHARE_A, R), F32), vm((CHIPS, SHARE_A, R), BF16),
            vm((CHIPS - 1, SHARE_A, R), BF16), vm((2, CHIPS, SHARE_A, R), BF16), vm((SHARE_A, R), F32),
            vm((NROW, SHARE_G, R), F32), vm((NROW - 1, SHARE_G, R), F32), vm((2, NROW, SHARE_G, R), F32),
            vm((R, R), F32), vm((R, R), F32), vm((SLAB_A, R), BF16), vm((R, SLAB_A), F32), vm((JBD * R, SLAB_A), BF16),
            vm((JBD * R, CHUNK), F32), vm((JPC, CHUNK), BF16),
            vm((NROW, SHARE_B, R), BF16), vm((NROW - 1, SHARE_B, R), BF16),
            vm((1, R), F32), vm((NROW - 1, 1, R), F32), vm((1, R), F32), vm((NCOL - 1, 1, R), F32),
            dma((13,)), dma((13,)),
        ],
        compiler_params=pltpu.CompilerParams(collective_id=0, has_side_effects=True),
    )(*args)
    return lax.cond(worst[0, 0] <= 1e-3, lambda: (hat_a, hat_b), lambda: three_kernels(*args))


def solution(mesh):
    return jax.shard_map(
        body,
        mesh=mesh,
        in_specs=(P("row", "col", None), P("col", None), P(), P("row", "col"), P("row", "col")),
        out_specs=(P(("row", "col"), None), P(("col", "row"), None)),
        check_vma=False,
    )
```

```python
import functools

import jax
import jax.numpy as jnp
from jax import lax
from jax.experimental import pallas as pl
from jax.experimental.pallas import tpu as pltpu
from jax.sharding import PartitionSpec as P

MESH = pl.DeviceIdType.MESH
HIGH = lax.Precision.HIGHEST
F32 = jnp.float32
BF16 = jnp.bfloat16
NROW, NCOL = 8, 32
R, K, BLK, SLOTS, IBD, JBD = 256, 64, 128, 4, 4, 2
SLAB_A = IBD * BLK
SLAB_B = JBD * BLK
WIDE = BLK * K
CHUNK = 1024
NCH = WIDE // CHUNK
JPC = CHUNK // K
SHARE_A = SLAB_A // NCOL
SHARE_B = SLAB_B // NROW
CHIPS = NCOL // 2
SHARE_G = BLK // NROW
PLANE = NROW * 4
ROWS_A = SLAB_A * NROW
ROWS_B = SLAB_B * NCOL
EPS = 1e-06
MAX_IT = 80


def dot_hi(a, b):
    return jnp.dot(a, b, precision=HIGH, preferred_element_type=F32)


def wait_bytes(ref, sem):
    pltpu.make_async_copy(ref, ref, sem).wait()


def greet(axes):
    barrier = pltpu.get_barrier_semaphore()
    total = 0
    for axis, count in axes:
        me = lax.axis_index(axis)

        def one(k, carry, axis=axis, count=count, me=me):
            pl.semaphore_signal(
                barrier, inc=1, device_id={axis: lax.rem(me + k, count)}, device_id_type=MESH
            )
            return carry

        lax.fori_loop(1, count, one, 0)
        total += count - 1
    return barrier, total


def scatter(axis, count, src, dst, send, recv):
    me = lax.axis_index(axis)

    def one(k, carry):
        d = lax.rem(me + k, count)
        pltpu.make_async_remote_copy(
            src_ref=src.at[d], dst_ref=dst.at[k - 1], send_sem=send, recv_sem=recv,
            device_id={axis: d}, device_id_type=MESH,
        ).start()
        return carry

    lax.fori_loop(1, count, one, 0)


def gather(axis, count, piece, send, recv):
    me = lax.axis_index(axis)

    def one(k, carry):
        pltpu.make_async_remote_copy(
            src_ref=piece, dst_ref=piece, send_sem=send, recv_sem=recv,
            device_id={axis: lax.rem(me + k, count)}, device_id_type=MESH,
        ).start()
        return carry

    lax.fori_loop(1, count, one, 0)


def spread(axis, count, src, dst, send, recv):
    me = lax.axis_index(axis)

    def one(k, carry):
        pltpu.make_async_remote_copy(
            src_ref=src, dst_ref=dst.at[k - 1], send_sem=send, recv_sem=recv,
            device_id={axis: lax.rem(me + k, count)}, device_id_type=MESH,
        ).start()
        return carry

    lax.fori_loop(1, count, one, 0)


def kernel_a(
    pos, cnt, x_hbm, b_ref, c_ref,
    gb_out, m16_out, ms_out, g_out,
    x_v, x_sem, br, w_v, acc,
    gram, gb_part, gb_recv, gb_col, gb_full,
    part, pair_recv, half, m_recv, ms, g_piece, g_recv, g_full,
    send, recv,
):
    me_r, me_c = lax.axis_index("row"), lax.axis_index("col")
    chip, core = me_c // 2, lax.rem(me_c, 2)
    mate = chip * 2 + 1 - core

    def to_mate(src, dst, n):
        pltpu.make_async_remote_copy(
            src_ref=src, dst_ref=dst, send_sem=send.at[n], recv_sem=recv.at[n],
            device_id={"col": mate}, device_id_type=MESH,
        ).start()

    def x_copy(ch):
        cols = pl.ds(pl.multiple_of(ch * CHUNK, CHUNK), CHUNK)
        return pltpu.make_async_copy(x_hbm.at[:, cols], x_v.at[:, cols], x_sem.at[ch])

    for ch in range(NCH):
        x_copy(ch).start()
    barrier, partners = greet((("col", NCOL), ("row", NROW)))

    b = b_ref[...]
    gram[...] = dot_hi(b.T, b)
    rows = gram[pl.ds(pl.multiple_of(me_r * 32, 32), 32), :]
    for i in range(32):
        gb_part[i] = rows[i:i + 1, :]
    br[...] = b.astype(BF16).astype(F32)
    cr = c_ref[...].astype(BF16).astype(F32)
    acc[...] = jnp.zeros_like(acc)

    def mode_one(ch, carry):
        for jb in range(JBD):
            tile = br[pl.ds(pl.multiple_of(jb * BLK + ch * JPC, JPC), JPC), :]
            for j in range(JPC):
                w_v[j * K:(j + 1) * K, jb * R:(jb + 1) * R] = (tile[j:j + 1, :] * cr).astype(BF16)
        x_copy(ch).wait()
        x = x_v[:, pl.ds(pl.multiple_of(ch * CHUNK, CHUNK), CHUNK)]
        acc[...] += jnp.dot(x, w_v[...], preferred_element_type=F32)
        return carry

    lax.fori_loop(0, NCH - 3, mode_one, 0)
    pl.semaphore_wait(barrier, partners)
    scatter("col", NCOL, gb_part, gb_recv, send.at[0], recv.at[0])
    lax.fori_loop(NCH - 3, NCH, mode_one, 0)

    count = cnt[0, 0]
    for ib in range(IBD):
        total = jnp.zeros((BLK, R), F32)
        for s in range(SLOTS):
            p = pos[0, s]
            live = jnp.where(count > s, 1.0, 0.0).astype(F32)
            for jb in range(JBD):
                keep = jnp.where(p == ib * JBD + jb, live, 0.0)
                total += acc[s * BLK:(s + 1) * BLK, jb * R:(jb + 1) * R] * keep
        for t in range(BLK // SHARE_A):
            at = ib * (BLK // SHARE_A) + t
            part[at % 2, at // 2] = total[t * SHARE_A:(t + 1) * SHARE_A, :]

    to_mate(part.at[1 - core], pair_recv, 1)
    wait_bytes(pair_recv, recv.at[1])
    half[...] = (part[core] + pair_recv[...]).astype(BF16)

    def to_chip(k, carry):
        d = lax.rem(chip + k, CHIPS)
        pltpu.make_async_remote_copy(
            src_ref=half.at[d], dst_ref=m_recv.at[k - 1], send_sem=send.at[2], recv_sem=recv.at[2],
            device_id={"col": d * 2 + core}, device_id_type=MESH,
        ).start()
        return carry

    lax.fori_loop(1, CHIPS, to_chip, 0)

    wait_bytes(gb_recv, recv.at[0])
    gb_col[me_c] = gb_part[me_c] + jnp.sum(gb_recv[...], axis=0)
    gather("col", NCOL, gb_col.at[me_c], send.at[3], recv.at[3])

    wait_bytes(m_recv, recv.at[2])
    m16 = part[core, chip] + pair_recv[chip] + jnp.sum(m_recv[...].astype(F32), axis=0)
    ms[core, chip] = m16.astype(BF16)

    def from_chip(k, carry):
        piece = ms.at[core, chip]
        pltpu.make_async_remote_copy(
            src_ref=piece, dst_ref=piece, send_sem=send.at[4], recv_sem=recv.at[4],
            device_id={"col": lax.rem(chip + k, CHIPS) * 2 + core}, device_id_type=MESH,
        ).start()
        return carry

    lax.fori_loop(1, CHIPS, from_chip, 0)
    m16_out[...] = m16

    wait_bytes(gb_col.at[pl.ds(0, NCOL - 1)], recv.at[3])
    for i in range(32):
        gb_full[me_r, i:i + 1, :] = gb_col[i]
    gather("row", NROW, gb_full.at[me_r], send.at[5], recv.at[5])

    wait_bytes(m_recv, recv.at[4])
    to_mate(ms.at[core], ms.at[core], 6)
    wait_bytes(ms.at[0], recv.at[6])

    slab = ms[...].reshape(SLAB_A, R)
    gram[...] = jnp.dot(slab.T, slab, preferred_element_type=F32)
    g_piece[...] = gram[pl.ds(pl.multiple_of(core * BLK, BLK), BLK), :].reshape(NROW, SHARE_G, R)
    scatter("row", NROW, g_piece, g_recv, send.at[7], recv.at[7])
    for at in range(NCOL):
        ms_out[at * SHARE_A:(at + 1) * SHARE_A, :] = ms[at % 2, at // 2]
    wait_bytes(g_recv, recv.at[7])
    g_full[core, me_r] = g_piece[me_r] + jnp.sum(g_recv[...], axis=0)
    gather("row", NROW, g_full.at[core, me_r], send.at[8], recv.at[8])
    wait_bytes(gb_full.at[pl.ds(0, NROW - 1)], recv.at[5])
    gb_out[...] = gb_full[...].reshape(R, R)
    wait_bytes(g_recv, recv.at[8])
    to_mate(g_full.at[core], g_full.at[core], 9)
    wait_bytes(g_full.at[0], recv.at[9])
    g_out[...] = g_full[...].reshape(R, R)

    wait_bytes(gb_recv, send.at[0])
    wait_bytes(pair_recv, send.at[1])
    wait_bytes(m_recv, send.at[2])
    wait_bytes(gb_col.at[pl.ds(0, NCOL - 1)], send.at[3])
    wait_bytes(m_recv, send.at[4])
    wait_bytes(gb_full.at[pl.ds(0, NROW - 1)], send.at[5])
    wait_bytes(ms.at[0], send.at[6])
    wait_bytes(g_recv, send.at[7])
    wait_bytes(g_recv, send.at[8])
    wait_bytes(g_full.at[0], send.at[9])


def eye():
    return lax.broadcasted_iota(jnp.int32, (R, R), 0) == lax.broadcasted_iota(jnp.int32, (R, R), 1)


def diagonals(v):
    only = jnp.where(eye(), v, 0.0)
    return jnp.sum(only, axis=1, keepdims=True), jnp.sum(only, axis=0, keepdims=True)


def inverse(v, x_ref, r_ref, c_ref):
    down, across = diagonals(v)
    down, across = 1.0 / jnp.sqrt(down), 1.0 / jnp.sqrt(across)
    unit = jnp.where(eye(), 1.0, 0.0)
    c = v * down * across
    c_ref[...] = c
    norm = jnp.max(jnp.sum(jnp.abs(c), axis=1, keepdims=True))
    alpha = jnp.where(norm < 1.9, 1.0, 1.0 / norm)
    res = unit - alpha * c
    x_ref[...] = alpha * (unit + res)
    res = unit - dot_hi(c, x_ref[...])
    r_ref[...] = res

    def more(state):
        it, size, before = state
        return (it < MAX_IT) & (size > 1e-5) & ((size > 1e-3) | (size < 0.5 * before))

    def step(state):
        it, size, _ = state
        x = x_ref[...]
        x = x + dot_hi(x, r_ref[...])
        x_ref[...] = x
        res = unit - dot_hi(c_ref[...], x)
        r_ref[...] = res
        return it + 1, jnp.max(jnp.abs(res)), size

    lax.while_loop(more, step, (0, jnp.max(jnp.abs(res)), jnp.float32(1e30)))
    x = x_ref[...]
    x = x + dot_hi(x, r_ref[...])
    return x * down * across


def kernel_b(
    pos, cnt, c_ref, gb_ref, m16_ref, ms_ref, g_ref,
    a_out, lhs_out, inv_out,
    x1, r1, c1, slab,
):
    c = c_ref[...]
    gram_c = dot_hi(c.T, c)
    inv1 = inverse(gb_ref[...] * gram_c, x1, r1, c1)
    gram_a = dot_hi(dot_hi(inv1, g_ref[...]), inv1)
    down, across = diagonals(gram_a)
    down = 1.0 / jnp.sqrt(down / ROWS_A + EPS)
    across = 1.0 / jnp.sqrt(across / ROWS_A + EPS)
    a_out[...] = dot_hi(m16_ref[...], inv1) * across
    slab[...] = dot_hi(ms_ref[...].astype(F32), inv1) * across

    inv_out[...] = inverse(gram_a * down * across * gram_c, x1, r1, c1)

    count = cnt[0, 0]
    for s in range(SLOTS):
        p = pos[0, s]
        tile = slab[pl.ds(pl.multiple_of(lax.shift_right_logical(p, 1) * BLK, BLK), BLK), :].T
        for jb in range(JBD):
            keep = jnp.where((count > s) & ((p & 1) == jb), 1.0, 0.0)
            lhs_out[jb * R:(jb + 1) * R, s * BLK:(s + 1) * BLK] = (tile * keep).astype(BF16)


def kernel_c(
    x_hbm, c_ref, lhs, inv_ref,
    b_out,
    x_v, x_sem, ct, acc, pb, pb_recv, sq_piece, sq_row, sq_all, sq_col, send, recv,
):
    me_r = lax.axis_index("row")

    def x_copy(ch):
        cols = pl.ds(pl.multiple_of(ch * CHUNK, CHUNK), CHUNK)
        return pltpu.make_async_copy(x_hbm.at[:, cols], x_v.at[:, cols], x_sem.at[ch])

    for ch in range(NCH):
        x_copy(ch).start()
    barrier, partners = greet((("row", NROW), ("col", NCOL)))
    c_low = c_ref[...].astype(BF16).astype(F32).T
    for jb in range(JBD):
        for t in range(CHUNK // K):
            ct[jb * R:(jb + 1) * R, t * K:(t + 1) * K] = c_low
    acc[...] = jnp.zeros_like(acc)

    def mode_two(ch, carry):
        x_copy(ch).wait()
        x = x_v[:, pl.ds(pl.multiple_of(ch * CHUNK, CHUNK), CHUNK)]
        t = jnp.dot(lhs[...], x, preferred_element_type=F32)
        t = (t * ct[...]).astype(BF16)
        j = lax.shift_right_logical(lax.broadcasted_iota(jnp.int32, (CHUNK, BLK), 0), 6) + ch * JPC
        ones = jnp.where(j == lax.broadcasted_iota(jnp.int32, (CHUNK, BLK), 1), 1.0, 0.0).astype(BF16)
        acc[...] += jnp.dot(t, ones, preferred_element_type=F32)
        return carry

    lax.fori_loop(0, NCH, mode_two, 0)
    for jb in range(JBD):
        rows = acc[jb * R:(jb + 1) * R, :].T.astype(BF16)
        for t in range(BLK // SHARE_B):
            pb[jb * (BLK // SHARE_B) + t] = rows[t * SHARE_B:(t + 1) * SHARE_B, :]

    pl.semaphore_wait(barrier, partners)
    scatter("row", NROW, pb, pb_recv, send.at[0], recv.at[0])
    wait_bytes(pb_recv, recv.at[0])
    m2 = pb[me_r].astype(F32) + jnp.sum(pb_recv[...].astype(F32), axis=0)
    raw = dot_hi(m2, inv_ref[...])
    sq_piece[...] = jnp.sum(raw * raw, axis=0, keepdims=True)
    spread("row", NROW, sq_piece, sq_row, send.at[1], recv.at[1])
    wait_bytes(sq_row, recv.at[1])
    sq_all[...] = sq_piece[...] + jnp.sum(sq_row[...], axis=0)
    spread("col", NCOL, sq_all, sq_col, send.at[2], recv.at[2])
    wait_bytes(sq_col, recv.at[2])
    squares = sq_all[...] + jnp.sum(sq_col[...], axis=0)
    b_out[...] = raw / jnp.sqrt(squares / ROWS_B + EPS)
    wait_bytes(pb_recv, send.at[0])
    wait_bytes(sq_row, send.at[1])
    wait_bytes(sq_col, send.at[2])


def low_dot(a, b):
    return jnp.dot(a.astype(BF16), b.astype(BF16), preferred_element_type=F32)


def dot_three(a, b):
    a_top, b_top = a.astype(BF16), b.astype(BF16)
    a_rest, b_rest = (a - a_top.astype(F32)).astype(BF16), (b - b_top.astype(F32)).astype(BF16)
    cross = jnp.dot(a_top, b_rest, preferred_element_type=F32) + jnp.dot(a_rest, b_top, preferred_element_type=F32)
    return jnp.dot(a_top, b_top, preferred_element_type=F32) + cross


def first_half(v):
    down, across = diagonals(v)
    down, across = 1.0 / jnp.sqrt(down), 1.0 / jnp.sqrt(across)
    unit = jnp.where(eye(), 1.0, 0.0)
    c = v * down * across
    norm = jnp.max(jnp.sum(jnp.abs(c), axis=0, keepdims=True), axis=1, keepdims=True)
    alpha = jnp.where(norm < 1.9, 1.0, 1.0 / norm)
    res = unit - alpha * c
    x = alpha * (unit + res)
    x = x + low_dot(x, low_dot(res, res))
    return c, x, down, across


def second_half(c, x, down, across):
    unit = jnp.where(eye(), 1.0, 0.0)
    x = x + low_dot(x, unit - dot_three(c, x))
    res = unit - dot_hi(c, x)
    worst = jnp.max(jnp.sum(jnp.abs(res), axis=0, keepdims=True), axis=1, keepdims=True)
    x = x + low_dot(x, res)
    return x * down * across, worst


def kernel_m(
    pos, cnt, x_hbm, b_ref, c_ref,
    a_out, b_out, worst_out,
    x_v, x_sem, br, w_even, w_odd, acc,
    gram, gb_part, gb_recv, gb_col, gb_full,
    part, pair_recv, half, m_recv, ms, m16, g_piece, g_recv, g_full,
    gram_c, inv1, slab, turned, lhs, ct, ones,
    pb, pb_recv, sq_piece, sq_row, sq_all, sq_col,
    send, recv,
):
    me_r, me_c = lax.axis_index("row"), lax.axis_index("col")
    chip, core = me_c // 2, lax.rem(me_c, 2)
    mate = chip * 2 + 1 - core

    def to_mate(src, dst, n):
        pltpu.make_async_remote_copy(
            src_ref=src, dst_ref=dst, send_sem=send.at[n], recv_sem=recv.at[n],
            device_id={"col": mate}, device_id_type=MESH,
        ).start()

    def chunk(ch):
        return pl.ds(pl.multiple_of(ch * CHUNK, CHUNK), CHUNK)

    def x_copy(ch):
        return pltpu.make_async_copy(x_hbm.at[:, chunk(ch)], x_v.at[:, chunk(ch)], x_sem.at[ch])

    for ch in range(NCH):
        x_copy(ch).start()
    barrier, partners = greet((("col", NCOL),))

    def in_plane(k):
        at = lax.rem(me_r * 4 + lax.rem(me_c, 4) + k, PLANE)
        return at // 4, me_c // 4 * 4 + lax.rem(at, 4)

    def greet_plane(k, carry):
        row, col = in_plane(k)
        pl.semaphore_signal(barrier, inc=1, device_id={"row": row, "col": col}, device_id_type=MESH)
        return carry

    lax.fori_loop(1, PLANE, greet_plane, 0)
    partners += PLANE - 1

    b = b_ref[...]
    gram[...] = dot_hi(b.T, b)
    rows = gram[pl.ds(pl.multiple_of(me_r * 32, 32), 32), :]
    for i in range(32):
        gb_part[i] = rows[i:i + 1, :]
    br[...] = b.astype(BF16).astype(F32)
    cr = c_ref[...].astype(BF16).astype(F32)
    acc[...] = jnp.zeros_like(acc)

    cb = cr.astype(BF16)

    def build(ch, w):
        for jb in range(JBD):
            tile = br[pl.ds(pl.multiple_of(jb * BLK + ch * JPC, JPC), JPC), :]
            for j in range(JPC):
                w[jb, j * K:(j + 1) * K, :] = jnp.broadcast_to(tile[j:j + 1, :].astype(BF16), (K, R)) * cb

    def add(ch, w):
        x_copy(ch).wait()
        for s in range(SLOTS):
            rows = slice(s * BLK, (s + 1) * BLK)
            acc[rows, :] += jnp.dot(x_v[rows, chunk(ch)], w[pos[0, s] & 1], preferred_element_type=F32)

    def mode_one(pair, carry):
        add(2 * pair, w_even)
        build(2 * pair + 1, w_odd)
        add(2 * pair + 1, w_odd)
        build(lax.rem(2 * pair + 2, NCH), w_even)
        return carry

    build(0, w_even)
    lax.fori_loop(0, NCH // 2 - 1, mode_one, 0)
    pl.semaphore_wait(barrier, partners)
    scatter("col", NCOL, gb_part, gb_recv, send.at[0], recv.at[0])
    lax.fori_loop(NCH // 2 - 1, NCH // 2, mode_one, 0)

    count = cnt[0, 0]
    for ib in range(IBD):
        total = jnp.zeros((BLK, R), F32)
        for s in range(SLOTS):
            live = jnp.where(count > s, 1.0, 0.0).astype(F32)
            keep = jnp.where(lax.shift_right_logical(pos[0, s], 1) == ib, live, 0.0)
            total += acc[s * BLK:(s + 1) * BLK, :] * keep
        for t in range(BLK // SHARE_A):
            at = ib * (BLK // SHARE_A) + t
            part[at % 2, at // 2] = total[t * SHARE_A:(t + 1) * SHARE_A, :]

    to_mate(part.at[1 - core], pair_recv, 1)
    c = c_ref[...]
    gram_c[...] = dot_hi(c.T, c)
    wait_bytes(pair_recv, recv.at[1])
    half[...] = (part[core] + pair_recv[...]).astype(BF16)

    def to_chip(k, carry):
        d = lax.rem(chip + k, CHIPS)
        pltpu.make_async_remote_copy(
            src_ref=half.at[d], dst_ref=m_recv.at[k - 1], send_sem=send.at[2], recv_sem=recv.at[2],
            device_id={"col": d * 2 + core}, device_id_type=MESH,
        ).start()
        return carry

    lax.fori_loop(1, CHIPS, to_chip, 0)

    wait_bytes(gb_recv, recv.at[0])
    gb_col[me_c] = gb_part[me_c] + jnp.sum(gb_recv[...], axis=0)
    gather("col", NCOL, gb_col.at[me_c], send.at[3], recv.at[3])
    c_low = cr.T
    for jb in range(JBD):
        for t in range(CHUNK // K):
            ct[jb * R:(jb + 1) * R, t * K:(t + 1) * K] = c_low
    whose = lax.shift_right_logical(lax.broadcasted_iota(jnp.int32, (JPC, CHUNK), 1), 6)
    ones[...] = jnp.where(whose == lax.broadcasted_iota(jnp.int32, (JPC, CHUNK), 0), 1.0, 0.0).astype(BF16)
    wait_bytes(gb_col.at[pl.ds(0, NCOL - 1)], recv.at[3])
    for i in range(16):
        gb_full[core, me_r, i:i + 1, :] = gb_col[core * 16 + i]
    gather("row", NROW, gb_full.at[core, me_r], send.at[5], recv.at[5])

    wait_bytes(m_recv, recv.at[2])
    mine = part[core, chip] + pair_recv[chip] + jnp.sum(m_recv[...].astype(F32), axis=0)
    ms[core, chip] = mine.astype(BF16)

    def from_chip(k, carry):
        piece = ms.at[core, chip]
        pltpu.make_async_remote_copy(
            src_ref=piece, dst_ref=piece, send_sem=send.at[4], recv_sem=recv.at[4],
            device_id={"col": lax.rem(chip + k, CHIPS) * 2 + core}, device_id_type=MESH,
        ).start()
        return carry

    lax.fori_loop(1, CHIPS, from_chip, 0)

    wait_bytes(gb_full.at[0, pl.ds(0, NROW - 1)], recv.at[5])
    to_mate(gb_full.at[core], gb_full.at[core], 13)
    m16[...] = mine
    wait_bytes(gb_full.at[0], recv.at[13])
    for at in range(R // 16):
        gram[at * 16:(at + 1) * 16, :] = gb_full[at % 2, at // 2]
    c_one, x_one, down_one, across_one = first_half(gram[...] * gram_c[...])
    turned[:, :R] = c_one
    turned[:, R:] = x_one

    wait_bytes(m_recv, recv.at[4])
    to_mate(ms.at[core], ms.at[core], 6)
    wait_bytes(ms.at[0], recv.at[6])
    for at in range(NCOL):
        slab[at * SHARE_A:(at + 1) * SHARE_A, :] = ms[at % 2, at // 2]

    gram[...] = jnp.dot(slab[...].T, slab[...], preferred_element_type=F32)
    g_piece[...] = gram[pl.ds(pl.multiple_of(core * BLK, BLK), BLK), :].reshape(NROW, SHARE_G, R)
    scatter("row", NROW, g_piece, g_recv, send.at[7], recv.at[7])

    solved, worst_one = second_half(turned[:, :R], turned[:, R:], down_one, across_one)
    inv1[...] = solved
    top = inv1[...].astype(BF16)
    rest = (inv1[...] - top.astype(F32)).astype(BF16)
    last = (((1,), (1,)), ((), ()))
    turned[...] = lax.dot_general(top, slab[...], last, preferred_element_type=F32) + lax.dot_general(
        rest, slab[...], last, preferred_element_type=F32
    )
    for s in range(SLOTS):
        p = pos[0, s]
        live = jnp.where(count > s, 1.0, 0.0).astype(F32)
        for jb in range(JBD):
            tile = jnp.zeros((R, BLK), F32)
            for ib in range(IBD):
                tile += turned[:, ib * BLK:(ib + 1) * BLK] * jnp.where(p == ib * JBD + jb, live, 0.0)
            lhs[jb * R:(jb + 1) * R, s * BLK:(s + 1) * BLK] = tile.astype(BF16)

    def mode_two(group, carry):
        for side in range(2):
            ch = 2 * group + side
            t = jnp.dot(lhs[...], x_v[:, chunk(ch)], preferred_element_type=F32)
            t = (t * ct[...]).astype(BF16)
            rows = lax.dot_general(ones[...], t, last, preferred_element_type=F32).astype(BF16)
            for jb in range(JBD):
                pb[jb * (NROW // 2) + group, side * JPC:(side + 1) * JPC, :] = rows[:, jb * R:(jb + 1) * R]
        for jb in range(JBD):
            to = jb * (NROW // 2) + group

            @pl.when(to != me_r)
            def _():
                pltpu.make_async_remote_copy(
                    src_ref=pb.at[to], dst_ref=pb_recv.at[lax.rem(to - me_r + NROW, NROW) - 1],
                    send_sem=send.at[10], recv_sem=recv.at[10],
                    device_id={"row": to}, device_id_type=MESH,
                ).start()

        return carry

    lax.fori_loop(0, 2, mode_two, 0)
    wait_bytes(g_recv, recv.at[7])
    g_full[core, me_r] = g_piece[me_r] + jnp.sum(g_recv[...], axis=0)
    gather("row", NROW, g_full.at[core, me_r], send.at[8], recv.at[8])
    lax.fori_loop(2, 4, mode_two, 0)
    wait_bytes(g_recv, recv.at[8])
    to_mate(g_full.at[core], g_full.at[core], 9)

    wait_bytes(g_full.at[0], recv.at[9])
    solved = inv1[...]
    gram_a = dot_three(dot_three(solved, g_full[...].reshape(R, R)), solved)
    down, across = diagonals(gram_a)
    down = 1.0 / jnp.sqrt(down / ROWS_A + EPS)
    across = 1.0 / jnp.sqrt(across / ROWS_A + EPS)
    a_out[...] = dot_three(m16[...], solved) * across
    inv2, worst_two = second_half(*first_half(gram_a * down * across * gram_c[...]))
    worst_out[...] = jnp.maximum(worst_one, worst_two)

    wait_bytes(pb_recv, recv.at[10])
    m2 = (pb[me_r].astype(F32) + jnp.sum(pb_recv[...].astype(F32), axis=0)) * across
    raw = dot_hi(m2, inv2)
    sq_piece[...] = jnp.sum(raw * raw, axis=0, keepdims=True)

    def to_plane(k, carry):
        row, col = in_plane(k)
        pltpu.make_async_remote_copy(
            src_ref=sq_piece, dst_ref=sq_col.at[k - 1], send_sem=send.at[11], recv_sem=recv.at[11],
            device_id={"row": row, "col": col}, device_id_type=MESH,
        ).start()
        return carry

    lax.fori_loop(1, PLANE, to_plane, 0)
    wait_bytes(sq_col, recv.at[11])
    sq_all[...] = sq_piece[...] + jnp.sum(sq_col[...], axis=0)

    def to_planes(k, carry):
        pltpu.make_async_remote_copy(
            src_ref=sq_all, dst_ref=sq_row.at[k - 1], send_sem=send.at[12], recv_sem=recv.at[12],
            device_id={"col": lax.rem(me_c + k * 4, NCOL)}, device_id_type=MESH,
        ).start()
        return carry

    lax.fori_loop(1, NCOL // 4, to_planes, 0)
    wait_bytes(gb_recv, send.at[0])
    wait_bytes(pair_recv, send.at[1])
    wait_bytes(m_recv, send.at[2])
    wait_bytes(gb_col.at[pl.ds(0, NCOL - 1)], send.at[3])
    wait_bytes(m_recv, send.at[4])
    wait_bytes(gb_full.at[0, pl.ds(0, NROW - 1)], send.at[5])
    wait_bytes(gb_full.at[0], send.at[13])
    wait_bytes(ms.at[0], send.at[6])
    wait_bytes(g_recv, send.at[7])
    wait_bytes(g_recv, send.at[8])
    wait_bytes(g_full.at[0], send.at[9])
    wait_bytes(pb_recv, send.at[10])
    wait_bytes(sq_col, send.at[11])
    wait_bytes(sq_row, recv.at[12])
    squares = sq_all[...] + jnp.sum(sq_row[...], axis=0)
    b_out[...] = raw / jnp.sqrt(squares / ROWS_B + EPS)
    wait_bytes(sq_row, send.at[12])


VM = pl.BlockSpec(memory_space=pltpu.VMEM)
SM = pl.BlockSpec(memory_space=pltpu.SMEM)
ANY = pl.BlockSpec(memory_space=pl.ANY)


def shape(dims, kind=F32):
    return jax.ShapeDtypeStruct(dims, kind)


def three_kernels(place, block_count, flat, factor_b, factor_c):
    vm, dma = pltpu.VMEM, pltpu.SemaphoreType.DMA
    gram_b, m16, ms, g = pl.pallas_call(
        kernel_a,
        name="mode_one",
        out_shape=(shape((R, R)), shape((SHARE_A, R)), shape((SLAB_A, R), BF16), shape((R, R))),
        in_specs=[SM, SM, ANY, VM, VM],
        out_specs=[VM] * 4,
        scratch_shapes=[
            vm((SLAB_A, WIDE), BF16), dma((NCH,)), vm((R, R), F32), vm((CHUNK, JBD * R), BF16), vm((SLAB_A, JBD * R), F32),
            vm((R, R), F32), vm((NCOL, 1, R), F32), vm((NCOL - 1, 1, R), F32), vm((NCOL, 1, R), F32), vm((NROW, 32, R), F32),
            vm((2, CHIPS, SHARE_A, R), F32), vm((CHIPS, SHARE_A, R), F32), vm((CHIPS, SHARE_A, R), BF16),
            vm((CHIPS - 1, SHARE_A, R), BF16), vm((2, CHIPS, SHARE_A, R), BF16),
            vm((NROW, SHARE_G, R), F32), vm((NROW - 1, SHARE_G, R), F32), vm((2, NROW, SHARE_G, R), F32),
            dma((10,)), dma((10,)),
        ],
        compiler_params=pltpu.CompilerParams(collective_id=1, has_side_effects=True),
    )(place, block_count, flat, factor_b, factor_c)
    hat_a, lhs, inv = pl.pallas_call(
        kernel_b,
        name="solve_two",
        out_shape=(shape((SHARE_A, R)), shape((JBD * R, SLAB_A), BF16), shape((R, R))),
        in_specs=[SM, SM, VM, VM, VM, VM, VM],
        out_specs=[VM] * 3,
        scratch_shapes=[vm((R, R), F32), vm((R, R), F32), vm((R, R), F32), vm((SLAB_A, R), F32)],
    )(place, block_count, factor_c, gram_b, m16, ms, g)
    hat_b = pl.pallas_call(
        kernel_c,
        name="mode_two",
        out_shape=shape((SHARE_B, R)),
        in_specs=[ANY, VM, VM, VM],
        out_specs=VM,
        scratch_shapes=[
            vm((SLAB_A, WIDE), BF16), dma((NCH,)), vm((JBD * R, CHUNK), F32), vm((JBD * R, BLK), F32),
            vm((NROW, SHARE_B, R), BF16), vm((NROW - 1, SHARE_B, R), BF16),
            vm((1, R), F32), vm((NROW - 1, 1, R), F32), vm((1, R), F32), vm((NCOL - 1, 1, R), F32),
            dma((3,)), dma((3,)),
        ],
        compiler_params=pltpu.CompilerParams(collective_id=2, has_side_effects=True),
    )(flat, factor_c, lhs, inv)
    return hat_a, hat_b


def body(blocks, factor_b, factor_c, block_pos, block_count):
    args = (block_pos.T, block_count, blocks.reshape(SLOTS * BLK, WIDE), factor_b, factor_c)
    vm, dma = pltpu.VMEM, pltpu.SemaphoreType.DMA
    hat_a, hat_b, worst = pl.pallas_call(
        kernel_m,
        name="sweep",
        out_shape=(shape((SHARE_A, R)), shape((SHARE_B, R)), shape((1, 1))),
        in_specs=[SM, SM, ANY, VM, VM],
        out_specs=[VM] * 3,
        scratch_shapes=[
            vm((SLAB_A, WIDE), BF16), dma((NCH,)), vm((R, R), F32), vm((JBD, CHUNK, R), BF16),
            vm((JBD, CHUNK, R), BF16), vm((SLAB_A, R), F32),
            vm((R, R), F32), vm((NCOL, 1, R), F32), vm((NCOL - 1, 1, R), F32), vm((NCOL, 1, R), F32), vm((2, NROW, 16, R), F32),
            vm((2, CHIPS, SHARE_A, R), F32), vm((CHIPS, SHARE_A, R), F32), vm((CHIPS, SHARE_A, R), BF16),
            vm((CHIPS - 1, SHARE_A, R), BF16), vm((2, CHIPS, SHARE_A, R), BF16), vm((SHARE_A, R), F32),
            vm((NROW, SHARE_G, R), F32), vm((NROW - 1, SHARE_G, R), F32), vm((2, NROW, SHARE_G, R), F32),
            vm((R, R), F32), vm((R, R), F32), vm((SLAB_A, R), BF16), vm((R, SLAB_A), F32), vm((JBD * R, SLAB_A), BF16),
            vm((JBD * R, CHUNK), F32), vm((JPC, CHUNK), BF16),
            vm((NROW, SHARE_B, R), BF16), vm((NROW - 1, SHARE_B, R), BF16),
            vm((1, R), F32), vm((NROW - 1, 1, R), F32), vm((1, R), F32), vm((NCOL - 1, 1, R), F32),
            dma((14,)), dma((14,)),
        ],
        compiler_params=pltpu.CompilerParams(collective_id=0, has_side_effects=True),
    )(*args)
    return lax.cond(worst[0, 0] <= 1e-3, lambda: (hat_a, hat_b), lambda: three_kernels(*args))


def solution(mesh):
    return jax.shard_map(
        body,
        mesh=mesh,
        in_specs=(P("row", "col", None), P("col", None), P(), P("row", "col"), P("row", "col")),
        out_specs=(P(("row", "col"), None), P(("col", "row"), None)),
        check_vma=False,
    )
```

```python
import functools

import jax
import jax.numpy as jnp
from jax import lax
from jax.experimental import pallas as pl
from jax.experimental.pallas import tpu as pltpu
from jax.sharding import PartitionSpec as P

MESH = pl.DeviceIdType.MESH
HIGH = lax.Precision.HIGHEST
F32 = jnp.float32
BF16 = jnp.bfloat16
NROW, NCOL = 8, 32
R, K, BLK, SLOTS, IBD, JBD = 256, 64, 128, 4, 4, 2
SLAB_A = IBD * BLK
SLAB_B = JBD * BLK
WIDE = BLK * K
CHUNK = 1024
NCH = WIDE // CHUNK
JPC = CHUNK // K
SHARE_A = SLAB_A // NCOL
SHARE_B = SLAB_B // NROW
CHIPS = NCOL // 2
SHARE_G = BLK // NROW
PLANE = NROW * 4
PIECE_G = SHARE_G * 3 // 2
ROWS_A = SLAB_A * NROW
ROWS_B = SLAB_B * NCOL
EPS = 1e-06
MAX_IT = 80


def dot_hi(a, b):
    return jnp.dot(a, b, precision=HIGH, preferred_element_type=F32)


def wait_bytes(ref, sem):
    pltpu.make_async_copy(ref, ref, sem).wait()


def greet(axes):
    barrier = pltpu.get_barrier_semaphore()
    total = 0
    for axis, count in axes:
        me = lax.axis_index(axis)

        def one(k, carry, axis=axis, count=count, me=me):
            pl.semaphore_signal(
                barrier, inc=1, device_id={axis: lax.rem(me + k, count)}, device_id_type=MESH
            )
            return carry

        lax.fori_loop(1, count, one, 0)
        total += count - 1
    return barrier, total


def scatter(axis, count, src, dst, send, recv):
    me = lax.axis_index(axis)

    def one(k, carry):
        d = lax.rem(me + k, count)
        pltpu.make_async_remote_copy(
            src_ref=src.at[d], dst_ref=dst.at[k - 1], send_sem=send, recv_sem=recv,
            device_id={axis: d}, device_id_type=MESH,
        ).start()
        return carry

    lax.fori_loop(1, count, one, 0)


def gather(axis, count, piece, send, recv):
    me = lax.axis_index(axis)

    def one(k, carry):
        pltpu.make_async_remote_copy(
            src_ref=piece, dst_ref=piece, send_sem=send, recv_sem=recv,
            device_id={axis: lax.rem(me + k, count)}, device_id_type=MESH,
        ).start()
        return carry

    lax.fori_loop(1, count, one, 0)


def spread(axis, count, src, dst, send, recv):
    me = lax.axis_index(axis)

    def one(k, carry):
        pltpu.make_async_remote_copy(
            src_ref=src, dst_ref=dst.at[k - 1], send_sem=send, recv_sem=recv,
            device_id={axis: lax.rem(me + k, count)}, device_id_type=MESH,
        ).start()
        return carry

    lax.fori_loop(1, count, one, 0)


def kernel_a(
    pos, cnt, x_hbm, b_ref, c_ref,
    gb_out, m16_out, ms_out, g_out,
    x_v, x_sem, br, w_v, acc,
    gram, gb_part, gb_recv, gb_col, gb_full,
    part, pair_recv, half, m_recv, ms, g_piece, g_recv, g_full,
    send, recv,
):
    me_r, me_c = lax.axis_index("row"), lax.axis_index("col")
    chip, core = me_c // 2, lax.rem(me_c, 2)
    mate = chip * 2 + 1 - core

    def to_mate(src, dst, n):
        pltpu.make_async_remote_copy(
            src_ref=src, dst_ref=dst, send_sem=send.at[n], recv_sem=recv.at[n],
            device_id={"col": mate}, device_id_type=MESH,
        ).start()

    def x_copy(ch):
        cols = pl.ds(pl.multiple_of(ch * CHUNK, CHUNK), CHUNK)
        return pltpu.make_async_copy(x_hbm.at[:, cols], x_v.at[:, cols], x_sem.at[ch])

    for ch in range(NCH):
        x_copy(ch).start()
    barrier, partners = greet((("col", NCOL), ("row", NROW)))

    b = b_ref[...]
    gram[...] = dot_hi(b.T, b)
    rows = gram[pl.ds(pl.multiple_of(me_r * 32, 32), 32), :]
    for i in range(32):
        gb_part[i] = rows[i:i + 1, :]
    br[...] = b.astype(BF16).astype(F32)
    cr = c_ref[...].astype(BF16).astype(F32)
    acc[...] = jnp.zeros_like(acc)

    def mode_one(ch, carry):
        for jb in range(JBD):
            tile = br[pl.ds(pl.multiple_of(jb * BLK + ch * JPC, JPC), JPC), :]
            for j in range(JPC):
                w_v[j * K:(j + 1) * K, jb * R:(jb + 1) * R] = (tile[j:j + 1, :] * cr).astype(BF16)
        x_copy(ch).wait()
        x = x_v[:, pl.ds(pl.multiple_of(ch * CHUNK, CHUNK), CHUNK)]
        acc[...] += jnp.dot(x, w_v[...], preferred_element_type=F32)
        return carry

    lax.fori_loop(0, NCH - 3, mode_one, 0)
    pl.semaphore_wait(barrier, partners)
    scatter("col", NCOL, gb_part, gb_recv, send.at[0], recv.at[0])
    lax.fori_loop(NCH - 3, NCH, mode_one, 0)

    count = cnt[0, 0]
    for ib in range(IBD):
        total = jnp.zeros((BLK, R), F32)
        for s in range(SLOTS):
            p = pos[0, s]
            live = jnp.where(count > s, 1.0, 0.0).astype(F32)
            for jb in range(JBD):
                keep = jnp.where(p == ib * JBD + jb, live, 0.0)
                total += acc[s * BLK:(s + 1) * BLK, jb * R:(jb + 1) * R] * keep
        for t in range(BLK // SHARE_A):
            at = ib * (BLK // SHARE_A) + t
            part[at % 2, at // 2] = total[t * SHARE_A:(t + 1) * SHARE_A, :]

    to_mate(part.at[1 - core], pair_recv, 1)
    wait_bytes(pair_recv, recv.at[1])
    half[...] = (part[core] + pair_recv[...]).astype(BF16)

    def to_chip(k, carry):
        d = lax.rem(chip + k, CHIPS)
        pltpu.make_async_remote_copy(
            src_ref=half.at[d], dst_ref=m_recv.at[k - 1], send_sem=send.at[2], recv_sem=recv.at[2],
            device_id={"col": d * 2 + core}, device_id_type=MESH,
        ).start()
        return carry

    lax.fori_loop(1, CHIPS, to_chip, 0)

    wait_bytes(gb_recv, recv.at[0])
    gb_col[me_c] = gb_part[me_c] + jnp.sum(gb_recv[...], axis=0)
    gather("col", NCOL, gb_col.at[me_c], send.at[3], recv.at[3])

    wait_bytes(m_recv, recv.at[2])
    m16 = part[core, chip] + pair_recv[chip] + jnp.sum(m_recv[...].astype(F32), axis=0)
    ms[core, chip] = m16.astype(BF16)

    def from_chip(k, carry):
        piece = ms.at[core, chip]
        pltpu.make_async_remote_copy(
            src_ref=piece, dst_ref=piece, send_sem=send.at[4], recv_sem=recv.at[4],
            device_id={"col": lax.rem(chip + k, CHIPS) * 2 + core}, device_id_type=MESH,
        ).start()
        return carry

    lax.fori_loop(1, CHIPS, from_chip, 0)
    m16_out[...] = m16

    wait_bytes(gb_col.at[pl.ds(0, NCOL - 1)], recv.at[3])
    for i in range(32):
        gb_full[me_r, i:i + 1, :] = gb_col[i]
    gather("row", NROW, gb_full.at[me_r], send.at[5], recv.at[5])

    wait_bytes(m_recv, recv.at[4])
    to_mate(ms.at[core], ms.at[core], 6)
    wait_bytes(ms.at[0], recv.at[6])

    slab = ms[...].reshape(SLAB_A, R)
    gram[...] = jnp.dot(slab.T, slab, preferred_element_type=F32)
    g_piece[...] = gram[pl.ds(pl.multiple_of(core * BLK, BLK), BLK), :].reshape(NROW, SHARE_G, R)
    scatter("row", NROW, g_piece, g_recv, send.at[7], recv.at[7])
    for at in range(NCOL):
        ms_out[at * SHARE_A:(at + 1) * SHARE_A, :] = ms[at % 2, at // 2]
    wait_bytes(g_recv, recv.at[7])
    g_full[core, me_r] = g_piece[me_r] + jnp.sum(g_recv[...], axis=0)
    gather("row", NROW, g_full.at[core, me_r], send.at[8], recv.at[8])
    wait_bytes(gb_full.at[pl.ds(0, NROW - 1)], recv.at[5])
    gb_out[...] = gb_full[...].reshape(R, R)
    wait_bytes(g_recv, recv.at[8])
    to_mate(g_full.at[core], g_full.at[core], 9)
    wait_bytes(g_full.at[0], recv.at[9])
    g_out[...] = g_full[...].reshape(R, R)

    wait_bytes(gb_recv, send.at[0])
    wait_bytes(pair_recv, send.at[1])
    wait_bytes(m_recv, send.at[2])
    wait_bytes(gb_col.at[pl.ds(0, NCOL - 1)], send.at[3])
    wait_bytes(m_recv, send.at[4])
    wait_bytes(gb_full.at[pl.ds(0, NROW - 1)], send.at[5])
    wait_bytes(ms.at[0], send.at[6])
    wait_bytes(g_recv, send.at[7])
    wait_bytes(g_recv, send.at[8])
    wait_bytes(g_full.at[0], send.at[9])


def eye():
    return lax.broadcasted_iota(jnp.int32, (R, R), 0) == lax.broadcasted_iota(jnp.int32, (R, R), 1)


def diagonals(v):
    only = jnp.where(eye(), v, 0.0)
    return jnp.sum(only, axis=1, keepdims=True), jnp.sum(only, axis=0, keepdims=True)


def inverse(v, x_ref, r_ref, c_ref):
    down, across = diagonals(v)
    down, across = 1.0 / jnp.sqrt(down), 1.0 / jnp.sqrt(across)
    unit = jnp.where(eye(), 1.0, 0.0)
    c = v * down * across
    c_ref[...] = c
    norm = jnp.max(jnp.sum(jnp.abs(c), axis=1, keepdims=True))
    alpha = jnp.where(norm < 1.9, 1.0, 1.0 / norm)
    res = unit - alpha * c
    x_ref[...] = alpha * (unit + res)
    res = unit - dot_hi(c, x_ref[...])
    r_ref[...] = res

    def more(state):
        it, size, before = state
        return (it < MAX_IT) & (size > 1e-5) & ((size > 1e-3) | (size < 0.5 * before))

    def step(state):
        it, size, _ = state
        x = x_ref[...]
        x = x + dot_hi(x, r_ref[...])
        x_ref[...] = x
        res = unit - dot_hi(c_ref[...], x)
        r_ref[...] = res
        return it + 1, jnp.max(jnp.abs(res)), size

    lax.while_loop(more, step, (0, jnp.max(jnp.abs(res)), jnp.float32(1e30)))
    x = x_ref[...]
    x = x + dot_hi(x, r_ref[...])
    return x * down * across


def kernel_b(
    pos, cnt, c_ref, gb_ref, m16_ref, ms_ref, g_ref,
    a_out, lhs_out, inv_out,
    x1, r1, c1, slab,
):
    c = c_ref[...]
    gram_c = dot_hi(c.T, c)
    inv1 = inverse(gb_ref[...] * gram_c, x1, r1, c1)
    gram_a = dot_hi(dot_hi(inv1, g_ref[...]), inv1)
    down, across = diagonals(gram_a)
    down = 1.0 / jnp.sqrt(down / ROWS_A + EPS)
    across = 1.0 / jnp.sqrt(across / ROWS_A + EPS)
    a_out[...] = dot_hi(m16_ref[...], inv1) * across
    slab[...] = dot_hi(ms_ref[...].astype(F32), inv1) * across

    inv_out[...] = inverse(gram_a * down * across * gram_c, x1, r1, c1)

    count = cnt[0, 0]
    for s in range(SLOTS):
        p = pos[0, s]
        tile = slab[pl.ds(pl.multiple_of(lax.shift_right_logical(p, 1) * BLK, BLK), BLK), :].T
        for jb in range(JBD):
            keep = jnp.where((count > s) & ((p & 1) == jb), 1.0, 0.0)
            lhs_out[jb * R:(jb + 1) * R, s * BLK:(s + 1) * BLK] = (tile * keep).astype(BF16)


def kernel_c(
    x_hbm, c_ref, lhs, inv_ref,
    b_out,
    x_v, x_sem, ct, acc, pb, pb_recv, sq_piece, sq_row, sq_all, sq_col, send, recv,
):
    me_r = lax.axis_index("row")

    def x_copy(ch):
        cols = pl.ds(pl.multiple_of(ch * CHUNK, CHUNK), CHUNK)
        return pltpu.make_async_copy(x_hbm.at[:, cols], x_v.at[:, cols], x_sem.at[ch])

    for ch in range(NCH):
        x_copy(ch).start()
    barrier, partners = greet((("row", NROW), ("col", NCOL)))
    c_low = c_ref[...].astype(BF16).astype(F32).T
    for jb in range(JBD):
        for t in range(CHUNK // K):
            ct[jb * R:(jb + 1) * R, t * K:(t + 1) * K] = c_low
    acc[...] = jnp.zeros_like(acc)

    def mode_two(ch, carry):
        x_copy(ch).wait()
        x = x_v[:, pl.ds(pl.multiple_of(ch * CHUNK, CHUNK), CHUNK)]
        t = jnp.dot(lhs[...], x, preferred_element_type=F32)
        t = (t * ct[...]).astype(BF16)
        j = lax.shift_right_logical(lax.broadcasted_iota(jnp.int32, (CHUNK, BLK), 0), 6) + ch * JPC
        ones = jnp.where(j == lax.broadcasted_iota(jnp.int32, (CHUNK, BLK), 1), 1.0, 0.0).astype(BF16)
        acc[...] += jnp.dot(t, ones, preferred_element_type=F32)
        return carry

    lax.fori_loop(0, NCH, mode_two, 0)
    for jb in range(JBD):
        rows = acc[jb * R:(jb + 1) * R, :].T.astype(BF16)
        for t in range(BLK // SHARE_B):
            pb[jb * (BLK // SHARE_B) + t] = rows[t * SHARE_B:(t + 1) * SHARE_B, :]

    pl.semaphore_wait(barrier, partners)
    scatter("row", NROW, pb, pb_recv, send.at[0], recv.at[0])
    wait_bytes(pb_recv, recv.at[0])
    m2 = pb[me_r].astype(F32) + jnp.sum(pb_recv[...].astype(F32), axis=0)
    raw = dot_hi(m2, inv_ref[...])
    sq_piece[...] = jnp.sum(raw * raw, axis=0, keepdims=True)
    spread("row", NROW, sq_piece, sq_row, send.at[1], recv.at[1])
    wait_bytes(sq_row, recv.at[1])
    sq_all[...] = sq_piece[...] + jnp.sum(sq_row[...], axis=0)
    spread("col", NCOL, sq_all, sq_col, send.at[2], recv.at[2])
    wait_bytes(sq_col, recv.at[2])
    squares = sq_all[...] + jnp.sum(sq_col[...], axis=0)
    b_out[...] = raw / jnp.sqrt(squares / ROWS_B + EPS)
    wait_bytes(pb_recv, send.at[0])
    wait_bytes(sq_row, send.at[1])
    wait_bytes(sq_col, send.at[2])


def low_dot(a, b):
    return jnp.dot(a.astype(BF16), b.astype(BF16), preferred_element_type=F32)


def dot_three(a, b):
    a_top, b_top = a.astype(BF16), b.astype(BF16)
    a_rest, b_rest = (a - a_top.astype(F32)).astype(BF16), (b - b_top.astype(F32)).astype(BF16)
    cross = jnp.dot(a_top, b_rest, preferred_element_type=F32) + jnp.dot(a_rest, b_top, preferred_element_type=F32)
    return jnp.dot(a_top, b_top, preferred_element_type=F32) + cross


def first_half(v):
    down, across = diagonals(v)
    down, across = 1.0 / jnp.sqrt(down), 1.0 / jnp.sqrt(across)
    unit = jnp.where(eye(), 1.0, 0.0)
    c = v * down * across
    norm = jnp.max(jnp.sum(jnp.abs(c), axis=0, keepdims=True), axis=1, keepdims=True)
    alpha = jnp.where(norm < 1.9, 1.0, 1.0 / norm)
    res = unit - alpha * c
    x = alpha * (unit + res)
    x = x + low_dot(x, low_dot(res, res))
    return c, x, down, across


def second_half(c, x, down, across):
    unit = jnp.where(eye(), 1.0, 0.0)
    x = x + low_dot(x, unit - dot_three(c, x))
    res = unit - dot_hi(c, x)
    worst = jnp.max(jnp.sum(jnp.abs(res), axis=0, keepdims=True), axis=1, keepdims=True)
    x = x + low_dot(x, res)
    return x * down * across, worst


def kernel_m(
    pos, cnt, x_hbm, b_ref, c_ref,
    a_out, b_out, worst_out,
    x_v, x_sem, br, w_even, w_odd, acc,
    gram, gb_part, gb_recv, gb_col, gb_full,
    part, pair_recv, half, m_recv, ms, m16, g_piece, g_recv, g_full,
    gram_c, inv1, slab, turned, lhs, ct, ones,
    pb, pb_recv, sq_piece, sq_row, sq_all, sq_col,
    send, recv,
):
    me_r, me_c = lax.axis_index("row"), lax.axis_index("col")
    chip, core = me_c // 2, lax.rem(me_c, 2)
    mate = chip * 2 + 1 - core

    def to_mate(src, dst, n):
        pltpu.make_async_remote_copy(
            src_ref=src, dst_ref=dst, send_sem=send.at[n], recv_sem=recv.at[n],
            device_id={"col": mate}, device_id_type=MESH,
        ).start()

    def chunk(ch):
        return pl.ds(pl.multiple_of(ch * CHUNK, CHUNK), CHUNK)

    def x_copy(ch):
        return pltpu.make_async_copy(x_hbm.at[:, chunk(ch)], x_v.at[:, chunk(ch)], x_sem.at[ch])

    for ch in range(NCH):
        x_copy(ch).start()
    barrier, partners = greet((("col", NCOL),))

    def in_plane(k):
        at = lax.rem(me_r * 4 + lax.rem(me_c, 4) + k, PLANE)
        return at // 4, me_c // 4 * 4 + lax.rem(at, 4)

    def greet_plane(k, carry):
        row, col = in_plane(k)
        pl.semaphore_signal(barrier, inc=1, device_id={"row": row, "col": col}, device_id_type=MESH)
        return carry

    lax.fori_loop(1, PLANE, greet_plane, 0)
    partners += PLANE - 1

    b = b_ref[...]
    gram[...] = dot_hi(b.T, b)
    rows = gram[pl.ds(pl.multiple_of(me_r * 32, 32), 32), :]
    for i in range(32):
        gb_part[i] = rows[i:i + 1, :]
    br[...] = b.astype(BF16).astype(F32)
    cr = c_ref[...].astype(BF16).astype(F32)
    acc[...] = jnp.zeros_like(acc)

    cb = cr.astype(BF16)

    def build(ch, w):
        for jb in range(JBD):
            tile = br[pl.ds(pl.multiple_of(jb * BLK + ch * JPC, JPC), JPC), :]
            for j in range(JPC):
                w[jb, j * K:(j + 1) * K, :] = jnp.broadcast_to(tile[j:j + 1, :].astype(BF16), (K, R)) * cb

    def add(ch, w):
        x_copy(ch).wait()
        for s in range(SLOTS):
            rows = slice(s * BLK, (s + 1) * BLK)
            acc[rows, :] += jnp.dot(x_v[rows, chunk(ch)], w[pos[0, s] & 1], preferred_element_type=F32)

    def mode_one(pair, carry):
        add(2 * pair, w_even)
        build(2 * pair + 1, w_odd)
        add(2 * pair + 1, w_odd)
        build(lax.rem(2 * pair + 2, NCH), w_even)
        return carry

    build(0, w_even)
    lax.fori_loop(0, NCH // 2 - 1, mode_one, 0)
    pl.semaphore_wait(barrier, partners)
    scatter("col", NCOL, gb_part, gb_recv, send.at[0], recv.at[0])
    lax.fori_loop(NCH // 2 - 1, NCH // 2, mode_one, 0)

    count = cnt[0, 0]
    for ib in range(IBD):
        total = jnp.zeros((BLK, R), F32)
        for s in range(SLOTS):
            live = jnp.where(count > s, 1.0, 0.0).astype(F32)
            keep = jnp.where(lax.shift_right_logical(pos[0, s], 1) == ib, live, 0.0)
            total += acc[s * BLK:(s + 1) * BLK, :] * keep
        for t in range(BLK // SHARE_A):
            at = ib * (BLK // SHARE_A) + t
            for side in range(2):
                part[side, at % 2, at // 2] = total[t * SHARE_A:(t + 1) * SHARE_A, side * BLK:(side + 1) * BLK]

    for side in range(2):
        to_mate(part.at[side, 1 - core], pair_recv.at[side], (1, 14)[side])
    c = c_ref[...]
    gram_c[...] = dot_hi(c.T, c)

    def to_chip(side, k, carry):
        d = lax.rem(chip + k, CHIPS)
        n = (2, 15)[side]
        pltpu.make_async_remote_copy(
            src_ref=half.at[side, d], dst_ref=m_recv.at[side, k - 1], send_sem=send.at[n], recv_sem=recv.at[n],
            device_id={"col": d * 2 + core}, device_id_type=MESH,
        ).start()
        return carry

    for side in range(2):
        wait_bytes(pair_recv.at[side], recv.at[(1, 14)[side]])
        half[side] = (part[side, core] + pair_recv[side]).astype(BF16)
        lax.fori_loop(1, CHIPS, functools.partial(to_chip, side), 0)

    wait_bytes(gb_recv, recv.at[0])
    gb_col[me_c] = gb_part[me_c] + jnp.sum(gb_recv[...], axis=0)
    gather("col", NCOL, gb_col.at[me_c], send.at[3], recv.at[3])
    c_low = cr.T
    for jb in range(JBD):
        for t in range(CHUNK // K):
            ct[jb * R:(jb + 1) * R, t * K:(t + 1) * K] = c_low
    whose = lax.shift_right_logical(lax.broadcasted_iota(jnp.int32, (JPC, CHUNK), 1), 6)
    ones[...] = jnp.where(whose == lax.broadcasted_iota(jnp.int32, (JPC, CHUNK), 0), 1.0, 0.0).astype(BF16)

    def from_chip(side, k, carry):
        piece = ms.at[side, core, chip]
        n = (4, 16)[side]
        pltpu.make_async_remote_copy(
            src_ref=piece, dst_ref=piece, send_sem=send.at[n], recv_sem=recv.at[n],
            device_id={"col": lax.rem(chip + k, CHIPS) * 2 + core}, device_id_type=MESH,
        ).start()
        return carry

    def pass_on(side):
        wait_bytes(m_recv.at[side], recv.at[(2, 15)[side]])
        mine = part[side, core, chip] + pair_recv[side, chip] + jnp.sum(m_recv[side].astype(F32), axis=0)
        ms[side, core, chip] = mine.astype(BF16)
        lax.fori_loop(1, CHIPS, functools.partial(from_chip, side), 0)
        m16[:, side * BLK:(side + 1) * BLK] = mine

    pass_on(0)
    wait_bytes(gb_col.at[pl.ds(0, NCOL - 1)], recv.at[3])
    for i in range(16):
        gb_full[core, me_r, i:i + 1, :] = gb_col[core * 16 + i]
    gather("row", NROW, gb_full.at[core, me_r], send.at[5], recv.at[5])
    pass_on(1)

    wait_bytes(gb_full.at[0, pl.ds(0, NROW - 1)], recv.at[5])
    to_mate(gb_full.at[core], gb_full.at[core], 13)
    wait_bytes(gb_full.at[0], recv.at[13])
    for at in range(R // 16):
        gram[at * 16:(at + 1) * 16, :] = gb_full[at % 2, at // 2]
    c_one, x_one, down_one, across_one = first_half(gram[...] * gram_c[...])
    turned[:, :R] = c_one
    turned[:, R:] = x_one

    for side in range(2):
        wait_bytes(m_recv.at[side], recv.at[(4, 16)[side]])
        to_mate(ms.at[side, core], ms.at[side, core], (6, 17)[side])
    for side in range(2):
        wait_bytes(ms.at[side, 0], recv.at[(6, 17)[side]])
        for at in range(NCOL):
            slab[at * SHARE_A:(at + 1) * SHARE_A, side * BLK:(side + 1) * BLK] = ms[side, at % 2, at // 2]

    gram[...] = jnp.dot(slab[...].T, slab[...], preferred_element_type=F32)
    own = jnp.where(core == 0, gram[:BLK, :BLK], gram[BLK:, BLK:])
    cross = gram[pl.ds(pl.multiple_of(core * (BLK // 2), BLK // 2), BLK // 2), BLK:]
    g_piece[:, :SHARE_G, :] = own.reshape(NROW, SHARE_G, BLK)
    g_piece[:, SHARE_G:, :] = cross.reshape(NROW, SHARE_G // 2, BLK)
    scatter("row", NROW, g_piece, g_recv, send.at[7], recv.at[7])

    solved, worst_one = second_half(turned[:, :R], turned[:, R:], down_one, across_one)
    inv1[...] = solved
    top = inv1[...].astype(BF16)
    rest = (inv1[...] - top.astype(F32)).astype(BF16)
    last = (((1,), (1,)), ((), ()))
    turned[...] = lax.dot_general(top, slab[...], last, preferred_element_type=F32) + lax.dot_general(
        rest, slab[...], last, preferred_element_type=F32
    )
    for s in range(SLOTS):
        p = pos[0, s]
        live = jnp.where(count > s, 1.0, 0.0).astype(F32)
        for jb in range(JBD):
            tile = jnp.zeros((R, BLK), F32)
            for ib in range(IBD):
                tile += turned[:, ib * BLK:(ib + 1) * BLK] * jnp.where(p == ib * JBD + jb, live, 0.0)
            lhs[jb * R:(jb + 1) * R, s * BLK:(s + 1) * BLK] = tile.astype(BF16)

    def mode_two(group, carry):
        for side in range(2):
            ch = 2 * group + side
            t = jnp.dot(lhs[...], x_v[:, chunk(ch)], preferred_element_type=F32)
            t = (t * ct[...]).astype(BF16)
            rows = lax.dot_general(ones[...], t, last, preferred_element_type=F32).astype(BF16)
            for jb in range(JBD):
                pb[jb * (NROW // 2) + group, side * JPC:(side + 1) * JPC, :] = rows[:, jb * R:(jb + 1) * R]
        for jb in range(JBD):
            to = jb * (NROW // 2) + group

            @pl.when(to != me_r)
            def _():
                pltpu.make_async_remote_copy(
                    src_ref=pb.at[to], dst_ref=pb_recv.at[lax.rem(to - me_r + NROW, NROW) - 1],
                    send_sem=send.at[10], recv_sem=recv.at[10],
                    device_id={"row": to}, device_id_type=MESH,
                ).start()

        return carry

    lax.fori_loop(0, 2, mode_two, 0)
    wait_bytes(g_recv, recv.at[7])
    g_full[core, me_r] = g_piece[me_r] + jnp.sum(g_recv[...], axis=0)
    gather("row", NROW, g_full.at[core, me_r], send.at[8], recv.at[8])
    lax.fori_loop(2, 4, mode_two, 0)
    wait_bytes(g_recv, recv.at[8])
    to_mate(g_full.at[core], g_full.at[core], 9)

    wait_bytes(g_full.at[0], recv.at[9])
    solved = inv1[...]
    for e in range(2):
        gram[e * BLK:(e + 1) * BLK, e * BLK:(e + 1) * BLK] = g_full[e, :, :SHARE_G, :].reshape(BLK, BLK)
        cross = g_full[e, :, SHARE_G:, :].reshape(BLK // 2, BLK)
        gram[e * (BLK // 2):(e + 1) * (BLK // 2), BLK:] = cross
    gram[BLK:, :BLK] = gram[:BLK, BLK:].T
    gram_a = dot_three(dot_three(solved, gram[...]), solved)
    down, across = diagonals(gram_a)
    down = 1.0 / jnp.sqrt(down / ROWS_A + EPS)
    across = 1.0 / jnp.sqrt(across / ROWS_A + EPS)
    a_out[...] = dot_three(m16[...], solved) * across
    inv2, worst_two = second_half(*first_half(gram_a * down * across * gram_c[...]))
    worst_out[...] = jnp.maximum(worst_one, worst_two)

    wait_bytes(pb_recv, recv.at[10])
    m2 = (pb[me_r].astype(F32) + jnp.sum(pb_recv[...].astype(F32), axis=0)) * across
    raw = dot_hi(m2, inv2)
    sq_piece[...] = jnp.sum(raw * raw, axis=0, keepdims=True)

    def to_plane(k, carry):
        row, col = in_plane(k)
        pltpu.make_async_remote_copy(
            src_ref=sq_piece, dst_ref=sq_col.at[k - 1], send_sem=send.at[11], recv_sem=recv.at[11],
            device_id={"row": row, "col": col}, device_id_type=MESH,
        ).start()
        return carry

    lax.fori_loop(1, PLANE, to_plane, 0)
    wait_bytes(sq_col, recv.at[11])
    sq_all[...] = sq_piece[...] + jnp.sum(sq_col[...], axis=0)

    def to_planes(k, carry):
        pltpu.make_async_remote_copy(
            src_ref=sq_all, dst_ref=sq_row.at[k - 1], send_sem=send.at[12], recv_sem=recv.at[12],
            device_id={"col": lax.rem(me_c + k * 4, NCOL)}, device_id_type=MESH,
        ).start()
        return carry

    lax.fori_loop(1, NCOL // 4, to_planes, 0)
    wait_bytes(gb_recv, send.at[0])
    for side in range(2):
        wait_bytes(pair_recv.at[side], send.at[(1, 14)[side]])
        wait_bytes(m_recv.at[side], send.at[(2, 15)[side]])
        wait_bytes(m_recv.at[side], send.at[(4, 16)[side]])
        wait_bytes(ms.at[side, 0], send.at[(6, 17)[side]])
    wait_bytes(gb_col.at[pl.ds(0, NCOL - 1)], send.at[3])
    wait_bytes(gb_full.at[0, pl.ds(0, NROW - 1)], send.at[5])
    wait_bytes(gb_full.at[0], send.at[13])
    wait_bytes(g_recv, send.at[7])
    wait_bytes(g_recv, send.at[8])
    wait_bytes(g_full.at[0], send.at[9])
    wait_bytes(pb_recv, send.at[10])
    wait_bytes(sq_col, send.at[11])
    wait_bytes(sq_row, recv.at[12])
    squares = sq_all[...] + jnp.sum(sq_row[...], axis=0)
    b_out[...] = raw / jnp.sqrt(squares / ROWS_B + EPS)
    wait_bytes(sq_row, send.at[12])


VM = pl.BlockSpec(memory_space=pltpu.VMEM)
SM = pl.BlockSpec(memory_space=pltpu.SMEM)
ANY = pl.BlockSpec(memory_space=pl.ANY)


def shape(dims, kind=F32):
    return jax.ShapeDtypeStruct(dims, kind)


def three_kernels(place, block_count, flat, factor_b, factor_c):
    vm, dma = pltpu.VMEM, pltpu.SemaphoreType.DMA
    gram_b, m16, ms, g = pl.pallas_call(
        kernel_a,
        name="mode_one",
        out_shape=(shape((R, R)), shape((SHARE_A, R)), shape((SLAB_A, R), BF16), shape((R, R))),
        in_specs=[SM, SM, ANY, VM, VM],
        out_specs=[VM] * 4,
        scratch_shapes=[
            vm((SLAB_A, WIDE), BF16), dma((NCH,)), vm((R, R), F32), vm((CHUNK, JBD * R), BF16), vm((SLAB_A, JBD * R), F32),
            vm((R, R), F32), vm((NCOL, 1, R), F32), vm((NCOL - 1, 1, R), F32), vm((NCOL, 1, R), F32), vm((NROW, 32, R), F32),
            vm((2, CHIPS, SHARE_A, R), F32), vm((CHIPS, SHARE_A, R), F32), vm((CHIPS, SHARE_A, R), BF16),
            vm((CHIPS - 1, SHARE_A, R), BF16), vm((2, CHIPS, SHARE_A, R), BF16),
            vm((NROW, SHARE_G, R), F32), vm((NROW - 1, SHARE_G, R), F32), vm((2, NROW, SHARE_G, R), F32),
            dma((10,)), dma((10,)),
        ],
        compiler_params=pltpu.CompilerParams(collective_id=1, has_side_effects=True),
    )(place, block_count, flat, factor_b, factor_c)
    hat_a, lhs, inv = pl.pallas_call(
        kernel_b,
        name="solve_two",
        out_shape=(shape((SHARE_A, R)), shape((JBD * R, SLAB_A), BF16), shape((R, R))),
        in_specs=[SM, SM, VM, VM, VM, VM, VM],
        out_specs=[VM] * 3,
        scratch_shapes=[vm((R, R), F32), vm((R, R), F32), vm((R, R), F32), vm((SLAB_A, R), F32)],
    )(place, block_count, factor_c, gram_b, m16, ms, g)
    hat_b = pl.pallas_call(
        kernel_c,
        name="mode_two",
        out_shape=shape((SHARE_B, R)),
        in_specs=[ANY, VM, VM, VM],
        out_specs=VM,
        scratch_shapes=[
            vm((SLAB_A, WIDE), BF16), dma((NCH,)), vm((JBD * R, CHUNK), F32), vm((JBD * R, BLK), F32),
            vm((NROW, SHARE_B, R), BF16), vm((NROW - 1, SHARE_B, R), BF16),
            vm((1, R), F32), vm((NROW - 1, 1, R), F32), vm((1, R), F32), vm((NCOL - 1, 1, R), F32),
            dma((3,)), dma((3,)),
        ],
        compiler_params=pltpu.CompilerParams(collective_id=2, has_side_effects=True),
    )(flat, factor_c, lhs, inv)
    return hat_a, hat_b


def body(blocks, factor_b, factor_c, block_pos, block_count):
    args = (block_pos.T, block_count, blocks.reshape(SLOTS * BLK, WIDE), factor_b, factor_c)
    vm, dma = pltpu.VMEM, pltpu.SemaphoreType.DMA
    hat_a, hat_b, worst = pl.pallas_call(
        kernel_m,
        name="sweep",
        out_shape=(shape((SHARE_A, R)), shape((SHARE_B, R)), shape((1, 1))),
        in_specs=[SM, SM, ANY, VM, VM],
        out_specs=[VM] * 3,
        scratch_shapes=[
            vm((SLAB_A, WIDE), BF16), dma((NCH,)), vm((R, R), F32), vm((JBD, CHUNK, R), BF16),
            vm((JBD, CHUNK, R), BF16), vm((SLAB_A, R), F32),
            vm((R, R), F32), vm((NCOL, 1, R), F32), vm((NCOL - 1, 1, R), F32), vm((NCOL, 1, R), F32), vm((2, NROW, 16, R), F32),
            vm((2, 2, CHIPS, SHARE_A, BLK), F32), vm((2, CHIPS, SHARE_A, BLK), F32), vm((2, CHIPS, SHARE_A, BLK), BF16),
            vm((2, CHIPS - 1, SHARE_A, BLK), BF16), vm((2, 2, CHIPS, SHARE_A, BLK), BF16), vm((SHARE_A, R), F32),
            vm((NROW, PIECE_G, BLK), F32), vm((NROW - 1, PIECE_G, BLK), F32), vm((2, NROW, PIECE_G, BLK), F32),
            vm((R, R), F32), vm((R, R), F32), vm((SLAB_A, R), BF16), vm((R, SLAB_A), F32), vm((JBD * R, SLAB_A), BF16),
            vm((JBD * R, CHUNK), F32), vm((JPC, CHUNK), BF16),
            vm((NROW, SHARE_B, R), BF16), vm((NROW - 1, SHARE_B, R), BF16),
            vm((1, R), F32), vm((NROW - 1, 1, R), F32), vm((1, R), F32), vm((NCOL - 1, 1, R), F32),
            dma((18,)), dma((18,)),
        ],
        compiler_params=pltpu.CompilerParams(collective_id=0, has_side_effects=True),
    )(*args)
    return lax.cond(worst[0, 0] <= 1e-3, lambda: (hat_a, hat_b), lambda: three_kernels(*args))


def solution(mesh):
    return jax.shard_map(
        body,
        mesh=mesh,
        in_specs=(P("row", "col", None), P("col", None), P(), P("row", "col"), P("row", "col")),
        out_specs=(P(("row", "col"), None), P(("col", "row"), None)),
        check_vma=False,
    )
```

```python
import functools

import jax
import jax.numpy as jnp
from jax import lax
from jax.experimental import pallas as pl
from jax.experimental.pallas import tpu as pltpu
from jax.sharding import PartitionSpec as P

MESH = pl.DeviceIdType.MESH
HIGH = lax.Precision.HIGHEST
F32 = jnp.float32
BF16 = jnp.bfloat16
NROW, NCOL = 8, 32
R, K, BLK, SLOTS, IBD, JBD = 256, 64, 128, 4, 4, 2
SLAB_A = IBD * BLK
SLAB_B = JBD * BLK
WIDE = BLK * K
CHUNK = 1024
NCH = WIDE // CHUNK
JPC = CHUNK // K
SHARE_A = SLAB_A // NCOL
SHARE_B = SLAB_B // NROW
CHIPS = NCOL // 2
SHARE_G = BLK // NROW
PLANE = NROW * 4
PIECE_G = SHARE_G * 3 // 2
ROWS_A = SLAB_A * NROW
ROWS_B = SLAB_B * NCOL
EPS = 1e-06
MAX_IT = 80


def dot_hi(a, b):
    return jnp.dot(a, b, precision=HIGH, preferred_element_type=F32)


def wait_bytes(ref, sem):
    pltpu.make_async_copy(ref, ref, sem).wait()


def greet(axes):
    barrier = pltpu.get_barrier_semaphore()
    total = 0
    for axis, count in axes:
        me = lax.axis_index(axis)

        def one(k, carry, axis=axis, count=count, me=me):
            pl.semaphore_signal(
                barrier, inc=1, device_id={axis: lax.rem(me + k, count)}, device_id_type=MESH
            )
            return carry

        lax.fori_loop(1, count, one, 0)
        total += count - 1
    return barrier, total


def scatter(axis, count, src, dst, send, recv):
    me = lax.axis_index(axis)

    def one(k, carry):
        d = lax.rem(me + k, count)
        pltpu.make_async_remote_copy(
            src_ref=src.at[d], dst_ref=dst.at[k - 1], send_sem=send, recv_sem=recv,
            device_id={axis: d}, device_id_type=MESH,
        ).start()
        return carry

    lax.fori_loop(1, count, one, 0)


def gather(axis, count, piece, send, recv):
    me = lax.axis_index(axis)

    def one(k, carry):
        pltpu.make_async_remote_copy(
            src_ref=piece, dst_ref=piece, send_sem=send, recv_sem=recv,
            device_id={axis: lax.rem(me + k, count)}, device_id_type=MESH,
        ).start()
        return carry

    lax.fori_loop(1, count, one, 0)


def spread(axis, count, src, dst, send, recv):
    me = lax.axis_index(axis)

    def one(k, carry):
        pltpu.make_async_remote_copy(
            src_ref=src, dst_ref=dst.at[k - 1], send_sem=send, recv_sem=recv,
            device_id={axis: lax.rem(me + k, count)}, device_id_type=MESH,
        ).start()
        return carry

    lax.fori_loop(1, count, one, 0)


def kernel_a(
    pos, cnt, x_hbm, b_ref, c_ref,
    gb_out, m16_out, ms_out, g_out,
    x_v, x_sem, br, w_v, acc,
    gram, gb_part, gb_recv, gb_col, gb_full,
    part, pair_recv, half, m_recv, ms, g_piece, g_recv, g_full,
    send, recv,
):
    me_r, me_c = lax.axis_index("row"), lax.axis_index("col")
    chip, core = me_c // 2, lax.rem(me_c, 2)
    mate = chip * 2 + 1 - core

    def to_mate(src, dst, n):
        pltpu.make_async_remote_copy(
            src_ref=src, dst_ref=dst, send_sem=send.at[n], recv_sem=recv.at[n],
            device_id={"col": mate}, device_id_type=MESH,
        ).start()

    def x_copy(ch):
        cols = pl.ds(pl.multiple_of(ch * CHUNK, CHUNK), CHUNK)
        return pltpu.make_async_copy(x_hbm.at[:, cols], x_v.at[:, cols], x_sem.at[ch])

    for ch in range(NCH):
        x_copy(ch).start()
    barrier, partners = greet((("col", NCOL), ("row", NROW)))

    b = b_ref[...]
    gram[...] = dot_hi(b.T, b)
    rows = gram[pl.ds(pl.multiple_of(me_r * 32, 32), 32), :]
    for i in range(32):
        gb_part[i] = rows[i:i + 1, :]
    br[...] = b.astype(BF16).astype(F32)
    cr = c_ref[...].astype(BF16).astype(F32)
    acc[...] = jnp.zeros_like(acc)

    def mode_one(ch, carry):
        for jb in range(JBD):
            tile = br[pl.ds(pl.multiple_of(jb * BLK + ch * JPC, JPC), JPC), :]
            for j in range(JPC):
                w_v[j * K:(j + 1) * K, jb * R:(jb + 1) * R] = (tile[j:j + 1, :] * cr).astype(BF16)
        x_copy(ch).wait()
        x = x_v[:, pl.ds(pl.multiple_of(ch * CHUNK, CHUNK), CHUNK)]
        acc[...] += jnp.dot(x, w_v[...], preferred_element_type=F32)
        return carry

    lax.fori_loop(0, NCH - 3, mode_one, 0)
    pl.semaphore_wait(barrier, partners)
    scatter("col", NCOL, gb_part, gb_recv, send.at[0], recv.at[0])
    lax.fori_loop(NCH - 3, NCH, mode_one, 0)

    count = cnt[0, 0]
    for ib in range(IBD):
        total = jnp.zeros((BLK, R), F32)
        for s in range(SLOTS):
            p = pos[0, s]
            live = jnp.where(count > s, 1.0, 0.0).astype(F32)
            for jb in range(JBD):
                keep = jnp.where(p == ib * JBD + jb, live, 0.0)
                total += acc[s * BLK:(s + 1) * BLK, jb * R:(jb + 1) * R] * keep
        for t in range(BLK // SHARE_A):
            at = ib * (BLK // SHARE_A) + t
            part[at % 2, at // 2] = total[t * SHARE_A:(t + 1) * SHARE_A, :]

    to_mate(part.at[1 - core], pair_recv, 1)
    wait_bytes(pair_recv, recv.at[1])
    half[...] = (part[core] + pair_recv[...]).astype(BF16)

    def to_chip(k, carry):
        d = lax.rem(chip + k, CHIPS)
        pltpu.make_async_remote_copy(
            src_ref=half.at[d], dst_ref=m_recv.at[k - 1], send_sem=send.at[2], recv_sem=recv.at[2],
            device_id={"col": d * 2 + core}, device_id_type=MESH,
        ).start()
        return carry

    lax.fori_loop(1, CHIPS, to_chip, 0)

    wait_bytes(gb_recv, recv.at[0])
    gb_col[me_c] = gb_part[me_c] + jnp.sum(gb_recv[...], axis=0)
    gather("col", NCOL, gb_col.at[me_c], send.at[3], recv.at[3])

    wait_bytes(m_recv, recv.at[2])
    m16 = part[core, chip] + pair_recv[chip] + jnp.sum(m_recv[...].astype(F32), axis=0)
    ms[core, chip] = m16.astype(BF16)

    def from_chip(k, carry):
        piece = ms.at[core, chip]
        pltpu.make_async_remote_copy(
            src_ref=piece, dst_ref=piece, send_sem=send.at[4], recv_sem=recv.at[4],
            device_id={"col": lax.rem(chip + k, CHIPS) * 2 + core}, device_id_type=MESH,
        ).start()
        return carry

    lax.fori_loop(1, CHIPS, from_chip, 0)
    m16_out[...] = m16

    wait_bytes(gb_col.at[pl.ds(0, NCOL - 1)], recv.at[3])
    for i in range(32):
        gb_full[me_r, i:i + 1, :] = gb_col[i]
    gather("row", NROW, gb_full.at[me_r], send.at[5], recv.at[5])

    wait_bytes(m_recv, recv.at[4])
    to_mate(ms.at[core], ms.at[core], 6)
    wait_bytes(ms.at[0], recv.at[6])

    slab = ms[...].reshape(SLAB_A, R)
    gram[...] = jnp.dot(slab.T, slab, preferred_element_type=F32)
    g_piece[...] = gram[pl.ds(pl.multiple_of(core * BLK, BLK), BLK), :].reshape(NROW, SHARE_G, R)
    scatter("row", NROW, g_piece, g_recv, send.at[7], recv.at[7])
    for at in range(NCOL):
        ms_out[at * SHARE_A:(at + 1) * SHARE_A, :] = ms[at % 2, at // 2]
    wait_bytes(g_recv, recv.at[7])
    g_full[core, me_r] = g_piece[me_r] + jnp.sum(g_recv[...], axis=0)
    gather("row", NROW, g_full.at[core, me_r], send.at[8], recv.at[8])
    wait_bytes(gb_full.at[pl.ds(0, NROW - 1)], recv.at[5])
    gb_out[...] = gb_full[...].reshape(R, R)
    wait_bytes(g_recv, recv.at[8])
    to_mate(g_full.at[core], g_full.at[core], 9)
    wait_bytes(g_full.at[0], recv.at[9])
    g_out[...] = g_full[...].reshape(R, R)

    wait_bytes(gb_recv, send.at[0])
    wait_bytes(pair_recv, send.at[1])
    wait_bytes(m_recv, send.at[2])
    wait_bytes(gb_col.at[pl.ds(0, NCOL - 1)], send.at[3])
    wait_bytes(m_recv, send.at[4])
    wait_bytes(gb_full.at[pl.ds(0, NROW - 1)], send.at[5])
    wait_bytes(ms.at[0], send.at[6])
    wait_bytes(g_recv, send.at[7])
    wait_bytes(g_recv, send.at[8])
    wait_bytes(g_full.at[0], send.at[9])


def eye():
    return lax.broadcasted_iota(jnp.int32, (R, R), 0) == lax.broadcasted_iota(jnp.int32, (R, R), 1)


def diagonals(v):
    only = jnp.where(eye(), v, 0.0)
    return jnp.sum(only, axis=1, keepdims=True), jnp.sum(only, axis=0, keepdims=True)


def inverse(v, x_ref, r_ref, c_ref):
    down, across = diagonals(v)
    down, across = 1.0 / jnp.sqrt(down), 1.0 / jnp.sqrt(across)
    unit = jnp.where(eye(), 1.0, 0.0)
    c = v * down * across
    c_ref[...] = c
    norm = jnp.max(jnp.sum(jnp.abs(c), axis=1, keepdims=True))
    alpha = jnp.where(norm < 1.9, 1.0, 1.0 / norm)
    res = unit - alpha * c
    x_ref[...] = alpha * (unit + res)
    res = unit - dot_hi(c, x_ref[...])
    r_ref[...] = res

    def more(state):
        it, size, before = state
        return (it < MAX_IT) & (size > 1e-5) & ((size > 1e-3) | (size < 0.5 * before))

    def step(state):
        it, size, _ = state
        x = x_ref[...]
        x = x + dot_hi(x, r_ref[...])
        x_ref[...] = x
        res = unit - dot_hi(c_ref[...], x)
        r_ref[...] = res
        return it + 1, jnp.max(jnp.abs(res)), size

    lax.while_loop(more, step, (0, jnp.max(jnp.abs(res)), jnp.float32(1e30)))
    x = x_ref[...]
    x = x + dot_hi(x, r_ref[...])
    return x * down * across


def kernel_b(
    pos, cnt, c_ref, gb_ref, m16_ref, ms_ref, g_ref,
    a_out, lhs_out, inv_out,
    x1, r1, c1, slab,
):
    c = c_ref[...]
    gram_c = dot_hi(c.T, c)
    inv1 = inverse(gb_ref[...] * gram_c, x1, r1, c1)
    gram_a = dot_hi(dot_hi(inv1, g_ref[...]), inv1)
    down, across = diagonals(gram_a)
    down = 1.0 / jnp.sqrt(down / ROWS_A + EPS)
    across = 1.0 / jnp.sqrt(across / ROWS_A + EPS)
    a_out[...] = dot_hi(m16_ref[...], inv1) * across
    slab[...] = dot_hi(ms_ref[...].astype(F32), inv1) * across

    inv_out[...] = inverse(gram_a * down * across * gram_c, x1, r1, c1)

    count = cnt[0, 0]
    for s in range(SLOTS):
        p = pos[0, s]
        tile = slab[pl.ds(pl.multiple_of(lax.shift_right_logical(p, 1) * BLK, BLK), BLK), :].T
        for jb in range(JBD):
            keep = jnp.where((count > s) & ((p & 1) == jb), 1.0, 0.0)
            lhs_out[jb * R:(jb + 1) * R, s * BLK:(s + 1) * BLK] = (tile * keep).astype(BF16)


def kernel_c(
    x_hbm, c_ref, lhs, inv_ref,
    b_out,
    x_v, x_sem, ct, acc, pb, pb_recv, sq_piece, sq_row, sq_all, sq_col, send, recv,
):
    me_r = lax.axis_index("row")

    def x_copy(ch):
        cols = pl.ds(pl.multiple_of(ch * CHUNK, CHUNK), CHUNK)
        return pltpu.make_async_copy(x_hbm.at[:, cols], x_v.at[:, cols], x_sem.at[ch])

    for ch in range(NCH):
        x_copy(ch).start()
    barrier, partners = greet((("row", NROW), ("col", NCOL)))
    c_low = c_ref[...].astype(BF16).astype(F32).T
    for jb in range(JBD):
        for t in range(CHUNK // K):
            ct[jb * R:(jb + 1) * R, t * K:(t + 1) * K] = c_low
    acc[...] = jnp.zeros_like(acc)

    def mode_two(ch, carry):
        x_copy(ch).wait()
        x = x_v[:, pl.ds(pl.multiple_of(ch * CHUNK, CHUNK), CHUNK)]
        t = jnp.dot(lhs[...], x, preferred_element_type=F32)
        t = (t * ct[...]).astype(BF16)
        j = lax.shift_right_logical(lax.broadcasted_iota(jnp.int32, (CHUNK, BLK), 0), 6) + ch * JPC
        ones = jnp.where(j == lax.broadcasted_iota(jnp.int32, (CHUNK, BLK), 1), 1.0, 0.0).astype(BF16)
        acc[...] += jnp.dot(t, ones, preferred_element_type=F32)
        return carry

    lax.fori_loop(0, NCH, mode_two, 0)
    for jb in range(JBD):
        rows = acc[jb * R:(jb + 1) * R, :].T.astype(BF16)
        for t in range(BLK // SHARE_B):
            pb[jb * (BLK // SHARE_B) + t] = rows[t * SHARE_B:(t + 1) * SHARE_B, :]

    pl.semaphore_wait(barrier, partners)
    scatter("row", NROW, pb, pb_recv, send.at[0], recv.at[0])
    wait_bytes(pb_recv, recv.at[0])
    m2 = pb[me_r].astype(F32) + jnp.sum(pb_recv[...].astype(F32), axis=0)
    raw = dot_hi(m2, inv_ref[...])
    sq_piece[...] = jnp.sum(raw * raw, axis=0, keepdims=True)
    spread("row", NROW, sq_piece, sq_row, send.at[1], recv.at[1])
    wait_bytes(sq_row, recv.at[1])
    sq_all[...] = sq_piece[...] + jnp.sum(sq_row[...], axis=0)
    spread("col", NCOL, sq_all, sq_col, send.at[2], recv.at[2])
    wait_bytes(sq_col, recv.at[2])
    squares = sq_all[...] + jnp.sum(sq_col[...], axis=0)
    b_out[...] = raw / jnp.sqrt(squares / ROWS_B + EPS)
    wait_bytes(pb_recv, send.at[0])
    wait_bytes(sq_row, send.at[1])
    wait_bytes(sq_col, send.at[2])


def far(n, count):
    return count // 2 + (1 - 2 * lax.rem(n, 2)) * ((n + 1) // 2)


def scatter_far(axis, count, src, dst, send, recv):
    me = lax.axis_index(axis)

    def one(n, carry):
        k = far(n, count)
        d = lax.rem(me + k, count)
        pltpu.make_async_remote_copy(
            src_ref=src.at[d], dst_ref=dst.at[k - 1], send_sem=send, recv_sem=recv,
            device_id={axis: d}, device_id_type=MESH,
        ).start()
        return carry

    lax.fori_loop(0, count - 1, one, 0)


def gather_far(axis, count, piece, send, recv):
    me = lax.axis_index(axis)

    def one(n, carry):
        pltpu.make_async_remote_copy(
            src_ref=piece, dst_ref=piece, send_sem=send, recv_sem=recv,
            device_id={axis: lax.rem(me + far(n, count), count)}, device_id_type=MESH,
        ).start()
        return carry

    lax.fori_loop(0, count - 1, one, 0)


def low_dot(a, b):
    return jnp.dot(a.astype(BF16), b.astype(BF16), preferred_element_type=F32)


def dot_three(a, b):
    a_top, b_top = a.astype(BF16), b.astype(BF16)
    a_rest, b_rest = (a - a_top.astype(F32)).astype(BF16), (b - b_top.astype(F32)).astype(BF16)
    cross = jnp.dot(a_top, b_rest, preferred_element_type=F32) + jnp.dot(a_rest, b_top, preferred_element_type=F32)
    return jnp.dot(a_top, b_top, preferred_element_type=F32) + cross


def first_half(v):
    down, across = diagonals(v)
    down, across = 1.0 / jnp.sqrt(down), 1.0 / jnp.sqrt(across)
    unit = jnp.where(eye(), 1.0, 0.0)
    c = v * down * across
    norm = jnp.max(jnp.sum(jnp.abs(c), axis=0, keepdims=True), axis=1, keepdims=True)
    alpha = jnp.where(norm < 1.9, 1.0, 1.0 / norm)
    res = unit - alpha * c
    x = alpha * (unit + res)
    x = x + low_dot(x, low_dot(res, res))
    return c, x, down, across


def second_half(c, x, down, across):
    unit = jnp.where(eye(), 1.0, 0.0)
    x = x + low_dot(x, unit - dot_three(c, x))
    res = unit - dot_three(c, x)
    worst = jnp.max(jnp.sum(jnp.abs(res), axis=0, keepdims=True), axis=1, keepdims=True)
    x = x + low_dot(x, res)
    return x * down * across, worst


def kernel_m(
    pos, cnt, x_hbm, b_ref, c_ref,
    a_out, b_out, worst_out,
    x_v, x_sem, br, w_even, w_odd, acc,
    gram, gb_part, gb_recv, gb_col, gb_full,
    part, pair_recv, half, m_recv, ms, m16, g_piece, g_recv, g_full,
    gram_c, inv1, slab, turned, lhs, ct, ones,
    pb, pb_recv, sq_piece, sq_row, sq_all, sq_col,
    send, recv,
):
    me_r, me_c = lax.axis_index("row"), lax.axis_index("col")
    chip, core = me_c // 2, lax.rem(me_c, 2)
    mate = chip * 2 + 1 - core

    def to_mate(src, dst, n):
        pltpu.make_async_remote_copy(
            src_ref=src, dst_ref=dst, send_sem=send.at[n], recv_sem=recv.at[n],
            device_id={"col": mate}, device_id_type=MESH,
        ).start()

    def chunk(ch):
        return pl.ds(pl.multiple_of(ch * CHUNK, CHUNK), CHUNK)

    def x_copy(ch):
        return pltpu.make_async_copy(x_hbm.at[:, chunk(ch)], x_v.at[:, chunk(ch)], x_sem.at[ch])

    for ch in range(NCH):
        x_copy(ch).start()
    barrier, partners = greet((("col", NCOL),))

    def in_plane(k):
        at = lax.rem(me_r * 4 + lax.rem(me_c, 4) + k, PLANE)
        return at // 4, me_c // 4 * 4 + lax.rem(at, 4)

    def greet_plane(k, carry):
        row, col = in_plane(k)
        pl.semaphore_signal(barrier, inc=1, device_id={"row": row, "col": col}, device_id_type=MESH)
        return carry

    lax.fori_loop(1, PLANE, greet_plane, 0)
    partners += PLANE - 1

    b = b_ref[...]
    gram[...] = dot_hi(b.T, b)
    rows = gram[pl.ds(pl.multiple_of(me_r * 32, 32), 32), :]
    for i in range(32):
        gb_part[i] = rows[i:i + 1, :]
    br[...] = b.astype(BF16).astype(F32)
    cr = c_ref[...].astype(BF16).astype(F32)
    acc[...] = jnp.zeros_like(acc)

    cb = cr.astype(BF16)

    def build(ch, w):
        for jb in range(JBD):
            tile = br[pl.ds(pl.multiple_of(jb * BLK + ch * JPC, JPC), JPC), :]
            for j in range(JPC):
                w[jb, j * K:(j + 1) * K, :] = jnp.broadcast_to(tile[j:j + 1, :].astype(BF16), (K, R)) * cb

    def add(ch, w):
        x_copy(ch).wait()
        for s in range(SLOTS):
            rows = slice(s * BLK, (s + 1) * BLK)
            acc[rows, :] += jnp.dot(x_v[rows, chunk(ch)], w[pos[0, s] & 1], preferred_element_type=F32)

    def mode_one(pair, carry):
        add(2 * pair, w_even)
        build(2 * pair + 1, w_odd)
        add(2 * pair + 1, w_odd)
        build(lax.rem(2 * pair + 2, NCH), w_even)
        return carry

    build(0, w_even)
    lax.fori_loop(0, NCH // 2 - 1, mode_one, 0)
    pl.semaphore_wait(barrier, partners)
    scatter_far("col", NCOL, gb_part, gb_recv, send.at[0], recv.at[0])
    lax.fori_loop(NCH // 2 - 1, NCH // 2, mode_one, 0)

    count = cnt[0, 0]
    for ib in range(IBD):
        total = jnp.zeros((BLK, R), F32)
        for s in range(SLOTS):
            live = jnp.where(count > s, 1.0, 0.0).astype(F32)
            keep = jnp.where(lax.shift_right_logical(pos[0, s], 1) == ib, live, 0.0)
            total += acc[s * BLK:(s + 1) * BLK, :] * keep
        for t in range(BLK // SHARE_A):
            at = ib * (BLK // SHARE_A) + t
            for side in range(2):
                part[side, at % 2, at // 2] = total[t * SHARE_A:(t + 1) * SHARE_A, side * BLK:(side + 1) * BLK]

    for side in range(2):
        to_mate(part.at[side, 1 - core], pair_recv.at[side], (1, 14)[side])
    c = c_ref[...]
    gram_c[...] = dot_hi(c.T, c)

    def to_chip(side, at, carry):
        k = far(at, CHIPS)
        d = lax.rem(chip + k, CHIPS)
        n = (2, 15)[side]
        pltpu.make_async_remote_copy(
            src_ref=half.at[side, d], dst_ref=m_recv.at[side, k - 1], send_sem=send.at[n], recv_sem=recv.at[n],
            device_id={"col": d * 2 + core}, device_id_type=MESH,
        ).start()
        return carry

    for side in range(2):
        wait_bytes(pair_recv.at[side], recv.at[(1, 14)[side]])
        half[side] = (part[side, core] + pair_recv[side]).astype(BF16)
        lax.fori_loop(0, CHIPS - 1, functools.partial(to_chip, side), 0)

    wait_bytes(gb_recv, recv.at[0])
    gb_col[me_c] = gb_part[me_c] + jnp.sum(gb_recv[...], axis=0)
    gather_far("col", NCOL, gb_col.at[me_c], send.at[3], recv.at[3])
    c_low = cr.T
    for jb in range(JBD):
        for t in range(CHUNK // K):
            ct[jb * R:(jb + 1) * R, t * K:(t + 1) * K] = c_low
    whose = lax.shift_right_logical(lax.broadcasted_iota(jnp.int32, (JPC, CHUNK), 1), 6)
    ones[...] = jnp.where(whose == lax.broadcasted_iota(jnp.int32, (JPC, CHUNK), 0), 1.0, 0.0).astype(BF16)

    def from_chip(side, at, carry):
        k = far(at, CHIPS)
        piece = ms.at[side, core, chip]
        n = (4, 16)[side]
        pltpu.make_async_remote_copy(
            src_ref=piece, dst_ref=piece, send_sem=send.at[n], recv_sem=recv.at[n],
            device_id={"col": lax.rem(chip + k, CHIPS) * 2 + core}, device_id_type=MESH,
        ).start()
        return carry

    def pass_on(side):
        wait_bytes(m_recv.at[side], recv.at[(2, 15)[side]])
        mine = part[side, core, chip] + pair_recv[side, chip] + jnp.sum(m_recv[side].astype(F32), axis=0)
        ms[side, core, chip] = mine.astype(BF16)
        lax.fori_loop(0, CHIPS - 1, functools.partial(from_chip, side), 0)
        m16[:, side * BLK:(side + 1) * BLK] = mine

    pass_on(0)
    wait_bytes(gb_col.at[pl.ds(0, NCOL - 1)], recv.at[3])
    for i in range(16):
        gb_full[core, me_r, i:i + 1, :] = gb_col[core * 16 + i]
    gather_far("row", NROW, gb_full.at[core, me_r], send.at[5], recv.at[5])
    pass_on(1)

    wait_bytes(gb_full.at[0, pl.ds(0, NROW - 1)], recv.at[5])
    to_mate(gb_full.at[core], gb_full.at[core], 13)
    wait_bytes(gb_full.at[0], recv.at[13])
    for at in range(R // 16):
        gram[at * 16:(at + 1) * 16, :] = gb_full[at % 2, at // 2]
    c_one, x_one, down_one, across_one = first_half(gram[...] * gram_c[...])
    turned[:, :R] = c_one
    turned[:, R:] = x_one

    for side in range(2):
        wait_bytes(m_recv.at[side], recv.at[(4, 16)[side]])
        to_mate(ms.at[side, core], ms.at[side, core], (6, 17)[side])
    for side in range(2):
        wait_bytes(ms.at[side, 0], recv.at[(6, 17)[side]])
        for at in range(NCOL):
            slab[at * SHARE_A:(at + 1) * SHARE_A, side * BLK:(side + 1) * BLK] = ms[side, at % 2, at // 2]

    gram[...] = jnp.dot(slab[...].T, slab[...], preferred_element_type=F32)
    own = jnp.where(core == 0, gram[:BLK, :BLK], gram[BLK:, BLK:])
    cross = gram[pl.ds(pl.multiple_of(core * (BLK // 2), BLK // 2), BLK // 2), BLK:]
    g_piece[:, :SHARE_G, :] = own.reshape(NROW, SHARE_G, BLK)
    g_piece[:, SHARE_G:, :] = cross.reshape(NROW, SHARE_G // 2, BLK)
    scatter_far("row", NROW, g_piece, g_recv, send.at[7], recv.at[7])

    solved, worst_one = second_half(turned[:, :R], turned[:, R:], down_one, across_one)
    inv1[...] = solved
    top = inv1[...].astype(BF16)
    rest = (inv1[...] - top.astype(F32)).astype(BF16)
    last = (((1,), (1,)), ((), ()))
    turned[...] = lax.dot_general(top, slab[...], last, preferred_element_type=F32) + lax.dot_general(
        rest, slab[...], last, preferred_element_type=F32
    )
    for s in range(SLOTS):
        p = pos[0, s]
        live = jnp.where(count > s, 1.0, 0.0).astype(F32)
        for jb in range(JBD):
            tile = jnp.zeros((R, BLK), F32)
            for ib in range(IBD):
                tile += turned[:, ib * BLK:(ib + 1) * BLK] * jnp.where(p == ib * JBD + jb, live, 0.0)
            lhs[jb * R:(jb + 1) * R, s * BLK:(s + 1) * BLK] = tile.astype(BF16)

    def mode_two(group, carry):
        for side in range(2):
            ch = 2 * group + side
            t = jnp.dot(lhs[...], x_v[:, chunk(ch)], preferred_element_type=F32)
            t = (t * ct[...]).astype(BF16)
            rows = lax.dot_general(ones[...], t, last, preferred_element_type=F32).astype(BF16)
            for jb in range(JBD):
                pb[jb * (NROW // 2) + group, side * JPC:(side + 1) * JPC, :] = rows[:, jb * R:(jb + 1) * R]
        for jb in range(JBD):
            to = jb * (NROW // 2) + group

            @pl.when(to != me_r)
            def _():
                pltpu.make_async_remote_copy(
                    src_ref=pb.at[to], dst_ref=pb_recv.at[lax.rem(to - me_r + NROW, NROW) - 1],
                    send_sem=send.at[10], recv_sem=recv.at[10],
                    device_id={"row": to}, device_id_type=MESH,
                ).start()

        return carry

    lax.fori_loop(0, 2, mode_two, 0)
    wait_bytes(g_recv, recv.at[7])
    g_full[core, me_r] = g_piece[me_r] + jnp.sum(g_recv[...], axis=0)
    gather_far("row", NROW, g_full.at[core, me_r], send.at[8], recv.at[8])
    lax.fori_loop(2, 4, mode_two, 0)
    wait_bytes(g_recv, recv.at[8])
    to_mate(g_full.at[core], g_full.at[core], 9)

    wait_bytes(g_full.at[0], recv.at[9])
    solved = inv1[...]
    for e in range(2):
        gram[e * BLK:(e + 1) * BLK, e * BLK:(e + 1) * BLK] = g_full[e, :, :SHARE_G, :].reshape(BLK, BLK)
        cross = g_full[e, :, SHARE_G:, :].reshape(BLK // 2, BLK)
        gram[e * (BLK // 2):(e + 1) * (BLK // 2), BLK:] = cross
    gram[BLK:, :BLK] = gram[:BLK, BLK:].T
    gram_a = dot_three(dot_three(solved, gram[...]), solved)
    down, across = diagonals(gram_a)
    down = 1.0 / jnp.sqrt(down / ROWS_A + EPS)
    across = 1.0 / jnp.sqrt(across / ROWS_A + EPS)
    a_out[...] = dot_three(m16[...], solved) * across
    inv2, worst_two = second_half(*first_half(gram_a * down * across * gram_c[...]))
    worst_out[...] = jnp.maximum(worst_one, worst_two)

    wait_bytes(pb_recv, recv.at[10])
    m2 = (pb[me_r].astype(F32) + jnp.sum(pb_recv[...].astype(F32), axis=0)) * across
    raw = dot_hi(m2, inv2)
    sq_piece[...] = jnp.sum(raw * raw, axis=0, keepdims=True)

    def to_plane(at, carry):
        k = far(at, PLANE)
        row, col = in_plane(k)
        pltpu.make_async_remote_copy(
            src_ref=sq_piece, dst_ref=sq_col.at[k - 1], send_sem=send.at[11], recv_sem=recv.at[11],
            device_id={"row": row, "col": col}, device_id_type=MESH,
        ).start()
        return carry

    lax.fori_loop(0, PLANE - 1, to_plane, 0)
    wait_bytes(sq_col, recv.at[11])
    sq_all[...] = sq_piece[...] + jnp.sum(sq_col[...], axis=0)

    def to_planes(at, carry):
        k = far(at, NCOL // 4)
        pltpu.make_async_remote_copy(
            src_ref=sq_all, dst_ref=sq_row.at[k - 1], send_sem=send.at[12], recv_sem=recv.at[12],
            device_id={"col": lax.rem(me_c + k * 4, NCOL)}, device_id_type=MESH,
        ).start()
        return carry

    lax.fori_loop(0, NCOL // 4 - 1, to_planes, 0)
    wait_bytes(gb_recv, send.at[0])
    for side in range(2):
        wait_bytes(pair_recv.at[side], send.at[(1, 14)[side]])
        wait_bytes(m_recv.at[side], send.at[(2, 15)[side]])
        wait_bytes(m_recv.at[side], send.at[(4, 16)[side]])
        wait_bytes(ms.at[side, 0], send.at[(6, 17)[side]])
    wait_bytes(gb_col.at[pl.ds(0, NCOL - 1)], send.at[3])
    wait_bytes(gb_full.at[0, pl.ds(0, NROW - 1)], send.at[5])
    wait_bytes(gb_full.at[0], send.at[13])
    wait_bytes(g_recv, send.at[7])
    wait_bytes(g_recv, send.at[8])
    wait_bytes(g_full.at[0], send.at[9])
    wait_bytes(pb_recv, send.at[10])
    wait_bytes(sq_col, send.at[11])
    wait_bytes(sq_row, recv.at[12])
    squares = sq_all[...] + jnp.sum(sq_row[...], axis=0)
    b_out[...] = raw / jnp.sqrt(squares / ROWS_B + EPS)
    wait_bytes(sq_row, send.at[12])


VM = pl.BlockSpec(memory_space=pltpu.VMEM)
SM = pl.BlockSpec(memory_space=pltpu.SMEM)
ANY = pl.BlockSpec(memory_space=pl.ANY)


def shape(dims, kind=F32):
    return jax.ShapeDtypeStruct(dims, kind)


def three_kernels(place, block_count, flat, factor_b, factor_c):
    vm, dma = pltpu.VMEM, pltpu.SemaphoreType.DMA
    gram_b, m16, ms, g = pl.pallas_call(
        kernel_a,
        name="mode_one",
        out_shape=(shape((R, R)), shape((SHARE_A, R)), shape((SLAB_A, R), BF16), shape((R, R))),
        in_specs=[SM, SM, ANY, VM, VM],
        out_specs=[VM] * 4,
        scratch_shapes=[
            vm((SLAB_A, WIDE), BF16), dma((NCH,)), vm((R, R), F32), vm((CHUNK, JBD * R), BF16), vm((SLAB_A, JBD * R), F32),
            vm((R, R), F32), vm((NCOL, 1, R), F32), vm((NCOL - 1, 1, R), F32), vm((NCOL, 1, R), F32), vm((NROW, 32, R), F32),
            vm((2, CHIPS, SHARE_A, R), F32), vm((CHIPS, SHARE_A, R), F32), vm((CHIPS, SHARE_A, R), BF16),
            vm((CHIPS - 1, SHARE_A, R), BF16), vm((2, CHIPS, SHARE_A, R), BF16),
            vm((NROW, SHARE_G, R), F32), vm((NROW - 1, SHARE_G, R), F32), vm((2, NROW, SHARE_G, R), F32),
            dma((10,)), dma((10,)),
        ],
        compiler_params=pltpu.CompilerParams(collective_id=1, has_side_effects=True),
    )(place, block_count, flat, factor_b, factor_c)
    hat_a, lhs, inv = pl.pallas_call(
        kernel_b,
        name="solve_two",
        out_shape=(shape((SHARE_A, R)), shape((JBD * R, SLAB_A), BF16), shape((R, R))),
        in_specs=[SM, SM, VM, VM, VM, VM, VM],
        out_specs=[VM] * 3,
        scratch_shapes=[vm((R, R), F32), vm((R, R), F32), vm((R, R), F32), vm((SLAB_A, R), F32)],
    )(place, block_count, factor_c, gram_b, m16, ms, g)
    hat_b = pl.pallas_call(
        kernel_c,
        name="mode_two",
        out_shape=shape((SHARE_B, R)),
        in_specs=[ANY, VM, VM, VM],
        out_specs=VM,
        scratch_shapes=[
            vm((SLAB_A, WIDE), BF16), dma((NCH,)), vm((JBD * R, CHUNK), F32), vm((JBD * R, BLK), F32),
            vm((NROW, SHARE_B, R), BF16), vm((NROW - 1, SHARE_B, R), BF16),
            vm((1, R), F32), vm((NROW - 1, 1, R), F32), vm((1, R), F32), vm((NCOL - 1, 1, R), F32),
            dma((3,)), dma((3,)),
        ],
        compiler_params=pltpu.CompilerParams(collective_id=2, has_side_effects=True),
    )(flat, factor_c, lhs, inv)
    return hat_a, hat_b


def body(blocks, factor_b, factor_c, block_pos, block_count):
    args = (block_pos.T, block_count, blocks.reshape(SLOTS * BLK, WIDE), factor_b, factor_c)
    vm, dma = pltpu.VMEM, pltpu.SemaphoreType.DMA
    hat_a, hat_b, worst = pl.pallas_call(
        kernel_m,
        name="sweep",
        out_shape=(shape((SHARE_A, R)), shape((SHARE_B, R)), shape((1, 1))),
        in_specs=[SM, SM, ANY, VM, VM],
        out_specs=[VM] * 3,
        scratch_shapes=[
            vm((SLAB_A, WIDE), BF16), dma((NCH,)), vm((R, R), F32), vm((JBD, CHUNK, R), BF16),
            vm((JBD, CHUNK, R), BF16), vm((SLAB_A, R), F32),
            vm((R, R), F32), vm((NCOL, 1, R), F32), vm((NCOL - 1, 1, R), F32), vm((NCOL, 1, R), F32), vm((2, NROW, 16, R), F32),
            vm((2, 2, CHIPS, SHARE_A, BLK), F32), vm((2, CHIPS, SHARE_A, BLK), F32), vm((2, CHIPS, SHARE_A, BLK), BF16),
            vm((2, CHIPS - 1, SHARE_A, BLK), BF16), vm((2, 2, CHIPS, SHARE_A, BLK), BF16), vm((SHARE_A, R), F32),
            vm((NROW, PIECE_G, BLK), F32), vm((NROW - 1, PIECE_G, BLK), F32), vm((2, NROW, PIECE_G, BLK), F32),
            vm((R, R), F32), vm((R, R), F32), vm((SLAB_A, R), BF16), vm((R, SLAB_A), F32), vm((JBD * R, SLAB_A), BF16),
            vm((JBD * R, CHUNK), F32), vm((JPC, CHUNK), BF16),
            vm((NROW, SHARE_B, R), BF16), vm((NROW - 1, SHARE_B, R), BF16),
            vm((1, R), F32), vm((NROW - 1, 1, R), F32), vm((1, R), F32), vm((NCOL - 1, 1, R), F32),
            dma((18,)), dma((18,)),
        ],
        compiler_params=pltpu.CompilerParams(collective_id=0, has_side_effects=True),
    )(*args)
    return lax.cond(worst[0, 0] <= 1e-3, lambda: (hat_a, hat_b), lambda: three_kernels(*args))


def solution(mesh):
    return jax.shard_map(
        body,
        mesh=mesh,
        in_specs=(P("row", "col", None), P("col", None), P(), P("row", "col"), P("row", "col")),
        out_specs=(P(("row", "col"), None), P(("col", "row"), None)),
        check_vma=False,
    )
```
